512 devices in a mesh: dp: 8 (over x, core), expert: 64 (over y, z).
Axes of the slice: x: 4, y: 4, z: 16, core: 2. Of those that a mesh axis runs over, the one named last changes fastest.
Arguments:
- tokens: bfloat16 [65536, 2048], P(('dp', 'expert')), may hold values from -6 to 6
- out_grad: bfloat16 [65536, 2048], P(('dp', 'expert')), may hold values from -3 to 3
- expert_ids: int32 [65536, 1], P(('dp', 'expert')), may hold values from 0 to 63, as said below
- gates: float32 [65536, 1], P(('dp', 'expert')), may hold values from 0.1 to 1
- w_gate: bfloat16 [64, 2048, 384], P('expert', 'dp'), may hold values from -0.125 to 0.125
- w_up: bfloat16 [64, 2048, 384], P('expert', 'dp'), may hold values from -0.125 to 0.125
- w_down: bfloat16 [64, 384, 2048], P('expert', None, 'dp'), may hold values from -0.3125 to 0.3125
Outputs:
- input_grad: bfloat16 [65536, 2048], P(('dp', 'expert'))
- gate_grad: bfloat16 [64, 2048, 384], P('expert', 'dp')
- up_grad: bfloat16 [64, 2048, 384], P('expert', 'dp')
- down_grad: bfloat16 [64, 384, 2048], P('expert')
The draws below stay inside these ranges and needn't reach their ends.
Inputs may be any that keep to these rules, and one draw needn't show every extreme that they name: `expert_ids`: among the rows of one device no expert is named more than 6 times; 4 experts, the same ones for every device, are named exactly 6 times by every device.
All inputs are finite; a program needn't handle non-finite values.
Results may differ from the reference program's by a relative error of at most 0.013.
Values may be sent and summed in bfloat16 or wider, within the bound.
A program may use at most 64 MiB of HBM per device.

```python
import jax
import jax.numpy as jnp
from jax import lax

D = 2048
HID = 384
TOK_DEV = 128
TOPK = 1
EXPERTS = 64
MOST = 6
HOT = 4
CAP = 384
GROUP_TOKENS = 8192
TOKENS = 65536
N_DP = 8


def draw_expert_ids(key, part):
    blocks = TOKENS // TOK_DEV
    entries = TOK_DEV * TOPK
    cold_count = EXPERTS - HOT
    cold_rows = entries - HOT * MOST
    sorting = jax.random.permutation(jax.random.fold_in(key, 11), EXPERTS).astype(jnp.int32)

    def one_block(block_index):
        block_key = jax.random.fold_in(jax.random.fold_in(key, 23), block_index)
        weights = jax.random.randint(jax.random.fold_in(block_key, 1), (cold_count,), 2, 7).astype(jnp.int32)
        quotas = cold_rows * weights // jnp.sum(weights)
        leftover = cold_rows - jnp.sum(quotas)
        quotas = quotas + (jnp.arange(cold_count, dtype=jnp.int32) < leftover).astype(jnp.int32)
        counts = jnp.zeros((EXPERTS,), jnp.int32).at[sorting[HOT:]].set(quotas)
        counts = counts.at[sorting[:HOT]].set(MOST)
        labels = jnp.repeat(jnp.arange(EXPERTS, dtype=jnp.int32), counts, total_repeat_length=entries)
        id_table = labels.reshape(TOPK, TOK_DEV).T
        shuffle = jax.random.permutation(jax.random.fold_in(block_key, 2), TOK_DEV)
        return id_table[shuffle]
    every_block = jax.vmap(one_block)(jnp.arange(blocks, dtype=jnp.int32))
    return every_block.reshape(TOKENS, TOPK).astype(jnp.int32)


def level_of(stream_key, shape, split, low, top_value):
    gain, own = 1.0, jax.random.fold_in(stream_key, 6)
    for axis_at, blocks in split:
        steps = jnp.exp(jax.random.uniform(jax.random.fold_in(own, axis_at), (blocks,), jnp.float32, low / len(split), top_value / len(split)))
        gain = gain * jnp.repeat(steps, shape[axis_at] // blocks).reshape([-1 if axis == axis_at else 1 for axis in range(len(shape))])
    return gain


def noise(rng, extent, deviation, limit, shards=(), kind=jnp.bfloat16):
    gain = level_of(rng, extent, shards, -0.22, 0.18) if shards else 1.0
    drawn = jax.random.normal(rng, extent, jnp.float32) * deviation * gain
    return jnp.minimum(jnp.maximum(drawn, -limit), limit).astype(kind)


def setup_inputs(seed: int = 0) -> dict:
    splits = jax.random.split(jax.random.key(seed), 8)
    return {
        "tokens": noise(splits[0], (TOKENS, D), 1.0, 6.0, ((0, 512),)),
        "out_grad": noise(splits[1], (TOKENS, D), 0.5, 3.0, ((0, 512),)),
        "expert_ids": draw_expert_ids(jax.random.fold_in(splits[7], 71), 0),
        "gates": jnp.clip(0.1 + 0.9 * jax.random.uniform(splits[3], (TOKENS, TOPK), jnp.float32) ** level_of(splits[3], (TOKENS, TOPK), ((0, 512),), -0.2, 0.2), 0.1, 1.0),
        "w_gate": noise(splits[4], (EXPERTS, D, HID), D ** -0.5, 0.125, ((0, 64), (1, 8))),
        "w_up": noise(splits[5], (EXPERTS, D, HID), D ** -0.5, 0.125, ((0, 64), (1, 8))),
        "w_down": noise(splits[6], (EXPERTS, HID, D), HID ** -0.5, 0.3125, ((0, 64), (2, 8))),
    }


def reference(tokens, out_grad, expert_ids, gates, w_gate, w_up, w_down):
    group_entries = GROUP_TOKENS * TOPK
    grouped = expert_ids.reshape(N_DP, group_entries)
    sorting = jnp.argsort(grouped, axis=1, stable=True).astype(jnp.int32)
    expert_range = jnp.arange(EXPERTS, dtype=jnp.int32)
    counts = jnp.sum((grouped[:, :, None] == expert_range[None, None, :]).astype(jnp.int32), axis=1).astype(jnp.int32)
    starts = (jnp.cumsum(counts, axis=1) - counts).astype(jnp.int32)
    slot_lane = jnp.arange(CAP, dtype=jnp.int32)
    group_base = (jnp.arange(N_DP, dtype=jnp.int32) * group_entries)[:, None]
    flat_gates = gates.reshape(-1)

    def per_expert(accumulated, expert):
        gate_w = w_gate[expert]
        up_w = w_up[expert]
        down_w = w_down[expert]
        joined = jnp.concatenate([gate_w, up_w], axis=1)
        positions = jnp.minimum(starts[:, expert][:, None] + slot_lane[None, :], group_entries - 1).astype(jnp.int32)
        usable = (slot_lane[None, :] < counts[:, expert][:, None]).reshape(-1)
        entry_ids = (jnp.take_along_axis(sorting, positions, axis=1) + group_base).reshape(-1).astype(jnp.int32)
        token_ids = (entry_ids // TOPK).astype(jnp.int32)
        inputs = jnp.where(usable[:, None], tokens[token_ids], jnp.zeros((), tokens.dtype))
        slot_gate = jnp.where(usable, flat_gates[entry_ids], jnp.zeros((), flat_gates.dtype))
        scaled = (slot_gate[:, None] * out_grad[token_ids].astype(jnp.float32)).astype(jnp.bfloat16)
        preact = jnp.dot(inputs, joined, preferred_element_type=jnp.float32)
        hidden_grad = lax.dot_general(scaled, down_w, (((1,), (1,)), ((), ())), preferred_element_type=jnp.float32)
        gate_pre = preact[:, :HID]
        up_pre = preact[:, HID:]
        sigmoid = jax.nn.sigmoid(gate_pre)
        silu_value = gate_pre * sigmoid
        activated = (silu_value * up_pre).astype(jnp.bfloat16)
        gate_side = (hidden_grad * up_pre * sigmoid * (1.0 + gate_pre * (1.0 - sigmoid))).astype(jnp.bfloat16)
        up_side = (hidden_grad * silu_value).astype(jnp.bfloat16)
        both_sides = jnp.concatenate([gate_side, up_side], axis=1)
        down_parts = jnp.einsum("rch,rcd->rhd", activated.reshape(N_DP, CAP, HID).astype(jnp.float32), scaled.reshape(N_DP, CAP, D).astype(jnp.float32))
        down_round = lax.optimization_barrier(down_parts.astype(jnp.bfloat16))
        down_total = jnp.sum(down_round.astype(jnp.float32), axis=0).astype(jnp.bfloat16)
        join_parts = jnp.einsum("rcd,rcj->rdj", inputs.reshape(N_DP, CAP, D).astype(jnp.float32), both_sides.reshape(N_DP, CAP, 2 * HID).astype(jnp.float32))
        join_round = lax.optimization_barrier(join_parts.astype(jnp.bfloat16))
        join_total = jnp.sum(join_round.astype(jnp.float32), axis=0).astype(jnp.bfloat16)
        slot_grad = lax.dot_general(both_sides, joined, (((1,), (1,)), ((), ())), preferred_element_type=jnp.float32)
        slot_round = lax.optimization_barrier(slot_grad.astype(jnp.bfloat16))
        adding = jnp.where(usable[:, None], slot_round.astype(jnp.float32), jnp.zeros((), jnp.float32))
        accumulated = accumulated.at[token_ids].add(adding)
        return accumulated, (join_total[:, :HID], join_total[:, HID:], down_total)

    start_grad = jnp.zeros((TOKENS, D), jnp.float32)
    summed, outputs = lax.scan(per_expert, start_grad, jnp.arange(EXPERTS, dtype=jnp.int32))
    gate_grad, up_grad, down_grad = outputs
    return summed.astype(jnp.bfloat16), gate_grad, up_grad, down_grad
```

```python
import jax
import jax.numpy as jnp
from jax import lax
from jax.sharding import PartitionSpec as P


def on_device(tokens, out_grad, expert_ids, gates, w_gate, w_up, w_down):
    expert_count = lax.axis_size("expert")
    tok_rows = tokens.shape[0]
    model_width = tokens.shape[1]
    per_token = expert_ids.shape[1]
    hidden = w_gate.shape[2]
    entries = tok_rows * per_token
    slot_depth = 3 * entries // expert_count
    slot_count = expert_count * slot_depth
    flat_ids = expert_ids.reshape(entries)
    onehot = (flat_ids[:, None] == jnp.arange(expert_count, dtype=jnp.int32)[None, :]).astype(
        jnp.int32
    )
    before = jnp.cumsum(onehot, axis=0) - onehot
    ranking = jnp.sum(before * onehot, axis=1)
    slot_of_entry = flat_ids * slot_depth + ranking
    source = (
        jnp.full((slot_count,), entries, jnp.int32)
        .at[slot_of_entry]
        .set(jnp.arange(entries, dtype=jnp.int32))
    )
    entry_scaled = (
        (gates[:, :, None] * out_grad.astype(jnp.float32)[:, None, :])
        .astype(jnp.bfloat16)
        .reshape(entries, model_width)
    )
    grad_table = jnp.concatenate([entry_scaled, jnp.zeros((1, model_width), jnp.bfloat16)], axis=0)
    input_table = jnp.concatenate([tokens, jnp.zeros((1, model_width), tokens.dtype)], axis=0)
    send_grads = grad_table[source].reshape(expert_count, slot_depth, model_width)
    send_inputs = input_table[source // per_token].reshape(expert_count, slot_depth, model_width)
    recv_both = lax.all_to_all(
        jnp.concatenate([send_inputs, send_grads], axis=2),
        "expert",
        split_axis=0,
        concat_axis=0,
        tiled=True,
    ).reshape(slot_count, 2 * model_width)
    rows_in = recv_both[:, :model_width]
    grads_in = recv_both[:, model_width:]
    local_joined = jnp.concatenate([w_gate[0], w_up[0]], axis=1)
    full_joined, full_down = (
        lax.all_gather(local_joined, "dp", axis=0, tiled=True),
        lax.all_gather(w_down[0], "dp", axis=1, tiled=True),
    )
    preact = jnp.dot(rows_in, full_joined, preferred_element_type=jnp.float32)
    hidden_grad = lax.dot_general(
        grads_in, full_down, (((1,), (1,)), ((), ())), preferred_element_type=jnp.float32
    )
    gate_pre = preact[:, :hidden]
    up_pre = preact[:, hidden:]
    sigmoid = jax.nn.sigmoid(gate_pre)
    silu_value = gate_pre * sigmoid
    activated = (silu_value * up_pre).astype(jnp.bfloat16)
    gate_side = (hidden_grad * up_pre * sigmoid * (1.0 + gate_pre * (1.0 - sigmoid))).astype(
        jnp.bfloat16
    )
    up_side = (hidden_grad * silu_value).astype(jnp.bfloat16)
    both_sides = jnp.concatenate([gate_side, up_side], axis=1)
    slot_grad = lax.dot_general(
        both_sides, full_joined, (((1,), (1,)), ((), ())), preferred_element_type=jnp.float32
    )
    slot_grad = slot_grad.astype(jnp.bfloat16).reshape(expert_count, slot_depth, model_width)
    returned = lax.all_to_all(slot_grad, "expert", split_axis=0, concat_axis=0, tiled=True).reshape(
        slot_count, model_width
    )
    picked = returned[slot_of_entry].astype(jnp.float32).reshape(tok_rows, per_token, model_width)
    input_grad = jnp.sum(picked, axis=1).astype(jnp.bfloat16)
    down_part = lax.dot_general(
        activated, grads_in, (((0,), (0,)), ((), ())), preferred_element_type=jnp.float32
    )
    down_grad = lax.psum(down_part.astype(jnp.bfloat16), "dp")[None]
    joined_grad = lax.psum_scatter(
        lax.dot_general(
            rows_in, both_sides, (((0,), (0,)), ((), ())), preferred_element_type=jnp.float32
        ).astype(jnp.bfloat16),
        "dp",
        scatter_dimension=0,
        tiled=True,
    )
    gate_grad = joined_grad[:, :hidden][None]
    up_grad = joined_grad[:, hidden:][None]
    return (input_grad, gate_grad, up_grad, down_grad)


def solution(mesh):
    in_specs = (
        P(("dp", "expert"), None),
        P(("dp", "expert"), None),
        P(("dp", "expert"), None),
        P(("dp", "expert"), None),
        P("expert", "dp", None),
        P("expert", "dp", None),
        P("expert", None, "dp"),
    )
    out_specs = (
        P(("dp", "expert"), None),
        P("expert", "dp", None),
        P("expert", "dp", None),
        P("expert", None, None),
    )
    return jax.shard_map(
        on_device, mesh=mesh, in_specs=in_specs, out_specs=out_specs, check_vma=False
    )
```

```python
import functools
import jax
import jax.numpy as jnp
from jax import lax
from jax.experimental import pallas as pl
from jax.experimental.pallas import tpu as pltpu
from jax.sharding import PartitionSpec as P

MESH = pl.DeviceIdType.MESH


def exchange_kernel(n, count, *refs):
    sources = refs[:count]
    targets = refs[count : 2 * count]
    send_sem, recv_sem, local_sem = refs[2 * count :]
    me = lax.axis_index("expert")
    row = lax.axis_index("dp")
    barrier = pltpu.get_barrier_semaphore()

    def greet(i, carry):
        peer = lax.rem(me + i, n)
        pl.semaphore_signal(barrier, inc=1, device_id=(row, peer), device_id_type=MESH)
        return carry

    lax.fori_loop(1, n, greet, 0)
    pl.semaphore_wait(barrier, n - 1)
    local = [
        pltpu.make_async_copy(sources[a].at[me], targets[a].at[me], local_sem.at[a])
        for a in range(count)
    ]
    for copy in local:
        copy.start()

    def remote(a, peer, slot):
        return pltpu.make_async_remote_copy(
            src_ref=sources[a].at[peer],
            dst_ref=targets[a].at[slot],
            send_sem=send_sem.at[a, peer],
            recv_sem=recv_sem.at[a, slot],
            device_id=(row, peer),
            device_id_type=MESH,
        )

    def start(i, carry):
        peer = lax.rem(me + i, n)
        for a in range(count):
            remote(a, peer, me).start()
        return carry

    lax.fori_loop(1, n, start, 0)

    def finish(i, carry):
        peer = lax.rem(me + i, n)
        source = lax.rem(me + n - i, n)
        for a in range(count):
            remote(a, peer, me).wait_send()
            remote(a, source, source).wait_recv()
        return carry

    lax.fori_loop(1, n, finish, 0)
    for copy in local:
        copy.wait()


def expert_exchange(arrays, collective_id):
    n = arrays[0].shape[0]
    count = len(arrays)
    return pl.pallas_call(
        functools.partial(exchange_kernel, n, count),
        out_shape=[jax.ShapeDtypeStruct(a.shape, a.dtype) for a in arrays],
        in_specs=[pl.BlockSpec(memory_space=pl.ANY)] * count,
        out_specs=[pl.BlockSpec(memory_space=pl.ANY)] * count,
        scratch_shapes=[
            pltpu.SemaphoreType.DMA((count, n)),
            pltpu.SemaphoreType.DMA((count, n)),
            pltpu.SemaphoreType.DMA((count,)),
        ],
        compiler_params=pltpu.CompilerParams(
            collective_id=collective_id, has_side_effects=True
        ),
    )(*arrays)


def on_device(tokens, out_grad, expert_ids, gates, w_gate, w_up, w_down):
    expert_count = lax.axis_size("expert")
    tok_rows = tokens.shape[0]
    model_width = tokens.shape[1]
    per_token = expert_ids.shape[1]
    hidden = w_gate.shape[2]
    entries = tok_rows * per_token
    slot_depth = 3 * entries // expert_count
    slot_count = expert_count * slot_depth
    flat_ids = expert_ids.reshape(entries)
    onehot = (flat_ids[:, None] == jnp.arange(expert_count, dtype=jnp.int32)[None, :]).astype(
        jnp.int32
    )
    before = jnp.cumsum(onehot, axis=0) - onehot
    ranking = jnp.sum(before * onehot, axis=1)
    slot_of_entry = flat_ids * slot_depth + ranking
    source = (
        jnp.full((slot_count,), entries, jnp.int32)
        .at[slot_of_entry]
        .set(jnp.arange(entries, dtype=jnp.int32))
    )
    entry_scaled = (
        (gates[:, :, None] * out_grad.astype(jnp.float32)[:, None, :])
        .astype(jnp.bfloat16)
        .reshape(entries, model_width)
    )
    grad_table = jnp.concatenate([entry_scaled, jnp.zeros((1, model_width), jnp.bfloat16)], axis=0)
    input_table = jnp.concatenate([tokens, jnp.zeros((1, model_width), tokens.dtype)], axis=0)
    send_grads = grad_table[source].reshape(expert_count, slot_depth, model_width)
    send_inputs = input_table[source // per_token].reshape(expert_count, slot_depth, model_width)
    recv_inputs, recv_grads = expert_exchange([send_inputs, send_grads], 0)
    rows_in = recv_inputs.reshape(slot_count, model_width)
    grads_in = recv_grads.reshape(slot_count, model_width)
    local_joined = jnp.concatenate([w_gate[0], w_up[0]], axis=1)
    full_joined, full_down = (
        lax.all_gather(local_joined, "dp", axis=0, tiled=True),
        lax.all_gather(w_down[0], "dp", axis=1, tiled=True),
    )
    preact = jnp.dot(rows_in, full_joined, preferred_element_type=jnp.float32)
    hidden_grad = lax.dot_general(
        grads_in, full_down, (((1,), (1,)), ((), ())), preferred_element_type=jnp.float32
    )
    gate_pre = preact[:, :hidden]
    up_pre = preact[:, hidden:]
    sigmoid = jax.nn.sigmoid(gate_pre)
    silu_value = gate_pre * sigmoid
    activated = (silu_value * up_pre).astype(jnp.bfloat16)
    gate_side = (hidden_grad * up_pre * sigmoid * (1.0 + gate_pre * (1.0 - sigmoid))).astype(
        jnp.bfloat16
    )
    up_side = (hidden_grad * silu_value).astype(jnp.bfloat16)
    both_sides = jnp.concatenate([gate_side, up_side], axis=1)
    slot_grad = lax.dot_general(
        both_sides, full_joined, (((1,), (1,)), ((), ())), preferred_element_type=jnp.float32
    )
    slot_grad = slot_grad.astype(jnp.bfloat16).reshape(expert_count, slot_depth, model_width)
    returned = expert_exchange([slot_grad], 1)[0].reshape(slot_count, model_width)
    picked = returned[slot_of_entry].astype(jnp.float32).reshape(tok_rows, per_token, model_width)
    input_grad = jnp.sum(picked, axis=1).astype(jnp.bfloat16)
    down_part = lax.dot_general(
        activated, grads_in, (((0,), (0,)), ((), ())), preferred_element_type=jnp.float32
    )
    down_grad = lax.psum(down_part.astype(jnp.bfloat16), "dp")[None]
    joined_grad = lax.psum_scatter(
        lax.dot_general(
            rows_in, both_sides, (((0,), (0,)), ((), ())), preferred_element_type=jnp.float32
        ).astype(jnp.bfloat16),
        "dp",
        scatter_dimension=0,
        tiled=True,
    )
    gate_grad = joined_grad[:, :hidden][None]
    up_grad = joined_grad[:, hidden:][None]
    return (input_grad, gate_grad, up_grad, down_grad)


def solution(mesh):
    in_specs = (
        P(("dp", "expert"), None),
        P(("dp", "expert"), None),
        P(("dp", "expert"), None),
        P(("dp", "expert"), None),
        P("expert", "dp", None),
        P("expert", "dp", None),
        P("expert", None, "dp"),
    )
    out_specs = (
        P(("dp", "expert"), None),
        P("expert", "dp", None),
        P("expert", "dp", None),
        P("expert", None, None),
    )
    return jax.shard_map(
        on_device, mesh=mesh, in_specs=in_specs, out_specs=out_specs, check_vma=False
    )
```

```python
import functools
import jax
import jax.numpy as jnp
from jax import lax
from jax.experimental import pallas as pl
from jax.experimental.pallas import tpu as pltpu
from jax.sharding import PartitionSpec as P

MESH = pl.DeviceIdType.MESH


def exchange_kernel(n, count, *refs):
    sources = refs[:count]
    targets = refs[count : 2 * count]
    send_sem, recv_sem, local_sem = refs[2 * count :]
    me = lax.axis_index("expert")
    row = lax.axis_index("dp")
    barrier = pltpu.get_barrier_semaphore()

    def greet(i, carry):
        peer = lax.rem(me + i, n)
        pl.semaphore_signal(barrier, inc=1, device_id=(row, peer), device_id_type=MESH)
        return carry

    lax.fori_loop(1, n, greet, 0)
    pl.semaphore_wait(barrier, n - 1)
    local = [
        pltpu.make_async_copy(sources[a].at[me], targets[a].at[me], local_sem.at[a])
        for a in range(count)
    ]
    for copy in local:
        copy.start()

    def remote(a, peer, slot):
        return pltpu.make_async_remote_copy(
            src_ref=sources[a].at[peer],
            dst_ref=targets[a].at[slot],
            send_sem=send_sem.at[a, peer],
            recv_sem=recv_sem.at[a, slot],
            device_id=(row, peer),
            device_id_type=MESH,
        )

    def start(i, carry):
        peer = lax.rem(me + i, n)
        for a in range(count):
            remote(a, peer, me).start()
        return carry

    lax.fori_loop(1, n, start, 0)

    def finish(i, carry):
        peer = lax.rem(me + i, n)
        source = lax.rem(me + n - i, n)
        for a in range(count):
            remote(a, peer, me).wait_send()
            remote(a, source, source).wait_recv()
        return carry

    lax.fori_loop(1, n, finish, 0)
    for copy in local:
        copy.wait()


def expert_exchange(arrays, collective_id):
    n = arrays[0].shape[0]
    count = len(arrays)
    return pl.pallas_call(
        functools.partial(exchange_kernel, n, count),
        out_shape=[jax.ShapeDtypeStruct(a.shape, a.dtype) for a in arrays],
        in_specs=[pl.BlockSpec(memory_space=pl.ANY)] * count,
        out_specs=[pl.BlockSpec(memory_space=pl.ANY)] * count,
        scratch_shapes=[
            pltpu.SemaphoreType.DMA((count, n)),
            pltpu.SemaphoreType.DMA((count, n)),
            pltpu.SemaphoreType.DMA((count,)),
        ],
        compiler_params=pltpu.CompilerParams(
            collective_id=collective_id, has_side_effects=True
        ),
    )(*arrays)


def on_device(tokens, out_grad, expert_ids, gates, w_gate, w_up, w_down):
    expert_count = lax.axis_size("expert")
    tok_rows = tokens.shape[0]
    model_width = tokens.shape[1]
    per_token = expert_ids.shape[1]
    hidden = w_gate.shape[2]
    entries = tok_rows * per_token
    slot_depth = 3 * entries // expert_count
    slot_count = expert_count * slot_depth
    flat_ids = expert_ids.reshape(entries)
    onehot = (flat_ids[:, None] == jnp.arange(expert_count, dtype=jnp.int32)[None, :]).astype(
        jnp.int32
    )
    before = jnp.cumsum(onehot, axis=0) - onehot
    ranking = jnp.sum(before * onehot, axis=1)
    slot_of_entry = flat_ids * slot_depth + ranking
    source = (
        jnp.full((slot_count,), entries, jnp.int32)
        .at[slot_of_entry]
        .set(jnp.arange(entries, dtype=jnp.int32))
    )
    entry_scaled = (
        (gates[:, :, None] * out_grad.astype(jnp.float32)[:, None, :])
        .astype(jnp.bfloat16)
        .reshape(entries, model_width)
    )
    grad_table = jnp.concatenate([entry_scaled, jnp.zeros((1, model_width), jnp.bfloat16)], axis=0)
    input_table = jnp.concatenate([tokens, jnp.zeros((1, model_width), tokens.dtype)], axis=0)
    picks = source.reshape(expert_count, slot_depth)
    send_grads = grad_table[picks]
    send_inputs = input_table[picks // per_token]
    rows_in, grads_in = expert_exchange([send_inputs, send_grads], 0)
    local_joined = jnp.concatenate([w_gate[0], w_up[0]], axis=1)
    full_joined, full_down = (
        lax.all_gather(local_joined, "dp", axis=0, tiled=True),
        lax.all_gather(w_down[0], "dp", axis=1, tiled=True),
    )
    preact = lax.dot_general(
        rows_in, full_joined, (((2,), (0,)), ((), ())), preferred_element_type=jnp.float32
    )
    hidden_grad = lax.dot_general(
        grads_in, full_down, (((2,), (1,)), ((), ())), preferred_element_type=jnp.float32
    )
    gate_pre = preact[:, :, :hidden]
    up_pre = preact[:, :, hidden:]
    sigmoid = jax.nn.sigmoid(gate_pre)
    silu_value = gate_pre * sigmoid
    activated = (silu_value * up_pre).astype(jnp.bfloat16)
    gate_side = (hidden_grad * up_pre * sigmoid * (1.0 + gate_pre * (1.0 - sigmoid))).astype(
        jnp.bfloat16
    )
    up_side = (hidden_grad * silu_value).astype(jnp.bfloat16)
    both_sides = jnp.concatenate([gate_side, up_side], axis=2)
    slot_grad = lax.dot_general(
        both_sides, full_joined, (((2,), (1,)), ((), ())), preferred_element_type=jnp.float32
    ).astype(jnp.bfloat16)
    returned = expert_exchange([slot_grad], 1)[0]
    picked = returned[flat_ids, ranking].astype(jnp.float32).reshape(tok_rows, per_token, model_width)
    input_grad = jnp.sum(picked, axis=1).astype(jnp.bfloat16)
    down_part = lax.dot_general(
        activated, grads_in, (((0, 1), (0, 1)), ((), ())), preferred_element_type=jnp.float32
    )
    down_grad = lax.psum(down_part.astype(jnp.bfloat16), "dp")[None]
    joined_grad = lax.psum_scatter(
        lax.dot_general(
            rows_in, both_sides, (((0, 1), (0, 1)), ((), ())), preferred_element_type=jnp.float32
        ).astype(jnp.bfloat16),
        "dp",
        scatter_dimension=0,
        tiled=True,
    )
    gate_grad = joined_grad[:, :hidden][None]
    up_grad = joined_grad[:, hidden:][None]
    return (input_grad, gate_grad, up_grad, down_grad)


def solution(mesh):
    in_specs = (
        P(("dp", "expert"), None),
        P(("dp", "expert"), None),
        P(("dp", "expert"), None),
        P(("dp", "expert"), None),
        P("expert", "dp", None),
        P("expert", "dp", None),
        P("expert", None, "dp"),
    )
    out_specs = (
        P(("dp", "expert"), None),
        P("expert", "dp", None),
        P("expert", "dp", None),
        P("expert", None, None),
    )
    return jax.shard_map(
        on_device, mesh=mesh, in_specs=in_specs, out_specs=out_specs, check_vma=False
    )
```

```python
import functools
import jax
import jax.numpy as jnp
from jax import lax
from jax.experimental import pallas as pl
from jax.experimental.pallas import tpu as pltpu
from jax.sharding import PartitionSpec as P

MESH = pl.DeviceIdType.MESH


def exchange_kernel(n, count, *refs):
    sources = refs[:count]
    targets = refs[count : 2 * count]
    send_sem, recv_sem, local_sem = refs[2 * count :]
    me = lax.axis_index("expert")
    row = lax.axis_index("dp")
    barrier = pltpu.get_barrier_semaphore()

    def greet(i, carry):
        peer = lax.rem(me + i, n)
        pl.semaphore_signal(barrier, inc=1, device_id=(row, peer), device_id_type=MESH)
        return carry

    lax.fori_loop(1, n, greet, 0)
    pl.semaphore_wait(barrier, n - 1)
    local = [
        pltpu.make_async_copy(sources[a].at[me], targets[a].at[me], local_sem.at[a])
        for a in range(count)
    ]
    for copy in local:
        copy.start()

    def remote(a, peer, slot):
        return pltpu.make_async_remote_copy(
            src_ref=sources[a].at[peer],
            dst_ref=targets[a].at[slot],
            send_sem=send_sem.at[a, peer],
            recv_sem=recv_sem.at[a, slot],
            device_id=(row, peer),
            device_id_type=MESH,
        )

    def start(i, carry):
        peer = lax.rem(me + i, n)
        for a in range(count):
            remote(a, peer, me).start()
        return carry

    lax.fori_loop(1, n, start, 0)

    def finish(i, carry):
        peer = lax.rem(me + i, n)
        source = lax.rem(me + n - i, n)
        for a in range(count):
            remote(a, peer, me).wait_send()
            remote(a, source, source).wait_recv()
        return carry

    lax.fori_loop(1, n, finish, 0)
    for copy in local:
        copy.wait()


def expert_exchange(arrays, collective_id):
    n = arrays[0].shape[0]
    count = len(arrays)
    return pl.pallas_call(
        functools.partial(exchange_kernel, n, count),
        out_shape=[jax.ShapeDtypeStruct(a.shape, a.dtype) for a in arrays],
        in_specs=[pl.BlockSpec(memory_space=pl.ANY)] * count,
        out_specs=[pl.BlockSpec(memory_space=pl.ANY)] * count,
        scratch_shapes=[
            pltpu.SemaphoreType.DMA((count, n)),
            pltpu.SemaphoreType.DMA((count, n)),
            pltpu.SemaphoreType.DMA((count,)),
        ],
        compiler_params=pltpu.CompilerParams(
            collective_id=collective_id, has_side_effects=True
        ),
    )(*arrays)


def return_kernel(n, groups, slot_ref, part_ref, out_ref, down_ref, send_sem, recv_sem,
                  local_sem, rs_send, rs_recv, ag_send, ag_recv, own_sem, parts, reduced):
    me = lax.axis_index("expert")
    row = lax.axis_index("dp")
    rows = reduced.shape[0]
    barrier = pltpu.get_barrier_semaphore()

    def greet(i, carry):
        peer = lax.rem(me + i, n)
        pl.semaphore_signal(barrier, inc=1, device_id=(row, peer), device_id_type=MESH)
        return carry

    def greet_group(i, carry):
        other = lax.rem(row + i, groups)
        pl.semaphore_signal(barrier, inc=1, device_id=(other, me), device_id_type=MESH)
        return carry

    lax.fori_loop(1, n, greet, 0)
    lax.fori_loop(1, groups, greet_group, 0)
    pl.semaphore_wait(barrier, n - 1 + groups - 1)
    local = pltpu.make_async_copy(slot_ref.at[me], out_ref.at[me], local_sem)
    local.start()

    def remote(peer, slot):
        return pltpu.make_async_remote_copy(
            src_ref=slot_ref.at[peer],
            dst_ref=out_ref.at[slot],
            send_sem=send_sem.at[peer],
            recv_sem=recv_sem.at[slot],
            device_id=(row, peer),
            device_id_type=MESH,
        )

    def start(i, carry):
        remote(lax.rem(me + i, n), me).start()
        return carry

    lax.fori_loop(1, n, start, 0)

    def scatter_copy(other, slot):
        return pltpu.make_async_remote_copy(
            src_ref=part_ref.at[pl.ds(pl.multiple_of(other * rows, rows), rows)],
            dst_ref=parts.at[slot],
            send_sem=rs_send.at[other],
            recv_sem=rs_recv.at[slot],
            device_id=(other, me),
            device_id_type=MESH,
        )

    own = pltpu.make_async_copy(
        part_ref.at[pl.ds(pl.multiple_of(row * rows, rows), rows)], parts.at[row], own_sem.at[0]
    )
    own.start()

    def scatter_start(i, carry):
        scatter_copy(lax.rem(row + i, groups), row).start()
        return carry

    lax.fori_loop(1, groups, scatter_start, 0)

    def scatter_finish(i, carry):
        scatter_copy(lax.rem(row + i, groups), row).wait_send()
        source = lax.rem(row + groups - i, groups)
        scatter_copy(source, source).wait_recv()
        return carry

    lax.fori_loop(1, groups, scatter_finish, 0)
    own.wait()
    total = parts[0].astype(jnp.float32)
    for slot in range(1, groups):
        total = total + parts[slot].astype(jnp.float32)
    reduced[...] = total.astype(reduced.dtype)

    def gather_copy(other, slot):
        return pltpu.make_async_remote_copy(
            src_ref=reduced,
            dst_ref=down_ref.at[pl.ds(pl.multiple_of(slot * rows, rows), rows)],
            send_sem=ag_send.at[other],
            recv_sem=ag_recv.at[slot],
            device_id=(other, me),
            device_id_type=MESH,
        )

    keep = pltpu.make_async_copy(
        reduced, down_ref.at[pl.ds(pl.multiple_of(row * rows, rows), rows)], own_sem.at[1]
    )
    keep.start()

    def gather_start(i, carry):
        gather_copy(lax.rem(row + i, groups), row).start()
        return carry

    lax.fori_loop(1, groups, gather_start, 0)

    def gather_finish(i, carry):
        gather_copy(lax.rem(row + i, groups), row).wait_send()
        source = lax.rem(row + groups - i, groups)
        gather_copy(source, source).wait_recv()
        return carry

    lax.fori_loop(1, groups, gather_finish, 0)
    keep.wait()

    def finish(i, carry):
        remote(lax.rem(me + i, n), me).wait_send()
        source = lax.rem(me + n - i, n)
        remote(source, source).wait_recv()
        return carry

    lax.fori_loop(1, n, finish, 0)
    local.wait()


def return_and_reduce(slot_grad, down_part, groups, collective_id):
    n = slot_grad.shape[0]
    rows = down_part.shape[0] // groups
    return pl.pallas_call(
        functools.partial(return_kernel, n, groups),
        out_shape=[
            jax.ShapeDtypeStruct(slot_grad.shape, slot_grad.dtype),
            jax.ShapeDtypeStruct(down_part.shape, down_part.dtype),
        ],
        in_specs=[pl.BlockSpec(memory_space=pl.ANY)] * 2,
        out_specs=[pl.BlockSpec(memory_space=pl.ANY)] * 2,
        scratch_shapes=[
            pltpu.SemaphoreType.DMA((n,)),
            pltpu.SemaphoreType.DMA((n,)),
            pltpu.SemaphoreType.DMA(()),
            pltpu.SemaphoreType.DMA((groups,)),
            pltpu.SemaphoreType.DMA((groups,)),
            pltpu.SemaphoreType.DMA((groups,)),
            pltpu.SemaphoreType.DMA((groups,)),
            pltpu.SemaphoreType.DMA((2,)),
            pltpu.VMEM((groups, rows, down_part.shape[1]), down_part.dtype),
            pltpu.VMEM((rows, down_part.shape[1]), down_part.dtype),
        ],
        compiler_params=pltpu.CompilerParams(
            collective_id=collective_id, has_side_effects=True
        ),
    )(slot_grad, down_part)


def on_device(tokens, out_grad, expert_ids, gates, w_gate, w_up, w_down):
    expert_count = lax.axis_size("expert")
    tok_rows = tokens.shape[0]
    model_width = tokens.shape[1]
    per_token = expert_ids.shape[1]
    hidden = w_gate.shape[2]
    entries = tok_rows * per_token
    slot_depth = 3 * entries // expert_count
    slot_count = expert_count * slot_depth
    flat_ids = expert_ids.reshape(entries)
    onehot = (flat_ids[:, None] == jnp.arange(expert_count, dtype=jnp.int32)[None, :]).astype(
        jnp.int32
    )
    before = jnp.cumsum(onehot, axis=0) - onehot
    ranking = jnp.sum(before * onehot, axis=1)
    slot_of_entry = flat_ids * slot_depth + ranking
    source = (
        jnp.full((slot_count,), entries, jnp.int32)
        .at[slot_of_entry]
        .set(jnp.arange(entries, dtype=jnp.int32))
    )
    entry_scaled = (
        (gates[:, :, None] * out_grad.astype(jnp.float32)[:, None, :])
        .astype(jnp.bfloat16)
        .reshape(entries, model_width)
    )
    grad_table = jnp.concatenate([entry_scaled, jnp.zeros((1, model_width), jnp.bfloat16)], axis=0)
    input_table = jnp.concatenate([tokens, jnp.zeros((1, model_width), tokens.dtype)], axis=0)
    picks = source.reshape(expert_count, slot_depth)
    send_grads = grad_table[picks]
    send_inputs = input_table[picks // per_token]
    rows_in, grads_in = expert_exchange([send_inputs, send_grads], 0)
    local_joined = jnp.concatenate([w_gate[0], w_up[0]], axis=1)
    full_joined, full_down = (
        lax.all_gather(local_joined, "dp", axis=0, tiled=True),
        lax.all_gather(w_down[0], "dp", axis=1, tiled=True),
    )
    preact = lax.dot_general(
        rows_in, full_joined, (((2,), (0,)), ((), ())), preferred_element_type=jnp.float32
    )
    hidden_grad = lax.dot_general(
        grads_in, full_down, (((2,), (1,)), ((), ())), preferred_element_type=jnp.float32
    )
    gate_pre = preact[:, :, :hidden]
    up_pre = preact[:, :, hidden:]
    sigmoid = jax.nn.sigmoid(gate_pre)
    silu_value = gate_pre * sigmoid
    activated = (silu_value * up_pre).astype(jnp.bfloat16)
    gate_side = (hidden_grad * up_pre * sigmoid * (1.0 + gate_pre * (1.0 - sigmoid))).astype(
        jnp.bfloat16
    )
    up_side = (hidden_grad * silu_value).astype(jnp.bfloat16)
    both_sides = jnp.concatenate([gate_side, up_side], axis=2)
    slot_grad = lax.dot_general(
        both_sides, full_joined, (((2,), (1,)), ((), ())), preferred_element_type=jnp.float32
    ).astype(jnp.bfloat16)
    down_part = lax.dot_general(
        activated, grads_in, (((0, 1), (0, 1)), ((), ())), preferred_element_type=jnp.float32
    ).astype(jnp.bfloat16)
    returned, down_grad = return_and_reduce(slot_grad, down_part, lax.axis_size("dp"), 1)
    down_grad = down_grad[None]
    picked = returned[flat_ids, ranking].astype(jnp.float32).reshape(tok_rows, per_token, model_width)
    input_grad = jnp.sum(picked, axis=1).astype(jnp.bfloat16)
    joined_grad = lax.psum_scatter(
        lax.dot_general(
            rows_in, both_sides, (((0, 1), (0, 1)), ((), ())), preferred_element_type=jnp.float32
        ).astype(jnp.bfloat16),
        "dp",
        scatter_dimension=0,
        tiled=True,
    )
    gate_grad = joined_grad[:, :hidden][None]
    up_grad = joined_grad[:, hidden:][None]
    return (input_grad, gate_grad, up_grad, down_grad)


def solution(mesh):
    in_specs = (
        P(("dp", "expert"), None),
        P(("dp", "expert"), None),
        P(("dp", "expert"), None),
        P(("dp", "expert"), None),
        P("expert", "dp", None),
        P("expert", "dp", None),
        P("expert", None, "dp"),
    )
    out_specs = (
        P(("dp", "expert"), None),
        P("expert", "dp", None),
        P("expert", "dp", None),
        P("expert", None, None),
    )
    return jax.shard_map(
        on_device, mesh=mesh, in_specs=in_specs, out_specs=out_specs, check_vma=False
    )
```

```python
import functools
import jax
import jax.numpy as jnp
from jax import lax
from jax.experimental import pallas as pl
from jax.experimental.pallas import tpu as pltpu
from jax.sharding import PartitionSpec as P

MESH = pl.DeviceIdType.MESH


def forward_kernel(n, groups, inputs_ref, grads_ref, wg_ref, wu_ref, wd_ref, inputs_out,
                   grads_out, joined_out, down_out, send_sem, recv_sem, local_sem, ag_send,
                   ag_recv, own_sem):
    me = lax.axis_index("expert")
    row = lax.axis_index("dp")
    width = wg_ref.shape[1]
    piece = wg_ref.shape[0]
    columns = wd_ref.shape[1]
    barrier = pltpu.get_barrier_semaphore()

    def greet(i, carry):
        peer = lax.rem(me + i, n)
        pl.semaphore_signal(barrier, inc=1, device_id=(row, peer), device_id_type=MESH)
        return carry

    def greet_group(i, carry):
        other = lax.rem(row + i, groups)
        pl.semaphore_signal(barrier, inc=1, device_id=(other, me), device_id_type=MESH)
        return carry

    lax.fori_loop(1, n, greet, 0)
    lax.fori_loop(1, groups, greet_group, 0)
    pl.semaphore_wait(barrier, n - 1 + groups - 1)
    sources = (inputs_ref, grads_ref)
    targets = (inputs_out, grads_out)
    local = [
        pltpu.make_async_copy(sources[a].at[me], targets[a].at[me], local_sem.at[a])
        for a in range(2)
    ]
    for copy in local:
        copy.start()

    def remote(a, peer, slot):
        return pltpu.make_async_remote_copy(
            src_ref=sources[a].at[peer],
            dst_ref=targets[a].at[slot],
            send_sem=send_sem.at[a, peer],
            recv_sem=recv_sem.at[a, slot],
            device_id=(row, peer),
            device_id_type=MESH,
        )

    def start(i, carry):
        peer = lax.rem(me + i, n)
        for a in range(2):
            remote(a, peer, me).start()
        return carry

    lax.fori_loop(1, n, start, 0)

    def places(slot):
        rows = pl.ds(pl.multiple_of(slot * piece, piece), piece)
        cols = pl.ds(pl.multiple_of(slot * columns, columns), columns)
        return (
            (wg_ref, joined_out.at[rows, pl.ds(0, width)]),
            (wu_ref, joined_out.at[rows, pl.ds(width, width)]),
            (wd_ref, down_out.at[:, cols]),
        )

    def gather_copy(k, other, slot):
        src, dst = places(slot)[k]
        return pltpu.make_async_remote_copy(
            src_ref=src,
            dst_ref=dst,
            send_sem=ag_send.at[k, other],
            recv_sem=ag_recv.at[k, slot],
            device_id=(other, me),
            device_id_type=MESH,
        )

    own = [
        pltpu.make_async_copy(src, dst, own_sem.at[k])
        for k, (src, dst) in enumerate(places(row))
    ]
    for copy in own:
        copy.start()

    def gather_start(i, carry):
        other = lax.rem(row + i, groups)
        for k in range(3):
            gather_copy(k, other, row).start()
        return carry

    lax.fori_loop(1, groups, gather_start, 0)

    def gather_finish(i, carry):
        other = lax.rem(row + i, groups)
        source = lax.rem(row + groups - i, groups)
        for k in range(3):
            gather_copy(k, other, row).wait_send()
            gather_copy(k, source, source).wait_recv()
        return carry

    lax.fori_loop(1, groups, gather_finish, 0)
    for copy in own:
        copy.wait()

    def finish(i, carry):
        peer = lax.rem(me + i, n)
        source = lax.rem(me + n - i, n)
        for a in range(2):
            remote(a, peer, me).wait_send()
            remote(a, source, source).wait_recv()
        return carry

    lax.fori_loop(1, n, finish, 0)
    for copy in local:
        copy.wait()


def forward_exchange(send_inputs, send_grads, wg, wu, wd, groups, collective_id):
    n = send_inputs.shape[0]
    any_spec = pl.BlockSpec(memory_space=pl.ANY)
    return pl.pallas_call(
        functools.partial(forward_kernel, n, groups),
        out_shape=[
            jax.ShapeDtypeStruct(send_inputs.shape, send_inputs.dtype),
            jax.ShapeDtypeStruct(send_grads.shape, send_grads.dtype),
            jax.ShapeDtypeStruct((groups * wg.shape[0], 2 * wg.shape[1]), wg.dtype),
            jax.ShapeDtypeStruct((wd.shape[0], groups * wd.shape[1]), wd.dtype),
        ],
        in_specs=[any_spec] * 5,
        out_specs=[any_spec] * 4,
        scratch_shapes=[
            pltpu.SemaphoreType.DMA((2, n)),
            pltpu.SemaphoreType.DMA((2, n)),
            pltpu.SemaphoreType.DMA((2,)),
            pltpu.SemaphoreType.DMA((3, groups)),
            pltpu.SemaphoreType.DMA((3, groups)),
            pltpu.SemaphoreType.DMA((3,)),
        ],
        compiler_params=pltpu.CompilerParams(
            collective_id=collective_id, has_side_effects=True
        ),
    )(send_inputs, send_grads, wg, wu, wd)


def return_kernel(n, groups, slot_ref, part_ref, joined_ref, out_ref, down_ref, gate_ref, up_ref,
                  send_sem, recv_sem, local_sem, rs_send, rs_recv, ag_send, ag_recv, js_send,
                  js_recv, own_sem, parts, reduced, joined_parts, joined_sum):
    me = lax.axis_index("expert")
    row = lax.axis_index("dp")
    rows = reduced.shape[0]
    joined_rows = joined_sum.shape[0]
    width = gate_ref.shape[1]
    barrier = pltpu.get_barrier_semaphore()

    def greet(i, carry):
        peer = lax.rem(me + i, n)
        pl.semaphore_signal(barrier, inc=1, device_id=(row, peer), device_id_type=MESH)
        return carry

    def greet_group(i, carry):
        other = lax.rem(row + i, groups)
        pl.semaphore_signal(barrier, inc=1, device_id=(other, me), device_id_type=MESH)
        return carry

    lax.fori_loop(1, n, greet, 0)
    lax.fori_loop(1, groups, greet_group, 0)
    pl.semaphore_wait(barrier, n - 1 + groups - 1)
    local = pltpu.make_async_copy(slot_ref.at[me], out_ref.at[me], local_sem)
    local.start()

    def remote(peer, slot):
        return pltpu.make_async_remote_copy(
            src_ref=slot_ref.at[peer],
            dst_ref=out_ref.at[slot],
            send_sem=send_sem.at[peer],
            recv_sem=recv_sem.at[slot],
            device_id=(row, peer),
            device_id_type=MESH,
        )

    def start(i, carry):
        remote(lax.rem(me + i, n), me).start()
        return carry

    lax.fori_loop(1, n, start, 0)

    def scatter_copy(other, slot):
        return pltpu.make_async_remote_copy(
            src_ref=part_ref.at[pl.ds(pl.multiple_of(other * rows, rows), rows)],
            dst_ref=parts.at[slot],
            send_sem=rs_send.at[other],
            recv_sem=rs_recv.at[slot],
            device_id=(other, me),
            device_id_type=MESH,
        )

    def joined_copy(other, slot):
        return pltpu.make_async_remote_copy(
            src_ref=joined_ref.at[pl.ds(pl.multiple_of(other * joined_rows, joined_rows), joined_rows)],
            dst_ref=joined_parts.at[slot],
            send_sem=js_send.at[other],
            recv_sem=js_recv.at[slot],
            device_id=(other, me),
            device_id_type=MESH,
        )

    own = pltpu.make_async_copy(
        part_ref.at[pl.ds(pl.multiple_of(row * rows, rows), rows)], parts.at[row], own_sem.at[0]
    )
    own.start()
    own_joined = pltpu.make_async_copy(
        joined_ref.at[pl.ds(pl.multiple_of(row * joined_rows, joined_rows), joined_rows)],
        joined_parts.at[row],
        own_sem.at[2],
    )
    own_joined.start()

    def scatter_start(i, carry):
        other = lax.rem(row + i, groups)
        scatter_copy(other, row).start()
        joined_copy(other, row).start()
        return carry

    lax.fori_loop(1, groups, scatter_start, 0)

    def scatter_finish(i, carry):
        scatter_copy(lax.rem(row + i, groups), row).wait_send()
        source = lax.rem(row + groups - i, groups)
        scatter_copy(source, source).wait_recv()
        return carry

    lax.fori_loop(1, groups, scatter_finish, 0)
    own.wait()
    total = parts[0].astype(jnp.float32)
    for slot in range(1, groups):
        total = total + parts[slot].astype(jnp.float32)
    reduced[...] = total.astype(reduced.dtype)

    def gather_copy(other, slot):
        return pltpu.make_async_remote_copy(
            src_ref=reduced,
            dst_ref=down_ref.at[pl.ds(pl.multiple_of(slot * rows, rows), rows)],
            send_sem=ag_send.at[other],
            recv_sem=ag_recv.at[slot],
            device_id=(other, me),
            device_id_type=MESH,
        )

    keep = pltpu.make_async_copy(
        reduced, down_ref.at[pl.ds(pl.multiple_of(row * rows, rows), rows)], own_sem.at[1]
    )
    keep.start()

    def gather_start(i, carry):
        gather_copy(lax.rem(row + i, groups), row).start()
        return carry

    lax.fori_loop(1, groups, gather_start, 0)

    def joined_finish(i, carry):
        joined_copy(lax.rem(row + i, groups), row).wait_send()
        source = lax.rem(row + groups - i, groups)
        joined_copy(source, source).wait_recv()
        return carry

    lax.fori_loop(1, groups, joined_finish, 0)
    own_joined.wait()
    joined_total = joined_parts[0].astype(jnp.float32)
    for slot in range(1, groups):
        joined_total = joined_total + joined_parts[slot].astype(jnp.float32)
    joined_sum[...] = joined_total.astype(joined_sum.dtype)
    halves = [
        pltpu.make_async_copy(joined_sum.at[:, pl.ds(0, width)], gate_ref, own_sem.at[3]),
        pltpu.make_async_copy(joined_sum.at[:, pl.ds(width, width)], up_ref, own_sem.at[4]),
    ]
    for copy in halves:
        copy.start()

    def gather_finish(i, carry):
        gather_copy(lax.rem(row + i, groups), row).wait_send()
        source = lax.rem(row + groups - i, groups)
        gather_copy(source, source).wait_recv()
        return carry

    lax.fori_loop(1, groups, gather_finish, 0)
    keep.wait()
    for copy in halves:
        copy.wait()

    def finish(i, carry):
        remote(lax.rem(me + i, n), me).wait_send()
        source = lax.rem(me + n - i, n)
        remote(source, source).wait_recv()
        return carry

    lax.fori_loop(1, n, finish, 0)
    local.wait()


def return_and_reduce(slot_grad, down_part, joined_part, groups, collective_id):
    n = slot_grad.shape[0]
    rows = down_part.shape[0] // groups
    joined_rows = joined_part.shape[0] // groups
    width = joined_part.shape[1] // 2
    any_spec = pl.BlockSpec(memory_space=pl.ANY)
    return pl.pallas_call(
        functools.partial(return_kernel, n, groups),
        out_shape=[
            jax.ShapeDtypeStruct(slot_grad.shape, slot_grad.dtype),
            jax.ShapeDtypeStruct(down_part.shape, down_part.dtype),
            jax.ShapeDtypeStruct((joined_rows, width), joined_part.dtype),
            jax.ShapeDtypeStruct((joined_rows, width), joined_part.dtype),
        ],
        in_specs=[any_spec] * 3,
        out_specs=[any_spec] * 4,
        scratch_shapes=[
            pltpu.SemaphoreType.DMA((n,)),
            pltpu.SemaphoreType.DMA((n,)),
            pltpu.SemaphoreType.DMA(()),
            pltpu.SemaphoreType.DMA((groups,)),
            pltpu.SemaphoreType.DMA((groups,)),
            pltpu.SemaphoreType.DMA((groups,)),
            pltpu.SemaphoreType.DMA((groups,)),
            pltpu.SemaphoreType.DMA((groups,)),
            pltpu.SemaphoreType.DMA((groups,)),
            pltpu.SemaphoreType.DMA((5,)),
            pltpu.VMEM((groups, rows, down_part.shape[1]), down_part.dtype),
            pltpu.VMEM((rows, down_part.shape[1]), down_part.dtype),
            pltpu.VMEM((groups, joined_rows, joined_part.shape[1]), joined_part.dtype),
            pltpu.VMEM((joined_rows, joined_part.shape[1]), joined_part.dtype),
        ],
        compiler_params=pltpu.CompilerParams(
            collective_id=collective_id, has_side_effects=True
        ),
    )(slot_grad, down_part, joined_part)


def on_device(tokens, out_grad, expert_ids, gates, w_gate, w_up, w_down):
    expert_count = lax.axis_size("expert")
    tok_rows = tokens.shape[0]
    model_width = tokens.shape[1]
    per_token = expert_ids.shape[1]
    hidden = w_gate.shape[2]
    entries = tok_rows * per_token
    slot_depth = 3 * entries // expert_count
    slot_count = expert_count * slot_depth
    flat_ids = expert_ids.reshape(entries)
    onehot = (flat_ids[:, None] == jnp.arange(expert_count, dtype=jnp.int32)[None, :]).astype(
        jnp.int32
    )
    before = jnp.cumsum(onehot, axis=0) - onehot
    ranking = jnp.sum(before * onehot, axis=1)
    slot_of_entry = flat_ids * slot_depth + ranking
    source = (
        jnp.full((slot_count,), entries, jnp.int32)
        .at[slot_of_entry]
        .set(jnp.arange(entries, dtype=jnp.int32))
    )
    entry_scaled = (
        (gates[:, :, None] * out_grad.astype(jnp.float32)[:, None, :])
        .astype(jnp.bfloat16)
        .reshape(entries, model_width)
    )
    grad_table = jnp.concatenate([entry_scaled, jnp.zeros((1, model_width), jnp.bfloat16)], axis=0)
    input_table = jnp.concatenate([tokens, jnp.zeros((1, model_width), tokens.dtype)], axis=0)
    picks = source.reshape(expert_count, slot_depth)
    send_grads = grad_table[picks]
    send_inputs = input_table[picks // per_token]
    groups = lax.axis_size("dp")
    rows_in, grads_in, full_joined, full_down = forward_exchange(
        send_inputs, send_grads, w_gate[0], w_up[0], w_down[0], groups, 0
    )
    preact = lax.dot_general(
        rows_in, full_joined, (((2,), (0,)), ((), ())), preferred_element_type=jnp.float32
    )
    hidden_grad = lax.dot_general(
        grads_in, full_down, (((2,), (1,)), ((), ())), preferred_element_type=jnp.float32
    )
    gate_pre = preact[:, :, :hidden]
    up_pre = preact[:, :, hidden:]
    sigmoid = jax.nn.sigmoid(gate_pre)
    silu_value = gate_pre * sigmoid
    activated = (silu_value * up_pre).astype(jnp.bfloat16)
    gate_side = (hidden_grad * up_pre * sigmoid * (1.0 + gate_pre * (1.0 - sigmoid))).astype(
        jnp.bfloat16
    )
    up_side = (hidden_grad * silu_value).astype(jnp.bfloat16)
    both_sides = jnp.concatenate([gate_side, up_side], axis=2)
    slot_grad = lax.dot_general(
        both_sides, full_joined, (((2,), (1,)), ((), ())), preferred_element_type=jnp.float32
    ).astype(jnp.bfloat16)
    down_part = lax.dot_general(
        activated, grads_in, (((0, 1), (0, 1)), ((), ())), preferred_element_type=jnp.float32
    ).astype(jnp.bfloat16)
    joined_part = lax.dot_general(
        rows_in, both_sides, (((0, 1), (0, 1)), ((), ())), preferred_element_type=jnp.float32
    ).astype(jnp.bfloat16)
    returned, down_grad, gate_grad, up_grad = return_and_reduce(
        slot_grad, down_part, joined_part, groups, 1
    )
    picked = returned[flat_ids, ranking].astype(jnp.float32).reshape(tok_rows, per_token, model_width)
    input_grad = jnp.sum(picked, axis=1).astype(jnp.bfloat16)
    down_grad = down_grad[None]
    gate_grad = gate_grad[None]
    up_grad = up_grad[None]
    return (input_grad, gate_grad, up_grad, down_grad)


def solution(mesh):
    in_specs = (
        P(("dp", "expert"), None),
        P(("dp", "expert"), None),
        P(("dp", "expert"), None),
        P(("dp", "expert"), None),
        P("expert", "dp", None),
        P("expert", "dp", None),
        P("expert", None, "dp"),
    )
    out_specs = (
        P(("dp", "expert"), None),
        P("expert", "dp", None),
        P("expert", "dp", None),
        P("expert", None, None),
    )
    return jax.shard_map(
        on_device, mesh=mesh, in_specs=in_specs, out_specs=out_specs, check_vma=False
    )
```

```python
import functools
import jax
import jax.numpy as jnp
from jax import lax
from jax.experimental import pallas as pl
from jax.experimental.pallas import tpu as pltpu
from jax.sharding import PartitionSpec as P

MESH = pl.DeviceIdType.MESH


def forward_kernel(n, groups, inputs_ref, grads_ref, wg_ref, wu_ref, wd_ref, inputs_out,
                   grads_out, joined_out, down_out, send_sem, recv_sem, local_sem, ag_send,
                   ag_recv, own_sem):
    me = lax.axis_index("expert")
    row = lax.axis_index("dp")
    width = wg_ref.shape[1]
    piece = wg_ref.shape[0]
    columns = wd_ref.shape[1]
    barrier = pltpu.get_barrier_semaphore()

    def greet(i, carry):
        peer = lax.rem(me + i, n)
        pl.semaphore_signal(barrier, inc=1, device_id=(row, peer), device_id_type=MESH)
        return carry

    def greet_group(i, carry):
        other = lax.rem(row + i, groups)
        pl.semaphore_signal(barrier, inc=1, device_id=(other, me), device_id_type=MESH)
        return carry

    lax.fori_loop(1, n, greet, 0)
    lax.fori_loop(1, groups, greet_group, 0)
    pl.semaphore_wait(barrier, n - 1 + groups - 1)
    sources = (inputs_ref, grads_ref)
    targets = (inputs_out, grads_out)
    local = [
        pltpu.make_async_copy(sources[a].at[me], targets[a].at[me], local_sem.at[a])
        for a in range(2)
    ]
    for copy in local:
        copy.start()

    def remote(a, peer, slot):
        return pltpu.make_async_remote_copy(
            src_ref=sources[a].at[peer],
            dst_ref=targets[a].at[slot],
            send_sem=send_sem.at[a, peer],
            recv_sem=recv_sem.at[a, slot],
            device_id=(row, peer),
            device_id_type=MESH,
        )

    def start(i, carry):
        peer = lax.rem(me + i, n)
        for a in range(2):
            remote(a, peer, me).start()
        return carry

    lax.fori_loop(1, n, start, 0)

    def places(slot):
        rows = pl.ds(pl.multiple_of(slot * piece, piece), piece)
        cols = pl.ds(pl.multiple_of(slot * columns, columns), columns)
        return (
            (wg_ref, joined_out.at[rows, pl.ds(0, width)]),
            (wu_ref, joined_out.at[rows, pl.ds(width, width)]),
            (wd_ref, down_out.at[:, cols]),
        )

    def gather_copy(k, other, slot):
        src, dst = places(slot)[k]
        return pltpu.make_async_remote_copy(
            src_ref=src,
            dst_ref=dst,
            send_sem=ag_send.at[k, other],
            recv_sem=ag_recv.at[k, slot],
            device_id=(other, me),
            device_id_type=MESH,
        )

    own = [
        pltpu.make_async_copy(src, dst, own_sem.at[k])
        for k, (src, dst) in enumerate(places(row))
    ]
    for copy in own:
        copy.start()

    def gather_start(i, carry):
        other = lax.rem(row + i, groups)
        for k in range(3):
            gather_copy(k, other, row).start()
        return carry

    lax.fori_loop(1, groups, gather_start, 0)

    def gather_finish(i, carry):
        other = lax.rem(row + i, groups)
        source = lax.rem(row + groups - i, groups)
        for k in range(3):
            gather_copy(k, other, row).wait_send()
            gather_copy(k, source, source).wait_recv()
        return carry

    lax.fori_loop(1, groups, gather_finish, 0)
    for copy in own:
        copy.wait()

    def finish(i, carry):
        peer = lax.rem(me + i, n)
        source = lax.rem(me + n - i, n)
        for a in range(2):
            remote(a, peer, me).wait_send()
            remote(a, source, source).wait_recv()
        return carry

    lax.fori_loop(1, n, finish, 0)
    for copy in local:
        copy.wait()


def forward_exchange(send_inputs, send_grads, wg, wu, wd, groups, collective_id):
    n = send_inputs.shape[0]
    any_spec = pl.BlockSpec(memory_space=pl.ANY)
    return pl.pallas_call(
        functools.partial(forward_kernel, n, groups),
        out_shape=[
            jax.ShapeDtypeStruct(send_inputs.shape, send_inputs.dtype),
            jax.ShapeDtypeStruct(send_grads.shape, send_grads.dtype),
            jax.ShapeDtypeStruct((groups * wg.shape[0], 2 * wg.shape[1]), wg.dtype),
            jax.ShapeDtypeStruct((wd.shape[0], groups * wd.shape[1]), wd.dtype),
        ],
        in_specs=[any_spec] * 5,
        out_specs=[any_spec] * 4,
        scratch_shapes=[
            pltpu.SemaphoreType.DMA((2, n)),
            pltpu.SemaphoreType.DMA((2, n)),
            pltpu.SemaphoreType.DMA((2,)),
            pltpu.SemaphoreType.DMA((3, groups)),
            pltpu.SemaphoreType.DMA((3, groups)),
            pltpu.SemaphoreType.DMA((3,)),
        ],
        compiler_params=pltpu.CompilerParams(
            collective_id=collective_id, has_side_effects=True
        ),
    )(send_inputs, send_grads, wg, wu, wd)


def return_kernel(n, groups, slot_ref, part_ref, joined_ref, out_ref, down_ref, gate_ref, up_ref,
                  send_sem, recv_sem, local_sem, rs_send, rs_recv, ag_send, ag_recv, js_send,
                  js_recv, own_sem, parts, reduced, joined_parts, joined_sum):
    me = lax.axis_index("expert")
    row = lax.axis_index("dp")
    rows = reduced.shape[0]
    joined_rows = joined_sum.shape[0]
    width = gate_ref.shape[1]
    barrier = pltpu.get_barrier_semaphore()

    def greet(i, carry):
        peer = lax.rem(me + i, n)
        pl.semaphore_signal(barrier, inc=1, device_id=(row, peer), device_id_type=MESH)
        return carry

    def greet_group(i, carry):
        other = lax.rem(row + i, groups)
        pl.semaphore_signal(barrier, inc=1, device_id=(other, me), device_id_type=MESH)
        return carry

    lax.fori_loop(1, n, greet, 0)
    lax.fori_loop(1, groups, greet_group, 0)
    pl.semaphore_wait(barrier, n - 1 + groups - 1)
    local = pltpu.make_async_copy(slot_ref.at[me], out_ref.at[me], local_sem)
    local.start()

    def remote(peer, slot):
        return pltpu.make_async_remote_copy(
            src_ref=slot_ref.at[peer],
            dst_ref=out_ref.at[slot],
            send_sem=send_sem.at[peer],
            recv_sem=recv_sem.at[slot],
            device_id=(row, peer),
            device_id_type=MESH,
        )

    def start(i, carry):
        remote(lax.rem(me + i, n), me).start()
        return carry

    lax.fori_loop(1, n, start, 0)

    def scatter_copy(other, slot):
        return pltpu.make_async_remote_copy(
            src_ref=part_ref.at[pl.ds(pl.multiple_of(other * rows, rows), rows)],
            dst_ref=parts.at[slot],
            send_sem=rs_send.at[other],
            recv_sem=rs_recv.at[slot],
            device_id=(other, me),
            device_id_type=MESH,
        )

    def joined_copy(other, slot):
        return pltpu.make_async_remote_copy(
            src_ref=joined_ref.at[pl.ds(pl.multiple_of(other * joined_rows, joined_rows), joined_rows)],
            dst_ref=joined_parts.at[slot],
            send_sem=js_send.at[other],
            recv_sem=js_recv.at[slot],
            device_id=(other, me),
            device_id_type=MESH,
        )

    own = pltpu.make_async_copy(
        part_ref.at[pl.ds(pl.multiple_of(row * rows, rows), rows)], parts.at[row], own_sem.at[0]
    )
    own.start()
    own_joined = pltpu.make_async_copy(
        joined_ref.at[pl.ds(pl.multiple_of(row * joined_rows, joined_rows), joined_rows)],
        joined_parts.at[row],
        own_sem.at[2],
    )
    own_joined.start()

    def scatter_start(i, carry):
        other = lax.rem(row + i, groups)
        scatter_copy(other, row).start()
        joined_copy(other, row).start()
        return carry

    lax.fori_loop(1, groups, scatter_start, 0)

    def scatter_finish(i, carry):
        scatter_copy(lax.rem(row + i, groups), row).wait_send()
        source = lax.rem(row + groups - i, groups)
        scatter_copy(source, source).wait_recv()
        return carry

    lax.fori_loop(1, groups, scatter_finish, 0)
    own.wait()
    total = parts[0].astype(jnp.float32)
    for slot in range(1, groups):
        total = total + parts[slot].astype(jnp.float32)
    reduced[...] = total.astype(reduced.dtype)

    def gather_copy(other, slot):
        return pltpu.make_async_remote_copy(
            src_ref=reduced,
            dst_ref=down_ref.at[pl.ds(pl.multiple_of(slot * rows, rows), rows)],
            send_sem=ag_send.at[other],
            recv_sem=ag_recv.at[slot],
            device_id=(other, me),
            device_id_type=MESH,
        )

    keep = pltpu.make_async_copy(
        reduced, down_ref.at[pl.ds(pl.multiple_of(row * rows, rows), rows)], own_sem.at[1]
    )
    keep.start()

    def gather_start(i, carry):
        gather_copy(lax.rem(row + i, groups), row).start()
        return carry

    lax.fori_loop(1, groups, gather_start, 0)

    def joined_finish(i, carry):
        joined_copy(lax.rem(row + i, groups), row).wait_send()
        source = lax.rem(row + groups - i, groups)
        joined_copy(source, source).wait_recv()
        return carry

    lax.fori_loop(1, groups, joined_finish, 0)
    own_joined.wait()
    joined_total = joined_parts[0].astype(jnp.float32)
    for slot in range(1, groups):
        joined_total = joined_total + joined_parts[slot].astype(jnp.float32)
    joined_sum[...] = joined_total.astype(joined_sum.dtype)
    halves = [
        pltpu.make_async_copy(joined_sum.at[:, pl.ds(0, width)], gate_ref, own_sem.at[3]),
        pltpu.make_async_copy(joined_sum.at[:, pl.ds(width, width)], up_ref, own_sem.at[4]),
    ]
    for copy in halves:
        copy.start()

    def gather_finish(i, carry):
        gather_copy(lax.rem(row + i, groups), row).wait_send()
        source = lax.rem(row + groups - i, groups)
        gather_copy(source, source).wait_recv()
        return carry

    lax.fori_loop(1, groups, gather_finish, 0)
    keep.wait()
    for copy in halves:
        copy.wait()

    def finish(i, carry):
        remote(lax.rem(me + i, n), me).wait_send()
        source = lax.rem(me + n - i, n)
        remote(source, source).wait_recv()
        return carry

    lax.fori_loop(1, n, finish, 0)
    local.wait()


def return_and_reduce(slot_grad, down_part, joined_part, groups, collective_id):
    n = slot_grad.shape[0]
    rows = down_part.shape[0] // groups
    joined_rows = joined_part.shape[0] // groups
    width = joined_part.shape[1] // 2
    any_spec = pl.BlockSpec(memory_space=pl.ANY)
    return pl.pallas_call(
        functools.partial(return_kernel, n, groups),
        out_shape=[
            jax.ShapeDtypeStruct(slot_grad.shape, slot_grad.dtype),
            jax.ShapeDtypeStruct(down_part.shape, down_part.dtype),
            jax.ShapeDtypeStruct((joined_rows, width), joined_part.dtype),
            jax.ShapeDtypeStruct((joined_rows, width), joined_part.dtype),
        ],
        in_specs=[any_spec] * 3,
        out_specs=[any_spec] * 4,
        scratch_shapes=[
            pltpu.SemaphoreType.DMA((n,)),
            pltpu.SemaphoreType.DMA((n,)),
            pltpu.SemaphoreType.DMA(()),
            pltpu.SemaphoreType.DMA((groups,)),
            pltpu.SemaphoreType.DMA((groups,)),
            pltpu.SemaphoreType.DMA((groups,)),
            pltpu.SemaphoreType.DMA((groups,)),
            pltpu.SemaphoreType.DMA((groups,)),
            pltpu.SemaphoreType.DMA((groups,)),
            pltpu.SemaphoreType.DMA((5,)),
            pltpu.VMEM((groups, rows, down_part.shape[1]), down_part.dtype),
            pltpu.VMEM((rows, down_part.shape[1]), down_part.dtype),
            pltpu.VMEM((groups, joined_rows, joined_part.shape[1]), joined_part.dtype),
            pltpu.VMEM((joined_rows, joined_part.shape[1]), joined_part.dtype),
        ],
        compiler_params=pltpu.CompilerParams(
            collective_id=collective_id, has_side_effects=True
        ),
    )(slot_grad, down_part, joined_part)


def on_device(tokens, out_grad, expert_ids, gates, w_gate, w_up, w_down):
    expert_count = lax.axis_size("expert")
    tok_rows = tokens.shape[0]
    model_width = tokens.shape[1]
    per_token = expert_ids.shape[1]
    hidden = w_gate.shape[2]
    entries = tok_rows * per_token
    slot_depth = 3 * entries // expert_count
    slot_count = expert_count * slot_depth
    flat_ids = expert_ids.reshape(entries)
    onehot = (flat_ids[:, None] == jnp.arange(expert_count, dtype=jnp.int32)[None, :]).astype(
        jnp.int32
    )
    before = jnp.cumsum(onehot, axis=0) - onehot
    ranking = jnp.sum(before * onehot, axis=1)
    slot_of_entry = flat_ids * slot_depth + ranking
    source = (
        jnp.full((slot_count,), entries, jnp.int32)
        .at[slot_of_entry]
        .set(jnp.arange(entries, dtype=jnp.int32))
    )
    entry_scaled = (
        (gates[:, :, None] * out_grad.astype(jnp.float32)[:, None, :])
        .astype(jnp.bfloat16)
        .reshape(entries, model_width)
    )
    grad_table = jnp.concatenate([entry_scaled, jnp.zeros((1, model_width), jnp.bfloat16)], axis=0)
    input_table = jnp.concatenate([tokens, jnp.zeros((1, model_width), tokens.dtype)], axis=0)
    picks = source.reshape(expert_count, slot_depth)
    send_grads = grad_table[picks]
    send_inputs = input_table[picks // per_token]
    groups = lax.axis_size("dp")
    rows_in, grads_in, full_joined, full_down = forward_exchange(
        send_inputs, send_grads, w_gate[0], w_up[0], w_down[0], groups, 0
    )
    preact = lax.dot_general(
        rows_in, full_joined, (((2,), (0,)), ((), ())), preferred_element_type=jnp.float32
    )
    hidden_grad = lax.dot_general(
        grads_in, full_down, (((2,), (1,)), ((), ())), preferred_element_type=jnp.float32
    )
    gate_pre = preact[:, :, :hidden]
    up_pre = preact[:, :, hidden:]
    sigmoid = jax.nn.sigmoid(gate_pre)
    silu_value = gate_pre * sigmoid
    activated = (silu_value * up_pre).astype(jnp.bfloat16)
    gate_side = (hidden_grad * up_pre * sigmoid * (1.0 + gate_pre * (1.0 - sigmoid))).astype(
        jnp.bfloat16
    )
    up_side = (hidden_grad * silu_value).astype(jnp.bfloat16)
    both_sides = jnp.concatenate([gate_side, up_side], axis=2)
    slot_grad = lax.dot_general(
        both_sides, full_joined, (((2,), (1,)), ((), ())), preferred_element_type=jnp.float32
    ).astype(jnp.bfloat16)
    down_part = lax.dot_general(
        activated, grads_in, (((0, 1), (0, 1)), ((), ())), preferred_element_type=jnp.float32
    ).astype(jnp.bfloat16)
    joined_part = lax.dot_general(
        rows_in, both_sides, (((0, 1), (0, 1)), ((), ())), preferred_element_type=jnp.float32
    ).astype(jnp.bfloat16)
    returned, down_grad, gate_grad, up_grad = return_and_reduce(
        slot_grad, down_part, joined_part, groups, 1
    )
    owner = (
        (flat_ids[:, None, None] == jnp.arange(expert_count, dtype=jnp.int32)[None, :, None])
        & (ranking[:, None, None] == jnp.arange(slot_depth, dtype=jnp.int32)[None, None, :])
    ).astype(jnp.bfloat16)
    input_grad = lax.dot_general(
        owner.reshape(tok_rows, per_token, expert_count, slot_depth).sum(axis=1),
        returned,
        (((1, 2), (0, 1)), ((), ())),
        preferred_element_type=jnp.float32,
    ).astype(jnp.bfloat16)
    down_grad = down_grad[None]
    gate_grad = gate_grad[None]
    up_grad = up_grad[None]
    return (input_grad, gate_grad, up_grad, down_grad)


def solution(mesh):
    in_specs = (
        P(("dp", "expert"), None),
        P(("dp", "expert"), None),
        P(("dp", "expert"), None),
        P(("dp", "expert"), None),
        P("expert", "dp", None),
        P("expert", "dp", None),
        P("expert", None, "dp"),
    )
    out_specs = (
        P(("dp", "expert"), None),
        P("expert", "dp", None),
        P("expert", "dp", None),
        P("expert", None, None),
    )
    return jax.shard_map(
        on_device, mesh=mesh, in_specs=in_specs, out_specs=out_specs, check_vma=False
    )
```

```python
import functools
import jax
import jax.numpy as jnp
from jax import lax
from jax.experimental import pallas as pl
from jax.experimental.pallas import tpu as pltpu
from jax.sharding import PartitionSpec as P

MESH = pl.DeviceIdType.MESH


def forward_kernel(n, groups, depth, inputs_ref, grads_ref, wg_ref, wu_ref, wd_ref, inputs_out,
                   grads_out, joined_out, down_out, send_sem, recv_sem, local_sem, ag_send,
                   ag_recv, own_sem):
    me = lax.axis_index("expert")
    row = lax.axis_index("dp")
    width = wg_ref.shape[1]
    piece = wg_ref.shape[0]
    columns = wd_ref.shape[1]
    barrier = pltpu.get_barrier_semaphore()

    def greet(i, carry):
        peer = lax.rem(me + i, n)
        pl.semaphore_signal(barrier, inc=1, device_id=(row, peer), device_id_type=MESH)
        return carry

    def greet_group(i, carry):
        other = lax.rem(row + i, groups)
        pl.semaphore_signal(barrier, inc=1, device_id=(other, me), device_id_type=MESH)
        return carry

    lax.fori_loop(1, n, greet, 0)
    lax.fori_loop(1, groups, greet_group, 0)
    pl.semaphore_wait(barrier, n - 1 + groups - 1)
    sources = (inputs_ref, grads_ref)
    targets = (inputs_out, grads_out)
    local = [
        pltpu.make_async_copy(
            sources[a].at[me, pl.ds(0, depth)], targets[a].at[me, pl.ds(0, depth)], local_sem.at[a]
        )
        for a in range(2)
    ]
    for copy in local:
        copy.start()

    def remote(a, peer, slot):
        return pltpu.make_async_remote_copy(
            src_ref=sources[a].at[peer, pl.ds(0, depth)],
            dst_ref=targets[a].at[slot, pl.ds(0, depth)],
            send_sem=send_sem.at[a, peer],
            recv_sem=recv_sem.at[a, slot],
            device_id=(row, peer),
            device_id_type=MESH,
        )

    def start(i, carry):
        peer = lax.rem(me + i, n)
        for a in range(2):
            remote(a, peer, me).start()
        return carry

    lax.fori_loop(1, n, start, 0)

    def places(slot):
        rows = pl.ds(pl.multiple_of(slot * piece, piece), piece)
        cols = pl.ds(pl.multiple_of(slot * columns, columns), columns)
        return (
            (wg_ref, joined_out.at[rows, pl.ds(0, width)]),
            (wu_ref, joined_out.at[rows, pl.ds(width, width)]),
            (wd_ref, down_out.at[:, cols]),
        )

    def gather_copy(k, other, slot):
        src, dst = places(slot)[k]
        return pltpu.make_async_remote_copy(
            src_ref=src,
            dst_ref=dst,
            send_sem=ag_send.at[k, other],
            recv_sem=ag_recv.at[k, slot],
            device_id=(other, me),
            device_id_type=MESH,
        )

    own = [
        pltpu.make_async_copy(src, dst, own_sem.at[k])
        for k, (src, dst) in enumerate(places(row))
    ]
    for copy in own:
        copy.start()

    def gather_start(i, carry):
        other = lax.rem(row + i, groups)
        for k in range(3):
            gather_copy(k, other, row).start()
        return carry

    lax.fori_loop(1, groups, gather_start, 0)

    def gather_finish(i, carry):
        other = lax.rem(row + i, groups)
        source = lax.rem(row + groups - i, groups)
        for k in range(3):
            gather_copy(k, other, row).wait_send()
            gather_copy(k, source, source).wait_recv()
        return carry

    lax.fori_loop(1, groups, gather_finish, 0)
    for copy in own:
        copy.wait()

    def finish(i, carry):
        peer = lax.rem(me + i, n)
        source = lax.rem(me + n - i, n)
        for a in range(2):
            remote(a, peer, me).wait_send()
            remote(a, source, source).wait_recv()
        return carry

    lax.fori_loop(1, n, finish, 0)
    for copy in local:
        copy.wait()


def forward_exchange(send_inputs, send_grads, wg, wu, wd, groups, depth, collective_id):
    n = send_inputs.shape[0]
    any_spec = pl.BlockSpec(memory_space=pl.ANY)
    return pl.pallas_call(
        functools.partial(forward_kernel, n, groups, depth),
        out_shape=[
            jax.ShapeDtypeStruct(send_inputs.shape, send_inputs.dtype),
            jax.ShapeDtypeStruct(send_grads.shape, send_grads.dtype),
            jax.ShapeDtypeStruct((groups * wg.shape[0], 2 * wg.shape[1]), wg.dtype),
            jax.ShapeDtypeStruct((wd.shape[0], groups * wd.shape[1]), wd.dtype),
        ],
        in_specs=[any_spec] * 5,
        out_specs=[any_spec] * 4,
        scratch_shapes=[
            pltpu.SemaphoreType.DMA((2, n)),
            pltpu.SemaphoreType.DMA((2, n)),
            pltpu.SemaphoreType.DMA((2,)),
            pltpu.SemaphoreType.DMA((3, groups)),
            pltpu.SemaphoreType.DMA((3, groups)),
            pltpu.SemaphoreType.DMA((3,)),
        ],
        compiler_params=pltpu.CompilerParams(
            collective_id=collective_id, has_side_effects=True
        ),
    )(send_inputs, send_grads, wg, wu, wd)


def return_kernel(n, groups, depth, slot_ref, part_ref, joined_ref, out_ref, down_ref, gate_ref, up_ref,
                  send_sem, recv_sem, local_sem, rs_send, rs_recv, ag_send, ag_recv, js_send,
                  js_recv, own_sem, parts, reduced, joined_parts, joined_sum):
    me = lax.axis_index("expert")
    row = lax.axis_index("dp")
    rows = reduced.shape[0]
    joined_rows = joined_sum.shape[0]
    width = gate_ref.shape[1]
    barrier = pltpu.get_barrier_semaphore()

    def greet(i, carry):
        peer = lax.rem(me + i, n)
        pl.semaphore_signal(barrier, inc=1, device_id=(row, peer), device_id_type=MESH)
        return carry

    def greet_group(i, carry):
        other = lax.rem(row + i, groups)
        pl.semaphore_signal(barrier, inc=1, device_id=(other, me), device_id_type=MESH)
        return carry

    lax.fori_loop(1, n, greet, 0)
    lax.fori_loop(1, groups, greet_group, 0)
    pl.semaphore_wait(barrier, n - 1 + groups - 1)
    local = pltpu.make_async_copy(
        slot_ref.at[me, pl.ds(0, depth)], out_ref.at[me, pl.ds(0, depth)], local_sem
    )
    local.start()

    def remote(peer, slot):
        return pltpu.make_async_remote_copy(
            src_ref=slot_ref.at[peer, pl.ds(0, depth)],
            dst_ref=out_ref.at[slot, pl.ds(0, depth)],
            send_sem=send_sem.at[peer],
            recv_sem=recv_sem.at[slot],
            device_id=(row, peer),
            device_id_type=MESH,
        )

    def start(i, carry):
        remote(lax.rem(me + i, n), me).start()
        return carry

    lax.fori_loop(1, n, start, 0)

    def scatter_copy(other, slot):
        return pltpu.make_async_remote_copy(
            src_ref=part_ref.at[pl.ds(pl.multiple_of(other * rows, rows), rows)],
            dst_ref=parts.at[slot],
            send_sem=rs_send.at[other],
            recv_sem=rs_recv.at[slot],
            device_id=(other, me),
            device_id_type=MESH,
        )

    def joined_copy(other, slot):
        return pltpu.make_async_remote_copy(
            src_ref=joined_ref.at[pl.ds(pl.multiple_of(other * joined_rows, joined_rows), joined_rows)],
            dst_ref=joined_parts.at[slot],
            send_sem=js_send.at[other],
            recv_sem=js_recv.at[slot],
            device_id=(other, me),
            device_id_type=MESH,
        )

    own = pltpu.make_async_copy(
        part_ref.at[pl.ds(pl.multiple_of(row * rows, rows), rows)], parts.at[row], own_sem.at[0]
    )
    own.start()
    own_joined = pltpu.make_async_copy(
        joined_ref.at[pl.ds(pl.multiple_of(row * joined_rows, joined_rows), joined_rows)],
        joined_parts.at[row],
        own_sem.at[2],
    )
    own_joined.start()

    def scatter_start(i, carry):
        other = lax.rem(row + i, groups)
        scatter_copy(other, row).start()
        joined_copy(other, row).start()
        return carry

    lax.fori_loop(1, groups, scatter_start, 0)

    def scatter_finish(i, carry):
        scatter_copy(lax.rem(row + i, groups), row).wait_send()
        source = lax.rem(row + groups - i, groups)
        scatter_copy(source, source).wait_recv()
        return carry

    lax.fori_loop(1, groups, scatter_finish, 0)
    own.wait()
    total = parts[0].astype(jnp.float32)
    for slot in range(1, groups):
        total = total + parts[slot].astype(jnp.float32)
    reduced[...] = total.astype(reduced.dtype)

    def gather_copy(other, slot):
        return pltpu.make_async_remote_copy(
            src_ref=reduced,
            dst_ref=down_ref.at[pl.ds(pl.multiple_of(slot * rows, rows), rows)],
            send_sem=ag_send.at[other],
            recv_sem=ag_recv.at[slot],
            device_id=(other, me),
            device_id_type=MESH,
        )

    keep = pltpu.make_async_copy(
        reduced, down_ref.at[pl.ds(pl.multiple_of(row * rows, rows), rows)], own_sem.at[1]
    )
    keep.start()

    def gather_start(i, carry):
        gather_copy(lax.rem(row + i, groups), row).start()
        return carry

    lax.fori_loop(1, groups, gather_start, 0)

    def joined_finish(i, carry):
        joined_copy(lax.rem(row + i, groups), row).wait_send()
        source = lax.rem(row + groups - i, groups)
        joined_copy(source, source).wait_recv()
        return carry

    lax.fori_loop(1, groups, joined_finish, 0)
    own_joined.wait()
    joined_total = joined_parts[0].astype(jnp.float32)
    for slot in range(1, groups):
        joined_total = joined_total + joined_parts[slot].astype(jnp.float32)
    joined_sum[...] = joined_total.astype(joined_sum.dtype)
    halves = [
        pltpu.make_async_copy(joined_sum.at[:, pl.ds(0, width)], gate_ref, own_sem.at[3]),
        pltpu.make_async_copy(joined_sum.at[:, pl.ds(width, width)], up_ref, own_sem.at[4]),
    ]
    for copy in halves:
        copy.start()

    def gather_finish(i, carry):
        gather_copy(lax.rem(row + i, groups), row).wait_send()
        source = lax.rem(row + groups - i, groups)
        gather_copy(source, source).wait_recv()
        return carry

    lax.fori_loop(1, groups, gather_finish, 0)
    keep.wait()
    for copy in halves:
        copy.wait()

    def finish(i, carry):
        remote(lax.rem(me + i, n), me).wait_send()
        source = lax.rem(me + n - i, n)
        remote(source, source).wait_recv()
        return carry

    lax.fori_loop(1, n, finish, 0)
    local.wait()


def return_and_reduce(slot_grad, down_part, joined_part, groups, depth, collective_id):
    n = slot_grad.shape[0]
    rows = down_part.shape[0] // groups
    joined_rows = joined_part.shape[0] // groups
    width = joined_part.shape[1] // 2
    any_spec = pl.BlockSpec(memory_space=pl.ANY)
    return pl.pallas_call(
        functools.partial(return_kernel, n, groups, depth),
        out_shape=[
            jax.ShapeDtypeStruct(slot_grad.shape, slot_grad.dtype),
            jax.ShapeDtypeStruct(down_part.shape, down_part.dtype),
            jax.ShapeDtypeStruct((joined_rows, width), joined_part.dtype),
            jax.ShapeDtypeStruct((joined_rows, width), joined_part.dtype),
        ],
        in_specs=[any_spec] * 3,
        out_specs=[any_spec] * 4,
        scratch_shapes=[
            pltpu.SemaphoreType.DMA((n,)),
            pltpu.SemaphoreType.DMA((n,)),
            pltpu.SemaphoreType.DMA(()),
            pltpu.SemaphoreType.DMA((groups,)),
            pltpu.SemaphoreType.DMA((groups,)),
            pltpu.SemaphoreType.DMA((groups,)),
            pltpu.SemaphoreType.DMA((groups,)),
            pltpu.SemaphoreType.DMA((groups,)),
            pltpu.SemaphoreType.DMA((groups,)),
            pltpu.SemaphoreType.DMA((5,)),
            pltpu.VMEM((groups, rows, down_part.shape[1]), down_part.dtype),
            pltpu.VMEM((rows, down_part.shape[1]), down_part.dtype),
            pltpu.VMEM((groups, joined_rows, joined_part.shape[1]), joined_part.dtype),
            pltpu.VMEM((joined_rows, joined_part.shape[1]), joined_part.dtype),
        ],
        compiler_params=pltpu.CompilerParams(
            collective_id=collective_id, has_side_effects=True
        ),
    )(slot_grad, down_part, joined_part)


def on_device(tokens, out_grad, expert_ids, gates, w_gate, w_up, w_down):
    expert_count = lax.axis_size("expert")
    groups = lax.axis_size("dp")
    tok_rows = tokens.shape[0]
    model_width = tokens.shape[1]
    per_token = expert_ids.shape[1]
    hidden = w_gate.shape[2]
    entries = tok_rows * per_token
    slot_depth = 3 * entries // expert_count
    block = 8 * pl.cdiv(slot_depth, 8)
    slot_count = expert_count * block
    flat_ids = expert_ids.reshape(entries)
    onehot = (flat_ids[:, None] == jnp.arange(expert_count, dtype=jnp.int32)[None, :]).astype(
        jnp.int32
    )
    before = jnp.cumsum(onehot, axis=0) - onehot
    ranking = jnp.sum(before * onehot, axis=1)
    slot_of_entry = flat_ids * block + ranking
    source = (
        jnp.full((slot_count,), entries, jnp.int32)
        .at[slot_of_entry]
        .set(jnp.arange(entries, dtype=jnp.int32))
    )
    entry_scaled = (
        (gates[:, :, None] * out_grad.astype(jnp.float32)[:, None, :])
        .astype(jnp.bfloat16)
        .reshape(entries, model_width)
    )
    grad_table = jnp.concatenate([entry_scaled, jnp.zeros((1, model_width), jnp.bfloat16)], axis=0)
    input_table = jnp.concatenate([tokens, jnp.zeros((1, model_width), tokens.dtype)], axis=0)
    send_grads = grad_table[source].reshape(expert_count, block, model_width)
    send_inputs = input_table[source // per_token].reshape(expert_count, block, model_width)
    rows_in, grads_in, full_joined, full_down = forward_exchange(
        send_inputs, send_grads, w_gate[0], w_up[0], w_down[0], groups, slot_depth, 0
    )
    filled = (jnp.arange(slot_count, dtype=jnp.int32) % block < slot_depth)[:, None]
    rows_in = jnp.where(filled, rows_in.reshape(slot_count, model_width), 0).astype(tokens.dtype)
    grads_in = jnp.where(filled, grads_in.reshape(slot_count, model_width), 0).astype(
        jnp.bfloat16
    )
    preact = jnp.dot(rows_in, full_joined, preferred_element_type=jnp.float32)
    hidden_grad = lax.dot_general(
        grads_in, full_down, (((1,), (1,)), ((), ())), preferred_element_type=jnp.float32
    )
    gate_pre = preact[:, :hidden]
    up_pre = preact[:, hidden:]
    sigmoid = jax.nn.sigmoid(gate_pre)
    silu_value = gate_pre * sigmoid
    activated = (silu_value * up_pre).astype(jnp.bfloat16)
    gate_side = (hidden_grad * up_pre * sigmoid * (1.0 + gate_pre * (1.0 - sigmoid))).astype(
        jnp.bfloat16
    )
    up_side = (hidden_grad * silu_value).astype(jnp.bfloat16)
    both_sides = jnp.concatenate([gate_side, up_side], axis=1)
    slot_grad = lax.dot_general(
        both_sides, full_joined, (((1,), (1,)), ((), ())), preferred_element_type=jnp.float32
    ).astype(jnp.bfloat16)
    down_part = lax.dot_general(
        activated, grads_in, (((0,), (0,)), ((), ())), preferred_element_type=jnp.float32
    ).astype(jnp.bfloat16)
    joined_part = lax.dot_general(
        rows_in, both_sides, (((0,), (0,)), ((), ())), preferred_element_type=jnp.float32
    ).astype(jnp.bfloat16)
    returned, down_grad, gate_grad, up_grad = return_and_reduce(
        slot_grad.reshape(expert_count, block, model_width),
        down_part,
        joined_part,
        groups,
        slot_depth,
        1,
    )
    picked = returned.reshape(slot_count, model_width)[slot_of_entry]
    picked = picked.astype(jnp.float32).reshape(tok_rows, per_token, model_width)
    input_grad = jnp.sum(picked, axis=1).astype(jnp.bfloat16)
    return (input_grad, gate_grad[None], up_grad[None], down_grad[None])


def solution(mesh):
    in_specs = (
        P(("dp", "expert"), None),
        P(("dp", "expert"), None),
        P(("dp", "expert"), None),
        P(("dp", "expert"), None),
        P("expert", "dp", None),
        P("expert", "dp", None),
        P("expert", None, "dp"),
    )
    out_specs = (
        P(("dp", "expert"), None),
        P("expert", "dp", None),
        P("expert", "dp", None),
        P("expert", None, None),
    )
    return jax.shard_map(
        on_device, mesh=mesh, in_specs=in_specs, out_specs=out_specs, check_vma=False
    )
```

```python
import functools
import jax
import jax.numpy as jnp
from jax import lax
from jax.experimental import pallas as pl
from jax.experimental.pallas import tpu as pltpu
from jax.sharding import PartitionSpec as P

MESH = pl.DeviceIdType.MESH


def forward_kernel(n, groups, depth, inputs_ref, wg_ref, wu_ref, wd_ref, inputs_out, joined_out,
                   down_out, send_sem, recv_sem, local_sem, ag_send, ag_recv, own_sem):
    me = lax.axis_index("expert")
    row = lax.axis_index("dp")
    width = wg_ref.shape[1]
    piece = wg_ref.shape[0]
    columns = wd_ref.shape[1]
    barrier = pltpu.get_barrier_semaphore()

    def greet(i, carry):
        peer = lax.rem(me + i, n)
        pl.semaphore_signal(barrier, inc=1, device_id=(row, peer), device_id_type=MESH)
        return carry

    def greet_group(i, carry):
        other = lax.rem(row + i, groups)
        pl.semaphore_signal(barrier, inc=1, device_id=(other, me), device_id_type=MESH)
        return carry

    lax.fori_loop(1, n, greet, 0)
    lax.fori_loop(1, groups, greet_group, 0)
    pl.semaphore_wait(barrier, n - 1 + groups - 1)
    sources = (inputs_ref,)
    targets = (inputs_out,)
    local = [
        pltpu.make_async_copy(
            sources[a].at[me, pl.ds(0, depth)], targets[a].at[me, pl.ds(0, depth)], local_sem.at[a]
        )
        for a in range(len(sources))
    ]
    for copy in local:
        copy.start()

    def remote(a, peer, slot):
        return pltpu.make_async_remote_copy(
            src_ref=sources[a].at[peer, pl.ds(0, depth)],
            dst_ref=targets[a].at[slot, pl.ds(0, depth)],
            send_sem=send_sem.at[a, peer],
            recv_sem=recv_sem.at[a, slot],
            device_id=(row, peer),
            device_id_type=MESH,
        )

    def start(i, carry):
        peer = lax.rem(me + i, n)
        for a in range(len(sources)):
            remote(a, peer, me).start()
        return carry

    lax.fori_loop(1, n, start, 0)

    def places(slot):
        rows = pl.ds(pl.multiple_of(slot * piece, piece), piece)
        cols = pl.ds(pl.multiple_of(slot * columns, columns), columns)
        return (
            (wg_ref, joined_out.at[rows, pl.ds(0, width)]),
            (wu_ref, joined_out.at[rows, pl.ds(width, width)]),
            (wd_ref, down_out.at[:, cols]),
        )

    def gather_copy(k, other, slot):
        src, dst = places(slot)[k]
        return pltpu.make_async_remote_copy(
            src_ref=src,
            dst_ref=dst,
            send_sem=ag_send.at[k, other],
            recv_sem=ag_recv.at[k, slot],
            device_id=(other, me),
            device_id_type=MESH,
        )

    own = [
        pltpu.make_async_copy(src, dst, own_sem.at[k])
        for k, (src, dst) in enumerate(places(row))
    ]
    for copy in own:
        copy.start()

    def gather_start(i, carry):
        other = lax.rem(row + i, groups)
        for k in range(3):
            gather_copy(k, other, row).start()
        return carry

    lax.fori_loop(1, groups, gather_start, 0)

    def gather_finish(i, carry):
        other = lax.rem(row + i, groups)
        source = lax.rem(row + groups - i, groups)
        for k in range(3):
            gather_copy(k, other, row).wait_send()
            gather_copy(k, source, source).wait_recv()
        return carry

    lax.fori_loop(1, groups, gather_finish, 0)
    for copy in own:
        copy.wait()

    def finish(i, carry):
        peer = lax.rem(me + i, n)
        source = lax.rem(me + n - i, n)
        for a in range(len(sources)):
            remote(a, peer, me).wait_send()
            remote(a, source, source).wait_recv()
        return carry

    lax.fori_loop(1, n, finish, 0)
    for copy in local:
        copy.wait()


def forward_exchange(send_rows, wg, wu, wd, groups, depth, collective_id):
    n = send_rows.shape[0]
    any_spec = pl.BlockSpec(memory_space=pl.ANY)
    return pl.pallas_call(
        functools.partial(forward_kernel, n, groups, depth),
        out_shape=[
            jax.ShapeDtypeStruct(send_rows.shape, send_rows.dtype),
            jax.ShapeDtypeStruct((groups * wg.shape[0], 2 * wg.shape[1]), wg.dtype),
            jax.ShapeDtypeStruct((wd.shape[0], groups * wd.shape[1]), wd.dtype),
        ],
        in_specs=[any_spec] * 4,
        out_specs=[any_spec] * 3,
        scratch_shapes=[
            pltpu.SemaphoreType.DMA((1, n)),
            pltpu.SemaphoreType.DMA((1, n)),
            pltpu.SemaphoreType.DMA((1,)),
            pltpu.SemaphoreType.DMA((3, groups)),
            pltpu.SemaphoreType.DMA((3, groups)),
            pltpu.SemaphoreType.DMA((3,)),
        ],
        compiler_params=pltpu.CompilerParams(
            collective_id=collective_id, has_side_effects=True
        ),
    )(send_rows, wg, wu, wd)


def return_kernel(n, groups, depth, slot_ref, part_ref, joined_ref, out_ref, down_ref, gate_ref, up_ref,
                  send_sem, recv_sem, local_sem, rs_send, rs_recv, ag_send, ag_recv, js_send,
                  js_recv, own_sem, parts, reduced, joined_parts, joined_sum):
    me = lax.axis_index("expert")
    row = lax.axis_index("dp")
    rows = reduced.shape[0]
    joined_rows = joined_sum.shape[0]
    width = gate_ref.shape[1]
    barrier = pltpu.get_barrier_semaphore()

    def greet(i, carry):
        peer = lax.rem(me + i, n)
        pl.semaphore_signal(barrier, inc=1, device_id=(row, peer), device_id_type=MESH)
        return carry

    def greet_group(i, carry):
        other = lax.rem(row + i, groups)
        pl.semaphore_signal(barrier, inc=1, device_id=(other, me), device_id_type=MESH)
        return carry

    lax.fori_loop(1, n, greet, 0)
    lax.fori_loop(1, groups, greet_group, 0)
    pl.semaphore_wait(barrier, n - 1 + groups - 1)
    local = pltpu.make_async_copy(
        slot_ref.at[me, pl.ds(0, depth)], out_ref.at[me, pl.ds(0, depth)], local_sem
    )
    local.start()

    def remote(peer, slot):
        return pltpu.make_async_remote_copy(
            src_ref=slot_ref.at[peer, pl.ds(0, depth)],
            dst_ref=out_ref.at[slot, pl.ds(0, depth)],
            send_sem=send_sem.at[peer],
            recv_sem=recv_sem.at[slot],
            device_id=(row, peer),
            device_id_type=MESH,
        )

    def start(i, carry):
        remote(lax.rem(me + i, n), me).start()
        return carry

    lax.fori_loop(1, n, start, 0)

    def scatter_copy(other, slot):
        return pltpu.make_async_remote_copy(
            src_ref=part_ref.at[pl.ds(pl.multiple_of(other * rows, rows), rows)],
            dst_ref=parts.at[slot],
            send_sem=rs_send.at[other],
            recv_sem=rs_recv.at[slot],
            device_id=(other, me),
            device_id_type=MESH,
        )

    def joined_copy(other, slot):
        return pltpu.make_async_remote_copy(
            src_ref=joined_ref.at[pl.ds(pl.multiple_of(other * joined_rows, joined_rows), joined_rows)],
            dst_ref=joined_parts.at[slot],
            send_sem=js_send.at[other],
            recv_sem=js_recv.at[slot],
            device_id=(other, me),
            device_id_type=MESH,
        )

    own = pltpu.make_async_copy(
        part_ref.at[pl.ds(pl.multiple_of(row * rows, rows), rows)], parts.at[row], own_sem.at[0]
    )
    own.start()
    own_joined = pltpu.make_async_copy(
        joined_ref.at[pl.ds(pl.multiple_of(row * joined_rows, joined_rows), joined_rows)],
        joined_parts.at[row],
        own_sem.at[2],
    )
    own_joined.start()

    def scatter_start(i, carry):
        other = lax.rem(row + i, groups)
        scatter_copy(other, row).start()
        joined_copy(other, row).start()
        return carry

    lax.fori_loop(1, groups, scatter_start, 0)

    def scatter_finish(i, carry):
        scatter_copy(lax.rem(row + i, groups), row).wait_send()
        source = lax.rem(row + groups - i, groups)
        scatter_copy(source, source).wait_recv()
        return carry

    lax.fori_loop(1, groups, scatter_finish, 0)
    own.wait()
    total = parts[0].astype(jnp.float32)
    for slot in range(1, groups):
        total = total + parts[slot].astype(jnp.float32)
    reduced[...] = total.astype(reduced.dtype)

    def gather_copy(other, slot):
        return pltpu.make_async_remote_copy(
            src_ref=reduced,
            dst_ref=down_ref.at[pl.ds(pl.multiple_of(slot * rows, rows), rows)],
            send_sem=ag_send.at[other],
            recv_sem=ag_recv.at[slot],
            device_id=(other, me),
            device_id_type=MESH,
        )

    keep = pltpu.make_async_copy(
        reduced, down_ref.at[pl.ds(pl.multiple_of(row * rows, rows), rows)], own_sem.at[1]
    )
    keep.start()

    def gather_start(i, carry):
        gather_copy(lax.rem(row + i, groups), row).start()
        return carry

    lax.fori_loop(1, groups, gather_start, 0)

    def joined_finish(i, carry):
        joined_copy(lax.rem(row + i, groups), row).wait_send()
        source = lax.rem(row + groups - i, groups)
        joined_copy(source, source).wait_recv()
        return carry

    lax.fori_loop(1, groups, joined_finish, 0)
    own_joined.wait()
    joined_total = joined_parts[0].astype(jnp.float32)
    for slot in range(1, groups):
        joined_total = joined_total + joined_parts[slot].astype(jnp.float32)
    joined_sum[...] = joined_total.astype(joined_sum.dtype)
    halves = [
        pltpu.make_async_copy(joined_sum.at[:, pl.ds(0, width)], gate_ref, own_sem.at[3]),
        pltpu.make_async_copy(joined_sum.at[:, pl.ds(width, width)], up_ref, own_sem.at[4]),
    ]
    for copy in halves:
        copy.start()

    def gather_finish(i, carry):
        gather_copy(lax.rem(row + i, groups), row).wait_send()
        source = lax.rem(row + groups - i, groups)
        gather_copy(source, source).wait_recv()
        return carry

    lax.fori_loop(1, groups, gather_finish, 0)
    keep.wait()
    for copy in halves:
        copy.wait()

    def finish(i, carry):
        remote(lax.rem(me + i, n), me).wait_send()
        source = lax.rem(me + n - i, n)
        remote(source, source).wait_recv()
        return carry

    lax.fori_loop(1, n, finish, 0)
    local.wait()


def return_and_reduce(slot_grad, down_part, joined_part, groups, depth, collective_id):
    n = slot_grad.shape[0]
    rows = down_part.shape[0] // groups
    joined_rows = joined_part.shape[0] // groups
    width = joined_part.shape[1] // 2
    any_spec = pl.BlockSpec(memory_space=pl.ANY)
    return pl.pallas_call(
        functools.partial(return_kernel, n, groups, depth),
        out_shape=[
            jax.ShapeDtypeStruct(slot_grad.shape, slot_grad.dtype),
            jax.ShapeDtypeStruct(down_part.shape, down_part.dtype),
            jax.ShapeDtypeStruct((joined_rows, width), joined_part.dtype),
            jax.ShapeDtypeStruct((joined_rows, width), joined_part.dtype),
        ],
        in_specs=[any_spec] * 3,
        out_specs=[any_spec] * 4,
        scratch_shapes=[
            pltpu.SemaphoreType.DMA((n,)),
            pltpu.SemaphoreType.DMA((n,)),
            pltpu.SemaphoreType.DMA(()),
            pltpu.SemaphoreType.DMA((groups,)),
            pltpu.SemaphoreType.DMA((groups,)),
            pltpu.SemaphoreType.DMA((groups,)),
            pltpu.SemaphoreType.DMA((groups,)),
            pltpu.SemaphoreType.DMA((groups,)),
            pltpu.SemaphoreType.DMA((groups,)),
            pltpu.SemaphoreType.DMA((5,)),
            pltpu.VMEM((groups, rows, down_part.shape[1]), down_part.dtype),
            pltpu.VMEM((rows, down_part.shape[1]), down_part.dtype),
            pltpu.VMEM((groups, joined_rows, joined_part.shape[1]), joined_part.dtype),
            pltpu.VMEM((joined_rows, joined_part.shape[1]), joined_part.dtype),
        ],
        compiler_params=pltpu.CompilerParams(
            collective_id=collective_id, has_side_effects=True
        ),
    )(slot_grad, down_part, joined_part)


def on_device(tokens, out_grad, expert_ids, gates, w_gate, w_up, w_down):
    expert_count = lax.axis_size("expert")
    groups = lax.axis_size("dp")
    tok_rows = tokens.shape[0]
    model_width = tokens.shape[1]
    per_token = expert_ids.shape[1]
    hidden = w_gate.shape[2]
    entries = tok_rows * per_token
    slot_depth = 3 * entries // expert_count
    block = 8 * pl.cdiv(slot_depth, 8)
    slot_count = expert_count * block
    flat_ids = expert_ids.reshape(entries)
    onehot = (flat_ids[:, None] == jnp.arange(expert_count, dtype=jnp.int32)[None, :]).astype(
        jnp.int32
    )
    before = jnp.cumsum(onehot, axis=0) - onehot
    ranking = jnp.sum(before * onehot, axis=1)
    slot_of_entry = flat_ids * block + ranking
    source = (
        jnp.full((slot_count,), entries, jnp.int32)
        .at[slot_of_entry]
        .set(jnp.arange(entries, dtype=jnp.int32))
    )
    entry_scaled = (
        (gates[:, :, None] * out_grad.astype(jnp.float32)[:, None, :])
        .astype(jnp.bfloat16)
        .reshape(entries, model_width)
    )
    grad_table = jnp.concatenate([entry_scaled, jnp.zeros((1, model_width), jnp.bfloat16)], axis=0)
    input_table = jnp.concatenate([tokens, jnp.zeros((1, model_width), tokens.dtype)], axis=0)
    send_rows = jnp.concatenate(
        [input_table[source // per_token], grad_table[source]], axis=1
    ).reshape(expert_count, block, 2 * model_width)
    received, full_joined, full_down = forward_exchange(
        send_rows, w_gate[0], w_up[0], w_down[0], groups, slot_depth, 0
    )
    received = received.reshape(slot_count, 2 * model_width)
    rows_in = received[:, :model_width]
    grads_in = received[:, model_width:]
    filled = (jnp.arange(slot_count, dtype=jnp.int32) % block < slot_depth)[:, None]
    rows_in = jnp.where(filled, rows_in, 0).astype(tokens.dtype)
    grads_in = jnp.where(filled, grads_in, 0).astype(jnp.bfloat16)
    preact = jnp.dot(rows_in, full_joined, preferred_element_type=jnp.float32)
    hidden_grad = lax.dot_general(
        grads_in, full_down, (((1,), (1,)), ((), ())), preferred_element_type=jnp.float32
    )
    gate_pre = preact[:, :hidden]
    up_pre = preact[:, hidden:]
    sigmoid = jax.nn.sigmoid(gate_pre)
    silu_value = gate_pre * sigmoid
    activated = (silu_value * up_pre).astype(jnp.bfloat16)
    gate_side = (hidden_grad * up_pre * sigmoid * (1.0 + gate_pre * (1.0 - sigmoid))).astype(
        jnp.bfloat16
    )
    up_side = (hidden_grad * silu_value).astype(jnp.bfloat16)
    both_sides = jnp.concatenate([gate_side, up_side], axis=1)
    slot_grad = lax.dot_general(
        both_sides, full_joined, (((1,), (1,)), ((), ())), preferred_element_type=jnp.float32
    ).astype(jnp.bfloat16)
    down_part = lax.dot_general(
        activated, grads_in, (((0,), (0,)), ((), ())), preferred_element_type=jnp.float32
    ).astype(jnp.bfloat16)
    joined_part = lax.dot_general(
        rows_in, both_sides, (((0,), (0,)), ((), ())), preferred_element_type=jnp.float32
    ).astype(jnp.bfloat16)
    returned, down_grad, gate_grad, up_grad = return_and_reduce(
        slot_grad.reshape(expert_count, block, model_width),
        down_part,
        joined_part,
        groups,
        slot_depth,
        1,
    )
    picked = returned.reshape(slot_count, model_width)[slot_of_entry]
    picked = picked.astype(jnp.float32).reshape(tok_rows, per_token, model_width)
    input_grad = jnp.sum(picked, axis=1).astype(jnp.bfloat16)
    return (input_grad, gate_grad[None], up_grad[None], down_grad[None])


def solution(mesh):
    in_specs = (
        P(("dp", "expert"), None),
        P(("dp", "expert"), None),
        P(("dp", "expert"), None),
        P(("dp", "expert"), None),
        P("expert", "dp", None),
        P("expert", "dp", None),
        P("expert", None, "dp"),
    )
    out_specs = (
        P(("dp", "expert"), None),
        P("expert", "dp", None),
        P("expert", "dp", None),
        P("expert", None, None),
    )
    return jax.shard_map(
        on_device, mesh=mesh, in_specs=in_specs, out_specs=out_specs, check_vma=False
    )
```

```python
import functools
import jax
import jax.numpy as jnp
from jax import lax
from jax.experimental import pallas as pl
from jax.experimental.pallas import tpu as pltpu
from jax.sharding import PartitionSpec as P

MESH = pl.DeviceIdType.MESH


def forward_kernel(n, groups, depth, inputs_ref, wg_ref, wu_ref, wd_ref, inputs_out, joined_out,
                   down_out, send_sem, recv_sem, local_sem, ag_send, ag_recv, own_sem):
    me = lax.axis_index("expert")
    row = lax.axis_index("dp")
    width = wg_ref.shape[1]
    piece = wg_ref.shape[0]
    columns = wd_ref.shape[1]
    barrier = pltpu.get_barrier_semaphore()

    def greet(i, carry):
        peer = lax.rem(me + i, n)
        pl.semaphore_signal(barrier, inc=1, device_id=(row, peer), device_id_type=MESH)
        return carry

    def greet_group(i, carry):
        other = lax.rem(row + i, groups)
        pl.semaphore_signal(barrier, inc=1, device_id=(other, me), device_id_type=MESH)
        return carry

    lax.fori_loop(1, n, greet, 0)
    lax.fori_loop(1, groups, greet_group, 0)
    pl.semaphore_wait(barrier, n - 1 + groups - 1)
    sources = (inputs_ref,)
    targets = (inputs_out,)
    local = [
        pltpu.make_async_copy(
            sources[a].at[me, pl.ds(0, depth)], targets[a].at[me, pl.ds(0, depth)], local_sem.at[a]
        )
        for a in range(len(sources))
    ]
    for copy in local:
        copy.start()

    def remote(a, peer, slot):
        return pltpu.make_async_remote_copy(
            src_ref=sources[a].at[peer, pl.ds(0, depth)],
            dst_ref=targets[a].at[slot, pl.ds(0, depth)],
            send_sem=send_sem.at[a, peer],
            recv_sem=recv_sem.at[a, slot],
            device_id=(row, peer),
            device_id_type=MESH,
        )

    def start(i, carry):
        peer = lax.rem(me + i, n)
        for a in range(len(sources)):
            remote(a, peer, me).start()
        return carry

    lax.fori_loop(1, n, start, 0)

    def places(slot):
        rows = pl.ds(pl.multiple_of(slot * piece, piece), piece)
        cols = pl.ds(pl.multiple_of(slot * columns, columns), columns)
        return (
            (wg_ref, joined_out.at[rows, pl.ds(0, width)]),
            (wu_ref, joined_out.at[rows, pl.ds(width, width)]),
            (wd_ref, down_out.at[:, cols]),
        )

    def gather_copy(k, other, slot):
        src, dst = places(slot)[k]
        return pltpu.make_async_remote_copy(
            src_ref=src,
            dst_ref=dst,
            send_sem=ag_send.at[k, other],
            recv_sem=ag_recv.at[k, slot],
            device_id=(other, me),
            device_id_type=MESH,
        )

    own = [
        pltpu.make_async_copy(src, dst, own_sem.at[k])
        for k, (src, dst) in enumerate(places(row))
    ]
    for copy in own:
        copy.start()

    def gather_start(i, carry):
        other = lax.rem(row + i, groups)
        for k in range(3):
            gather_copy(k, other, row).start()
        return carry

    lax.fori_loop(1, groups, gather_start, 0)

    def gather_finish(i, carry):
        other = lax.rem(row + i, groups)
        source = lax.rem(row + groups - i, groups)
        for k in range(3):
            gather_copy(k, other, row).wait_send()
            gather_copy(k, source, source).wait_recv()
        return carry

    lax.fori_loop(1, groups, gather_finish, 0)
    for copy in own:
        copy.wait()

    def finish(i, carry):
        peer = lax.rem(me + i, n)
        source = lax.rem(me + n - i, n)
        for a in range(len(sources)):
            remote(a, peer, me).wait_send()
            remote(a, source, source).wait_recv()
        return carry

    lax.fori_loop(1, n, finish, 0)
    for copy in local:
        copy.wait()


def forward_exchange(send_rows, wg, wu, wd, groups, depth, collective_id):
    n = send_rows.shape[0]
    any_spec = pl.BlockSpec(memory_space=pl.ANY)
    return pl.pallas_call(
        functools.partial(forward_kernel, n, groups, depth),
        out_shape=[
            jax.ShapeDtypeStruct(send_rows.shape, send_rows.dtype),
            jax.ShapeDtypeStruct((groups * wg.shape[0], 2 * wg.shape[1]), wg.dtype),
            jax.ShapeDtypeStruct((wd.shape[0], groups * wd.shape[1]), wd.dtype),
        ],
        in_specs=[any_spec] * 4,
        out_specs=[any_spec] * 3,
        scratch_shapes=[
            pltpu.SemaphoreType.DMA((1, n)),
            pltpu.SemaphoreType.DMA((1, n)),
            pltpu.SemaphoreType.DMA((1,)),
            pltpu.SemaphoreType.DMA((3, groups)),
            pltpu.SemaphoreType.DMA((3, groups)),
            pltpu.SemaphoreType.DMA((3,)),
        ],
        compiler_params=pltpu.CompilerParams(
            collective_id=collective_id, has_side_effects=True
        ),
    )(send_rows, wg, wu, wd)


def return_kernel(n, groups, depth, slot_ref, act_ref, grads_ref, rows_ref, sides_ref, out_ref,
                  down_ref, gate_ref, up_ref, send_sem, recv_sem, local_sem, rs_send, rs_recv,
                  ag_send, ag_recv, js_send, js_recv, own_sem, parts, reduced, joined_parts,
                  joined_sum, part_ref, joined_ref):
    me = lax.axis_index("expert")
    row = lax.axis_index("dp")
    rows = reduced.shape[0]
    joined_rows = joined_sum.shape[0]
    width = gate_ref.shape[1]
    barrier = pltpu.get_barrier_semaphore()

    def greet(i, carry):
        peer = lax.rem(me + i, n)
        pl.semaphore_signal(barrier, inc=1, device_id=(row, peer), device_id_type=MESH)
        return carry

    def greet_group(i, carry):
        other = lax.rem(row + i, groups)
        pl.semaphore_signal(barrier, inc=1, device_id=(other, me), device_id_type=MESH)
        return carry

    lax.fori_loop(1, n, greet, 0)
    lax.fori_loop(1, groups, greet_group, 0)
    pl.semaphore_wait(barrier, n - 1 + groups - 1)
    local = pltpu.make_async_copy(
        slot_ref.at[me, pl.ds(0, depth)], out_ref.at[me, pl.ds(0, depth)], local_sem
    )
    local.start()

    def remote(peer, slot):
        return pltpu.make_async_remote_copy(
            src_ref=slot_ref.at[peer, pl.ds(0, depth)],
            dst_ref=out_ref.at[slot, pl.ds(0, depth)],
            send_sem=send_sem.at[peer],
            recv_sem=recv_sem.at[slot],
            device_id=(row, peer),
            device_id_type=MESH,
        )

    def start(i, carry):
        remote(lax.rem(me + i, n), me).start()
        return carry

    lax.fori_loop(1, n, start, 0)
    part_ref[...] = lax.dot_general(
        act_ref[...], grads_ref[...], (((0,), (0,)), ((), ())), preferred_element_type=jnp.float32
    ).astype(part_ref.dtype)
    joined_ref[...] = lax.dot_general(
        rows_ref[...], sides_ref[...], (((0,), (0,)), ((), ())), preferred_element_type=jnp.float32
    ).astype(joined_ref.dtype)

    def scatter_copy(other, slot):
        return pltpu.make_async_remote_copy(
            src_ref=part_ref.at[pl.ds(pl.multiple_of(other * rows, rows), rows)],
            dst_ref=parts.at[slot],
            send_sem=rs_send.at[other],
            recv_sem=rs_recv.at[slot],
            device_id=(other, me),
            device_id_type=MESH,
        )

    def joined_copy(other, slot):
        return pltpu.make_async_remote_copy(
            src_ref=joined_ref.at[pl.ds(pl.multiple_of(other * joined_rows, joined_rows), joined_rows)],
            dst_ref=joined_parts.at[slot],
            send_sem=js_send.at[other],
            recv_sem=js_recv.at[slot],
            device_id=(other, me),
            device_id_type=MESH,
        )

    own = pltpu.make_async_copy(
        part_ref.at[pl.ds(pl.multiple_of(row * rows, rows), rows)], parts.at[row], own_sem.at[0]
    )
    own.start()
    own_joined = pltpu.make_async_copy(
        joined_ref.at[pl.ds(pl.multiple_of(row * joined_rows, joined_rows), joined_rows)],
        joined_parts.at[row],
        own_sem.at[2],
    )
    own_joined.start()

    def scatter_start(i, carry):
        other = lax.rem(row + i, groups)
        scatter_copy(other, row).start()
        joined_copy(other, row).start()
        return carry

    lax.fori_loop(1, groups, scatter_start, 0)

    def scatter_finish(i, carry):
        scatter_copy(lax.rem(row + i, groups), row).wait_send()
        source = lax.rem(row + groups - i, groups)
        scatter_copy(source, source).wait_recv()
        return carry

    lax.fori_loop(1, groups, scatter_finish, 0)
    own.wait()
    total = parts[0].astype(jnp.float32)
    for slot in range(1, groups):
        total = total + parts[slot].astype(jnp.float32)
    reduced[...] = total.astype(reduced.dtype)

    def gather_copy(other, slot):
        return pltpu.make_async_remote_copy(
            src_ref=reduced,
            dst_ref=down_ref.at[pl.ds(pl.multiple_of(slot * rows, rows), rows)],
            send_sem=ag_send.at[other],
            recv_sem=ag_recv.at[slot],
            device_id=(other, me),
            device_id_type=MESH,
        )

    keep = pltpu.make_async_copy(
        reduced, down_ref.at[pl.ds(pl.multiple_of(row * rows, rows), rows)], own_sem.at[1]
    )
    keep.start()

    def gather_start(i, carry):
        gather_copy(lax.rem(row + i, groups), row).start()
        return carry

    lax.fori_loop(1, groups, gather_start, 0)

    def joined_finish(i, carry):
        joined_copy(lax.rem(row + i, groups), row).wait_send()
        source = lax.rem(row + groups - i, groups)
        joined_copy(source, source).wait_recv()
        return carry

    lax.fori_loop(1, groups, joined_finish, 0)
    own_joined.wait()
    joined_total = joined_parts[0].astype(jnp.float32)
    for slot in range(1, groups):
        joined_total = joined_total + joined_parts[slot].astype(jnp.float32)
    joined_sum[...] = joined_total.astype(joined_sum.dtype)
    halves = [
        pltpu.make_async_copy(joined_sum.at[:, pl.ds(0, width)], gate_ref, own_sem.at[3]),
        pltpu.make_async_copy(joined_sum.at[:, pl.ds(width, width)], up_ref, own_sem.at[4]),
    ]
    for copy in halves:
        copy.start()

    def gather_finish(i, carry):
        gather_copy(lax.rem(row + i, groups), row).wait_send()
        source = lax.rem(row + groups - i, groups)
        gather_copy(source, source).wait_recv()
        return carry

    lax.fori_loop(1, groups, gather_finish, 0)
    keep.wait()
    for copy in halves:
        copy.wait()

    def finish(i, carry):
        remote(lax.rem(me + i, n), me).wait_send()
        source = lax.rem(me + n - i, n)
        remote(source, source).wait_recv()
        return carry

    lax.fori_loop(1, n, finish, 0)
    local.wait()


def return_and_reduce(slot_grad, activated, grads_in, rows_in, both_sides, groups, depth,
                      collective_id):
    n = slot_grad.shape[0]
    hidden = activated.shape[1]
    width = grads_in.shape[1]
    joined_width = both_sides.shape[1]
    rows = hidden // groups
    joined_rows = width // groups
    any_spec = pl.BlockSpec(memory_space=pl.ANY)
    vmem_spec = pl.BlockSpec(memory_space=pltpu.VMEM)
    return pl.pallas_call(
        functools.partial(return_kernel, n, groups, depth),
        out_shape=[
            jax.ShapeDtypeStruct(slot_grad.shape, slot_grad.dtype),
            jax.ShapeDtypeStruct((hidden, width), grads_in.dtype),
            jax.ShapeDtypeStruct((joined_rows, joined_width // 2), rows_in.dtype),
            jax.ShapeDtypeStruct((joined_rows, joined_width // 2), rows_in.dtype),
        ],
        in_specs=[any_spec] + [vmem_spec] * 4,
        out_specs=[any_spec] * 4,
        scratch_shapes=[
            pltpu.SemaphoreType.DMA((n,)),
            pltpu.SemaphoreType.DMA((n,)),
            pltpu.SemaphoreType.DMA(()),
            pltpu.SemaphoreType.DMA((groups,)),
            pltpu.SemaphoreType.DMA((groups,)),
            pltpu.SemaphoreType.DMA((groups,)),
            pltpu.SemaphoreType.DMA((groups,)),
            pltpu.SemaphoreType.DMA((groups,)),
            pltpu.SemaphoreType.DMA((groups,)),
            pltpu.SemaphoreType.DMA((5,)),
            pltpu.VMEM((groups, rows, width), grads_in.dtype),
            pltpu.VMEM((rows, width), grads_in.dtype),
            pltpu.VMEM((groups, joined_rows, joined_width), rows_in.dtype),
            pltpu.VMEM((joined_rows, joined_width), rows_in.dtype),
            pltpu.VMEM((hidden, width), grads_in.dtype),
            pltpu.VMEM((width, joined_width), rows_in.dtype),
        ],
        compiler_params=pltpu.CompilerParams(
            collective_id=collective_id, has_side_effects=True, vmem_limit_bytes=60 * 1024 * 1024
        ),
    )(slot_grad, activated, grads_in, rows_in, both_sides)


def on_device(tokens, out_grad, expert_ids, gates, w_gate, w_up, w_down):
    expert_count = lax.axis_size("expert")
    groups = lax.axis_size("dp")
    tok_rows = tokens.shape[0]
    model_width = tokens.shape[1]
    per_token = expert_ids.shape[1]
    hidden = w_gate.shape[2]
    entries = tok_rows * per_token
    slot_depth = 3 * entries // expert_count
    block = 8 * pl.cdiv(slot_depth, 8)
    slot_count = expert_count * block
    flat_ids = expert_ids.reshape(entries)
    onehot = (flat_ids[:, None] == jnp.arange(expert_count, dtype=jnp.int32)[None, :]).astype(
        jnp.int32
    )
    before = jnp.cumsum(onehot, axis=0) - onehot
    ranking = jnp.sum(before * onehot, axis=1)
    slot_of_entry = flat_ids * block + ranking
    source = (
        jnp.full((slot_count,), entries, jnp.int32)
        .at[slot_of_entry]
        .set(jnp.arange(entries, dtype=jnp.int32))
    )
    entry_scaled = (
        (gates[:, :, None] * out_grad.astype(jnp.float32)[:, None, :])
        .astype(jnp.bfloat16)
        .reshape(entries, model_width)
    )
    grad_table = jnp.concatenate([entry_scaled, jnp.zeros((1, model_width), jnp.bfloat16)], axis=0)
    input_table = jnp.concatenate([tokens, jnp.zeros((1, model_width), tokens.dtype)], axis=0)
    send_rows = jnp.concatenate(
        [input_table[source // per_token], grad_table[source]], axis=1
    ).reshape(expert_count, block, 2 * model_width)
    received, full_joined, full_down = forward_exchange(
        send_rows, w_gate[0], w_up[0], w_down[0], groups, slot_depth, 0
    )
    received = received.reshape(slot_count, 2 * model_width)
    rows_in = received[:, :model_width]
    grads_in = received[:, model_width:]
    filled = (jnp.arange(slot_count, dtype=jnp.int32) % block < slot_depth)[:, None]
    rows_in = jnp.where(filled, rows_in, 0).astype(tokens.dtype)
    grads_in = jnp.where(filled, grads_in, 0).astype(jnp.bfloat16)
    preact = jnp.dot(rows_in, full_joined, preferred_element_type=jnp.float32)
    hidden_grad = lax.dot_general(
        grads_in, full_down, (((1,), (1,)), ((), ())), preferred_element_type=jnp.float32
    )
    gate_pre = preact[:, :hidden]
    up_pre = preact[:, hidden:]
    sigmoid = jax.nn.sigmoid(gate_pre)
    silu_value = gate_pre * sigmoid
    activated = (silu_value * up_pre).astype(jnp.bfloat16)
    gate_side = (hidden_grad * up_pre * sigmoid * (1.0 + gate_pre * (1.0 - sigmoid))).astype(
        jnp.bfloat16
    )
    up_side = (hidden_grad * silu_value).astype(jnp.bfloat16)
    both_sides = jnp.concatenate([gate_side, up_side], axis=1)
    slot_grad = lax.dot_general(
        both_sides, full_joined, (((1,), (1,)), ((), ())), preferred_element_type=jnp.float32
    ).astype(jnp.bfloat16)
    returned, down_grad, gate_grad, up_grad = return_and_reduce(
        slot_grad.reshape(expert_count, block, model_width),
        activated,
        grads_in,
        rows_in,
        both_sides,
        groups,
        slot_depth,
        1,
    )
    picked = returned.reshape(slot_count, model_width)[slot_of_entry]
    picked = picked.astype(jnp.float32).reshape(tok_rows, per_token, model_width)
    input_grad = jnp.sum(picked, axis=1).astype(jnp.bfloat16)
    return (input_grad, gate_grad[None], up_grad[None], down_grad[None])


def solution(mesh):
    in_specs = (
        P(("dp", "expert"), None),
        P(("dp", "expert"), None),
        P(("dp", "expert"), None),
        P(("dp", "expert"), None),
        P("expert", "dp", None),
        P("expert", "dp", None),
        P("expert", None, "dp"),
    )
    out_specs = (
        P(("dp", "expert"), None),
        P("expert", "dp", None),
        P("expert", "dp", None),
        P("expert", None, None),
    )
    return jax.shard_map(
        on_device, mesh=mesh, in_specs=in_specs, out_specs=out_specs, check_vma=False
    )
```

```python
import functools
import jax
import jax.numpy as jnp
from jax import lax
from jax.experimental import pallas as pl
from jax.experimental.pallas import tpu as pltpu
from jax.sharding import PartitionSpec as P

MESH = pl.DeviceIdType.MESH


def forward_kernel(n, groups, depth, inputs_ref, grads_ref, wg_ref, wu_ref, wd_ref, inputs_out,
                   grads_out, joined_out, down_out, send_sem, recv_sem, local_sem, ag_send,
                   ag_recv, own_sem):
    me = lax.axis_index("expert")
    row = lax.axis_index("dp")
    width = wg_ref.shape[1]
    piece = wg_ref.shape[0]
    columns = wd_ref.shape[1]
    barrier = pltpu.get_barrier_semaphore()

    def greet(i, carry):
        peer = lax.rem(me + i, n)
        pl.semaphore_signal(barrier, inc=1, device_id=(row, peer), device_id_type=MESH)
        return carry

    def greet_group(i, carry):
        other = lax.rem(row + i, groups)
        pl.semaphore_signal(barrier, inc=1, device_id=(other, me), device_id_type=MESH)
        return carry

    lax.fori_loop(1, n, greet, 0)
    lax.fori_loop(1, groups, greet_group, 0)
    pl.semaphore_wait(barrier, n - 1 + groups - 1)
    sources = (inputs_ref, grads_ref)
    targets = (inputs_out, grads_out)
    local = [
        pltpu.make_async_copy(
            sources[a].at[me, pl.ds(0, depth)], targets[a].at[me, pl.ds(0, depth)], local_sem.at[a]
        )
        for a in range(2)
    ]
    for copy in local:
        copy.start()

    def remote(a, peer, slot):
        return pltpu.make_async_remote_copy(
            src_ref=sources[a].at[peer, pl.ds(0, depth)],
            dst_ref=targets[a].at[slot, pl.ds(0, depth)],
            send_sem=send_sem.at[a, peer],
            recv_sem=recv_sem.at[a, slot],
            device_id=(row, peer),
            device_id_type=MESH,
        )

    def start(i, carry):
        peer = lax.rem(me + i, n)
        for a in range(2):
            remote(a, peer, me).start()
        return carry

    lax.fori_loop(1, n, start, 0)

    def places(slot):
        rows = pl.ds(pl.multiple_of(slot * piece, piece), piece)
        cols = pl.ds(pl.multiple_of(slot * columns, columns), columns)
        return (
            (wg_ref, joined_out.at[rows, pl.ds(0, width)]),
            (wu_ref, joined_out.at[rows, pl.ds(width, width)]),
            (wd_ref, down_out.at[:, cols]),
        )

    def gather_copy(k, other, slot):
        src, dst = places(slot)[k]
        return pltpu.make_async_remote_copy(
            src_ref=src,
            dst_ref=dst,
            send_sem=ag_send.at[k, other],
            recv_sem=ag_recv.at[k, slot],
            device_id=(other, me),
            device_id_type=MESH,
        )

    own = [
        pltpu.make_async_copy(src, dst, own_sem.at[k])
        for k, (src, dst) in enumerate(places(row))
    ]
    for copy in own:
        copy.start()

    def gather_start(i, carry):
        other = lax.rem(row + i, groups)
        for k in range(3):
            gather_copy(k, other, row).start()
        return carry

    lax.fori_loop(1, groups, gather_start, 0)

    def gather_finish(i, carry):
        other = lax.rem(row + i, groups)
        source = lax.rem(row + groups - i, groups)
        for k in range(3):
            gather_copy(k, other, row).wait_send()
            gather_copy(k, source, source).wait_recv()
        return carry

    lax.fori_loop(1, groups, gather_finish, 0)
    for copy in own:
        copy.wait()

    def finish(i, carry):
        peer = lax.rem(me + i, n)
        source = lax.rem(me + n - i, n)
        for a in range(2):
            remote(a, peer, me).wait_send()
            remote(a, source, source).wait_recv()
        return carry

    lax.fori_loop(1, n, finish, 0)
    for copy in local:
        copy.wait()


def forward_exchange(send_inputs, send_grads, wg, wu, wd, groups, depth, collective_id):
    n = send_inputs.shape[0]
    any_spec = pl.BlockSpec(memory_space=pl.ANY)
    return pl.pallas_call(
        functools.partial(forward_kernel, n, groups, depth),
        out_shape=[
            jax.ShapeDtypeStruct(send_inputs.shape, send_inputs.dtype),
            jax.ShapeDtypeStruct(send_grads.shape, send_grads.dtype),
            jax.ShapeDtypeStruct((groups * wg.shape[0], 2 * wg.shape[1]), wg.dtype),
            jax.ShapeDtypeStruct((wd.shape[0], groups * wd.shape[1]), wd.dtype),
        ],
        in_specs=[any_spec] * 5,
        out_specs=[any_spec] * 4,
        scratch_shapes=[
            pltpu.SemaphoreType.DMA((2, n)),
            pltpu.SemaphoreType.DMA((2, n)),
            pltpu.SemaphoreType.DMA((2,)),
            pltpu.SemaphoreType.DMA((3, groups)),
            pltpu.SemaphoreType.DMA((3, groups)),
            pltpu.SemaphoreType.DMA((3,)),
        ],
        compiler_params=pltpu.CompilerParams(
            collective_id=collective_id, has_side_effects=True
        ),
    )(send_inputs, send_grads, wg, wu, wd)


def return_kernel(n, groups, depth, slot_ref, part_ref, joined_ref, out_ref, down_ref, gate_ref, up_ref,
                  send_sem, recv_sem, local_sem, rs_send, rs_recv, ag_send, ag_recv, js_send,
                  js_recv, own_sem, parts, reduced, joined_parts, joined_sum):
    me = lax.axis_index("expert")
    row = lax.axis_index("dp")
    rows = reduced.shape[0]
    joined_rows = joined_sum.shape[0]
    width = gate_ref.shape[1]
    barrier = pltpu.get_barrier_semaphore()

    def greet(i, carry):
        peer = lax.rem(me + i, n)
        pl.semaphore_signal(barrier, inc=1, device_id=(row, peer), device_id_type=MESH)
        return carry

    def greet_group(i, carry):
        other = lax.rem(row + i, groups)
        pl.semaphore_signal(barrier, inc=1, device_id=(other, me), device_id_type=MESH)
        return carry

    lax.fori_loop(1, n, greet, 0)
    lax.fori_loop(1, groups, greet_group, 0)
    pl.semaphore_wait(barrier, n - 1 + groups - 1)
    local = pltpu.make_async_copy(
        slot_ref.at[me, pl.ds(0, depth)], out_ref.at[me, pl.ds(0, depth)], local_sem
    )
    local.start()

    def remote(peer, slot):
        return pltpu.make_async_remote_copy(
            src_ref=slot_ref.at[peer, pl.ds(0, depth)],
            dst_ref=out_ref.at[slot, pl.ds(0, depth)],
            send_sem=send_sem.at[peer],
            recv_sem=recv_sem.at[slot],
            device_id=(row, peer),
            device_id_type=MESH,
        )

    def start(i, carry):
        remote(lax.rem(me + i, n), me).start()
        return carry

    lax.fori_loop(1, n, start, 0)

    def scatter_copy(other, slot):
        return pltpu.make_async_remote_copy(
            src_ref=part_ref.at[pl.ds(pl.multiple_of(other * rows, rows), rows)],
            dst_ref=parts.at[slot],
            send_sem=rs_send.at[other],
            recv_sem=rs_recv.at[slot],
            device_id=(other, me),
            device_id_type=MESH,
        )

    def joined_copy(other, slot):
        return pltpu.make_async_remote_copy(
            src_ref=joined_ref.at[pl.ds(pl.multiple_of(other * joined_rows, joined_rows), joined_rows)],
            dst_ref=joined_parts.at[slot],
            send_sem=js_send.at[other],
            recv_sem=js_recv.at[slot],
            device_id=(other, me),
            device_id_type=MESH,
        )

    own = pltpu.make_async_copy(
        part_ref.at[pl.ds(pl.multiple_of(row * rows, rows), rows)], parts.at[row], own_sem.at[0]
    )
    own.start()
    own_joined = pltpu.make_async_copy(
        joined_ref.at[pl.ds(pl.multiple_of(row * joined_rows, joined_rows), joined_rows)],
        joined_parts.at[row],
        own_sem.at[2],
    )
    own_joined.start()

    def scatter_start(i, carry):
        other = lax.rem(row + i, groups)
        scatter_copy(other, row).start()
        joined_copy(other, row).start()
        return carry

    lax.fori_loop(1, groups, scatter_start, 0)

    def scatter_finish(i, carry):
        scatter_copy(lax.rem(row + i, groups), row).wait_send()
        source = lax.rem(row + groups - i, groups)
        scatter_copy(source, source).wait_recv()
        return carry

    lax.fori_loop(1, groups, scatter_finish, 0)
    own.wait()
    total = parts[0].astype(jnp.float32)
    for slot in range(1, groups):
        total = total + parts[slot].astype(jnp.float32)
    reduced[...] = total.astype(reduced.dtype)

    def gather_copy(other, slot):
        return pltpu.make_async_remote_copy(
            src_ref=reduced,
            dst_ref=down_ref.at[pl.ds(pl.multiple_of(slot * rows, rows), rows)],
            send_sem=ag_send.at[other],
            recv_sem=ag_recv.at[slot],
            device_id=(other, me),
            device_id_type=MESH,
        )

    keep = pltpu.make_async_copy(
        reduced, down_ref.at[pl.ds(pl.multiple_of(row * rows, rows), rows)], own_sem.at[1]
    )
    keep.start()

    def gather_start(i, carry):
        gather_copy(lax.rem(row + i, groups), row).start()
        return carry

    lax.fori_loop(1, groups, gather_start, 0)

    def joined_finish(i, carry):
        joined_copy(lax.rem(row + i, groups), row).wait_send()
        source = lax.rem(row + groups - i, groups)
        joined_copy(source, source).wait_recv()
        return carry

    lax.fori_loop(1, groups, joined_finish, 0)
    own_joined.wait()
    joined_total = joined_parts[0].astype(jnp.float32)
    for slot in range(1, groups):
        joined_total = joined_total + joined_parts[slot].astype(jnp.float32)
    joined_sum[...] = joined_total.astype(joined_sum.dtype)
    halves = [
        pltpu.make_async_copy(joined_sum.at[:, pl.ds(0, width)], gate_ref, own_sem.at[3]),
        pltpu.make_async_copy(joined_sum.at[:, pl.ds(width, width)], up_ref, own_sem.at[4]),
    ]
    for copy in halves:
        copy.start()

    def gather_finish(i, carry):
        gather_copy(lax.rem(row + i, groups), row).wait_send()
        source = lax.rem(row + groups - i, groups)
        gather_copy(source, source).wait_recv()
        return carry

    lax.fori_loop(1, groups, gather_finish, 0)
    keep.wait()
    for copy in halves:
        copy.wait()

    def finish(i, carry):
        remote(lax.rem(me + i, n), me).wait_send()
        source = lax.rem(me + n - i, n)
        remote(source, source).wait_recv()
        return carry

    lax.fori_loop(1, n, finish, 0)
    local.wait()


def return_and_reduce(slot_grad, down_part, joined_part, groups, depth, collective_id):
    n = slot_grad.shape[0]
    rows = down_part.shape[0] // groups
    joined_rows = joined_part.shape[0] // groups
    width = joined_part.shape[1] // 2
    any_spec = pl.BlockSpec(memory_space=pl.ANY)
    return pl.pallas_call(
        functools.partial(return_kernel, n, groups, depth),
        out_shape=[
            jax.ShapeDtypeStruct(slot_grad.shape, slot_grad.dtype),
            jax.ShapeDtypeStruct(down_part.shape, down_part.dtype),
            jax.ShapeDtypeStruct((joined_rows, width), joined_part.dtype),
            jax.ShapeDtypeStruct((joined_rows, width), joined_part.dtype),
        ],
        in_specs=[any_spec] * 3,
        out_specs=[any_spec] * 4,
        scratch_shapes=[
            pltpu.SemaphoreType.DMA((n,)),
            pltpu.SemaphoreType.DMA((n,)),
            pltpu.SemaphoreType.DMA(()),
            pltpu.SemaphoreType.DMA((groups,)),
            pltpu.SemaphoreType.DMA((groups,)),
            pltpu.SemaphoreType.DMA((groups,)),
            pltpu.SemaphoreType.DMA((groups,)),
            pltpu.SemaphoreType.DMA((groups,)),
            pltpu.SemaphoreType.DMA((groups,)),
            pltpu.SemaphoreType.DMA((5,)),
            pltpu.VMEM((groups, rows, down_part.shape[1]), down_part.dtype),
            pltpu.VMEM((rows, down_part.shape[1]), down_part.dtype),
            pltpu.VMEM((groups, joined_rows, joined_part.shape[1]), joined_part.dtype),
            pltpu.VMEM((joined_rows, joined_part.shape[1]), joined_part.dtype),
        ],
        compiler_params=pltpu.CompilerParams(
            collective_id=collective_id, has_side_effects=True
        ),
    )(slot_grad, down_part, joined_part)


def on_device(tokens, out_grad, expert_ids, gates, w_gate, w_up, w_down):
    expert_count = lax.axis_size("expert")
    groups = lax.axis_size("dp")
    tok_rows = tokens.shape[0]
    model_width = tokens.shape[1]
    per_token = expert_ids.shape[1]
    hidden = w_gate.shape[2]
    entries = tok_rows * per_token
    slot_depth = 3 * entries // expert_count
    block = 8 * pl.cdiv(slot_depth, 8)
    slot_count = expert_count * block
    flat_ids = expert_ids.reshape(entries)
    onehot = (flat_ids[:, None] == jnp.arange(expert_count, dtype=jnp.int32)[None, :]).astype(
        jnp.int32
    )
    before = jnp.cumsum(onehot, axis=0) - onehot
    ranking = jnp.sum(before * onehot, axis=1)
    slot_of_entry = flat_ids * block + ranking
    source = (
        jnp.full((slot_count,), entries, jnp.int32)
        .at[slot_of_entry]
        .set(jnp.arange(entries, dtype=jnp.int32))
    )
    entry_scaled = (
        (gates[:, :, None] * out_grad.astype(jnp.float32)[:, None, :])
        .astype(jnp.bfloat16)
        .reshape(entries, model_width)
    )
    grad_table = jnp.concatenate([entry_scaled, jnp.zeros((1, model_width), jnp.bfloat16)], axis=0)
    input_table = jnp.concatenate([tokens, jnp.zeros((1, model_width), tokens.dtype)], axis=0)
    send_grads = grad_table[source].reshape(expert_count, block, model_width)
    send_inputs = input_table[source // per_token].reshape(expert_count, block, model_width)
    rows_in, grads_in, full_joined, full_down = forward_exchange(
        send_inputs, send_grads, w_gate[0], w_up[0], w_down[0], groups, slot_depth, 0
    )
    filled = (jnp.arange(slot_count, dtype=jnp.int32) % block < slot_depth)[:, None]
    rows_in = jnp.where(filled, rows_in.reshape(slot_count, model_width), 0).astype(tokens.dtype)
    grads_in = jnp.where(filled, grads_in.reshape(slot_count, model_width), 0).astype(
        jnp.bfloat16
    )
    preact = jnp.dot(rows_in, full_joined, preferred_element_type=jnp.float32)
    hidden_grad = lax.dot_general(
        grads_in, full_down, (((1,), (1,)), ((), ())), preferred_element_type=jnp.float32
    )
    gate_pre = preact[:, :hidden]
    up_pre = preact[:, hidden:]
    sigmoid = jax.nn.sigmoid(gate_pre)
    silu_value = gate_pre * sigmoid
    activated = (silu_value * up_pre).astype(jnp.bfloat16)
    gate_side = (hidden_grad * up_pre * sigmoid * (1.0 + gate_pre * (1.0 - sigmoid))).astype(
        jnp.bfloat16
    )
    up_side = (hidden_grad * silu_value).astype(jnp.bfloat16)
    both_sides = jnp.concatenate([gate_side, up_side], axis=1)
    slot_grad = lax.dot_general(
        both_sides, full_joined, (((1,), (1,)), ((), ())), preferred_element_type=jnp.float32
    ).astype(jnp.bfloat16)
    down_part = lax.dot_general(
        activated, grads_in, (((0,), (0,)), ((), ())), preferred_element_type=jnp.float32
    ).astype(jnp.bfloat16)
    joined_part = lax.dot_general(
        rows_in, both_sides, (((0,), (0,)), ((), ())), preferred_element_type=jnp.float32
    ).astype(jnp.bfloat16)
    returned, down_grad, gate_grad, up_grad = return_and_reduce(
        slot_grad.reshape(expert_count, block, model_width),
        down_part,
        joined_part,
        groups,
        slot_depth,
        1,
    )
    owner = (slot_of_entry[:, None] == jnp.arange(slot_count, dtype=jnp.int32)[None, :]).astype(
        jnp.bfloat16
    )
    input_grad = jnp.dot(
        owner.reshape(tok_rows, per_token, slot_count).sum(axis=1),
        jnp.where(filled, returned.reshape(slot_count, model_width), 0).astype(jnp.bfloat16),
        preferred_element_type=jnp.float32,
    ).astype(jnp.bfloat16)
    return (input_grad, gate_grad[None], up_grad[None], down_grad[None])


def solution(mesh):
    in_specs = (
        P(("dp", "expert"), None),
        P(("dp", "expert"), None),
        P(("dp", "expert"), None),
        P(("dp", "expert"), None),
        P("expert", "dp", None),
        P("expert", "dp", None),
        P("expert", None, "dp"),
    )
    out_specs = (
        P(("dp", "expert"), None),
        P("expert", "dp", None),
        P("expert", "dp", None),
        P("expert", None, None),
    )
    return jax.shard_map(
        on_device, mesh=mesh, in_specs=in_specs, out_specs=out_specs, check_vma=False
    )
```

```python
import functools
import jax
import jax.numpy as jnp
from jax import lax
from jax.experimental import pallas as pl
from jax.experimental.pallas import tpu as pltpu
from jax.sharding import PartitionSpec as P

MESH = pl.DeviceIdType.MESH


def forward_kernel(n, groups, depth, inputs_ref, grads_ref, wg_ref, wu_ref, wd_ref, inputs_out,
                   grads_out, joined_out, down_out, send_sem, recv_sem, local_sem, ag_send,
                   ag_recv, own_sem):
    me = lax.axis_index("expert")
    row = lax.axis_index("dp")
    width = wg_ref.shape[1]
    piece = wg_ref.shape[0]
    columns = wd_ref.shape[1]
    barrier = pltpu.get_barrier_semaphore()

    def greet(i, carry):
        peer = lax.rem(me + i, n)
        pl.semaphore_signal(barrier, inc=1, device_id=(row, peer), device_id_type=MESH)
        return carry

    def greet_group(i, carry):
        other = lax.rem(row + i, groups)
        pl.semaphore_signal(barrier, inc=1, device_id=(other, me), device_id_type=MESH)
        return carry

    lax.fori_loop(1, n, greet, 0)
    lax.fori_loop(1, groups, greet_group, 0)
    pl.semaphore_wait(barrier, n - 1 + groups - 1)
    sources = (inputs_ref, grads_ref)
    targets = (inputs_out, grads_out)
    local = [
        pltpu.make_async_copy(
            sources[a].at[me, pl.ds(0, depth)], targets[a].at[me, pl.ds(0, depth)], local_sem.at[a]
        )
        for a in range(2)
    ]
    for copy in local:
        copy.start()

    def remote(a, peer, slot):
        return pltpu.make_async_remote_copy(
            src_ref=sources[a].at[peer, pl.ds(0, depth)],
            dst_ref=targets[a].at[slot, pl.ds(0, depth)],
            send_sem=send_sem.at[a, peer],
            recv_sem=recv_sem.at[a, slot],
            device_id=(row, peer),
            device_id_type=MESH,
        )

    def start(i, carry):
        peer = lax.rem(me + i, n)
        for a in range(2):
            remote(a, peer, me).start()
        return carry

    lax.fori_loop(1, n, start, 0)

    def places(slot):
        rows = pl.ds(pl.multiple_of(slot * piece, piece), piece)
        cols = pl.ds(pl.multiple_of(slot * columns, columns), columns)
        return (
            (wg_ref, joined_out.at[rows, pl.ds(0, width)]),
            (wu_ref, joined_out.at[rows, pl.ds(width, width)]),
            (wd_ref, down_out.at[:, cols]),
        )

    def gather_copy(k, other, slot):
        src, dst = places(slot)[k]
        return pltpu.make_async_remote_copy(
            src_ref=src,
            dst_ref=dst,
            send_sem=ag_send.at[k, other],
            recv_sem=ag_recv.at[k, slot],
            device_id=(other, me),
            device_id_type=MESH,
        )

    own = [
        pltpu.make_async_copy(src, dst, own_sem.at[k])
        for k, (src, dst) in enumerate(places(row))
    ]
    for copy in own:
        copy.start()

    def gather_start(i, carry):
        other = lax.rem(row + i, groups)
        for k in range(3):
            gather_copy(k, other, row).start()
        return carry

    lax.fori_loop(1, groups, gather_start, 0)

    def gather_finish(i, carry):
        other = lax.rem(row + i, groups)
        source = lax.rem(row + groups - i, groups)
        for k in range(3):
            gather_copy(k, other, row).wait_send()
            gather_copy(k, source, source).wait_recv()
        return carry

    lax.fori_loop(1, groups, gather_finish, 0)
    for copy in own:
        copy.wait()

    def finish(i, carry):
        peer = lax.rem(me + i, n)
        source = lax.rem(me + n - i, n)
        for a in range(2):
            remote(a, peer, me).wait_send()
            remote(a, source, source).wait_recv()
        return carry

    lax.fori_loop(1, n, finish, 0)
    for copy in local:
        copy.wait()


def forward_exchange(send_inputs, send_grads, wg, wu, wd, groups, depth, collective_id):
    n = send_inputs.shape[0]
    any_spec = pl.BlockSpec(memory_space=pl.ANY)
    return pl.pallas_call(
        functools.partial(forward_kernel, n, groups, depth),
        out_shape=[
            jax.ShapeDtypeStruct(send_inputs.shape, send_inputs.dtype),
            jax.ShapeDtypeStruct(send_grads.shape, send_grads.dtype),
            jax.ShapeDtypeStruct((groups * wg.shape[0], 2 * wg.shape[1]), wg.dtype),
            jax.ShapeDtypeStruct((wd.shape[0], groups * wd.shape[1]), wd.dtype),
        ],
        in_specs=[any_spec] * 5,
        out_specs=[any_spec] * 4,
        scratch_shapes=[
            pltpu.SemaphoreType.DMA((2, n)),
            pltpu.SemaphoreType.DMA((2, n)),
            pltpu.SemaphoreType.DMA((2,)),
            pltpu.SemaphoreType.DMA((3, groups)),
            pltpu.SemaphoreType.DMA((3, groups)),
            pltpu.SemaphoreType.DMA((3,)),
        ],
        compiler_params=pltpu.CompilerParams(
            collective_id=collective_id, has_side_effects=True
        ),
    )(send_inputs, send_grads, wg, wu, wd)


def return_kernel(n, groups, depth, slot_ref, part_ref, joined_ref, out_ref, down_ref, gate_ref, up_ref,
                  send_sem, recv_sem, local_sem, rs_send, rs_recv, ag_send, ag_recv, js_send,
                  js_recv, own_sem, parts, reduced, joined_parts, joined_sum):
    me = lax.axis_index("expert")
    row = lax.axis_index("dp")
    rows = reduced.shape[0]
    joined_rows = joined_sum.shape[0]
    width = gate_ref.shape[1]
    barrier = pltpu.get_barrier_semaphore()

    def greet(i, carry):
        peer = lax.rem(me + i, n)
        pl.semaphore_signal(barrier, inc=1, device_id=(row, peer), device_id_type=MESH)
        return carry

    def greet_group(i, carry):
        other = lax.rem(row + i, groups)
        pl.semaphore_signal(barrier, inc=1, device_id=(other, me), device_id_type=MESH)
        return carry

    lax.fori_loop(1, n, greet, 0)
    lax.fori_loop(1, groups, greet_group, 0)
    pl.semaphore_wait(barrier, n - 1 + groups - 1)
    local = pltpu.make_async_copy(
        slot_ref.at[me, pl.ds(0, depth)], out_ref.at[me, pl.ds(0, depth)], local_sem
    )
    local.start()

    def remote(peer, slot):
        return pltpu.make_async_remote_copy(
            src_ref=slot_ref.at[peer, pl.ds(0, depth)],
            dst_ref=out_ref.at[slot, pl.ds(0, depth)],
            send_sem=send_sem.at[peer],
            recv_sem=recv_sem.at[slot],
            device_id=(row, peer),
            device_id_type=MESH,
        )

    def start(i, carry):
        remote(lax.rem(me + i, n), me).start()
        return carry

    lax.fori_loop(1, n, start, 0)

    def scatter_copy(other, slot):
        return pltpu.make_async_remote_copy(
            src_ref=part_ref.at[pl.ds(pl.multiple_of(other * rows, rows), rows)],
            dst_ref=parts.at[slot],
            send_sem=rs_send.at[other],
            recv_sem=rs_recv.at[slot],
            device_id=(other, me),
            device_id_type=MESH,
        )

    def joined_copy(other, slot):
        return pltpu.make_async_remote_copy(
            src_ref=joined_ref.at[pl.ds(pl.multiple_of(other * joined_rows, joined_rows), joined_rows)],
            dst_ref=joined_parts.at[slot],
            send_sem=js_send.at[other],
            recv_sem=js_recv.at[slot],
            device_id=(other, me),
            device_id_type=MESH,
        )

    own = pltpu.make_async_copy(
        part_ref.at[pl.ds(pl.multiple_of(row * rows, rows), rows)], parts.at[row], own_sem.at[0]
    )
    own.start()
    own_joined = pltpu.make_async_copy(
        joined_ref.at[pl.ds(pl.multiple_of(row * joined_rows, joined_rows), joined_rows)],
        joined_parts.at[row],
        own_sem.at[2],
    )
    own_joined.start()

    def scatter_start(i, carry):
        other = lax.rem(row + i, groups)
        scatter_copy(other, row).start()
        joined_copy(other, row).start()
        return carry

    lax.fori_loop(1, groups, scatter_start, 0)

    def scatter_finish(i, carry):
        scatter_copy(lax.rem(row + i, groups), row).wait_send()
        source = lax.rem(row + groups - i, groups)
        scatter_copy(source, source).wait_recv()
        return carry

    lax.fori_loop(1, groups, scatter_finish, 0)
    own.wait()
    total = parts[0].astype(jnp.float32)
    for slot in range(1, groups):
        total = total + parts[slot].astype(jnp.float32)
    reduced[...] = total.astype(reduced.dtype)

    def gather_copy(other, slot):
        return pltpu.make_async_remote_copy(
            src_ref=reduced,
            dst_ref=down_ref.at[pl.ds(pl.multiple_of(slot * rows, rows), rows)],
            send_sem=ag_send.at[other],
            recv_sem=ag_recv.at[slot],
            device_id=(other, me),
            device_id_type=MESH,
        )

    keep = pltpu.make_async_copy(
        reduced, down_ref.at[pl.ds(pl.multiple_of(row * rows, rows), rows)], own_sem.at[1]
    )
    keep.start()

    def gather_start(i, carry):
        gather_copy(lax.rem(row + i, groups), row).start()
        return carry

    lax.fori_loop(1, groups, gather_start, 0)

    def joined_finish(i, carry):
        joined_copy(lax.rem(row + i, groups), row).wait_send()
        source = lax.rem(row + groups - i, groups)
        joined_copy(source, source).wait_recv()
        return carry

    lax.fori_loop(1, groups, joined_finish, 0)
    own_joined.wait()
    joined_total = joined_parts[0].astype(jnp.float32)
    for slot in range(1, groups):
        joined_total = joined_total + joined_parts[slot].astype(jnp.float32)
    joined_sum[...] = joined_total.astype(joined_sum.dtype)
    halves = [
        pltpu.make_async_copy(joined_sum.at[:, pl.ds(0, width)], gate_ref, own_sem.at[3]),
        pltpu.make_async_copy(joined_sum.at[:, pl.ds(width, width)], up_ref, own_sem.at[4]),
    ]
    for copy in halves:
        copy.start()

    def gather_finish(i, carry):
        gather_copy(lax.rem(row + i, groups), row).wait_send()
        source = lax.rem(row + groups - i, groups)
        gather_copy(source, source).wait_recv()
        return carry

    lax.fori_loop(1, groups, gather_finish, 0)
    keep.wait()
    for copy in halves:
        copy.wait()

    def finish(i, carry):
        remote(lax.rem(me + i, n), me).wait_send()
        source = lax.rem(me + n - i, n)
        remote(source, source).wait_recv()
        return carry

    lax.fori_loop(1, n, finish, 0)
    local.wait()


def return_and_reduce(slot_grad, down_part, joined_part, groups, depth, collective_id):
    n = slot_grad.shape[0]
    rows = down_part.shape[0] // groups
    joined_rows = joined_part.shape[0] // groups
    width = joined_part.shape[1] // 2
    any_spec = pl.BlockSpec(memory_space=pl.ANY)
    return pl.pallas_call(
        functools.partial(return_kernel, n, groups, depth),
        out_shape=[
            jax.ShapeDtypeStruct(slot_grad.shape, slot_grad.dtype),
            jax.ShapeDtypeStruct(down_part.shape, down_part.dtype),
            jax.ShapeDtypeStruct((joined_rows, width), joined_part.dtype),
            jax.ShapeDtypeStruct((joined_rows, width), joined_part.dtype),
        ],
        in_specs=[any_spec] * 3,
        out_specs=[any_spec] * 4,
        scratch_shapes=[
            pltpu.SemaphoreType.DMA((n,)),
            pltpu.SemaphoreType.DMA((n,)),
            pltpu.SemaphoreType.DMA(()),
            pltpu.SemaphoreType.DMA((groups,)),
            pltpu.SemaphoreType.DMA((groups,)),
            pltpu.SemaphoreType.DMA((groups,)),
            pltpu.SemaphoreType.DMA((groups,)),
            pltpu.SemaphoreType.DMA((groups,)),
            pltpu.SemaphoreType.DMA((groups,)),
            pltpu.SemaphoreType.DMA((5,)),
            pltpu.VMEM((groups, rows, down_part.shape[1]), down_part.dtype),
            pltpu.VMEM((rows, down_part.shape[1]), down_part.dtype),
            pltpu.VMEM((groups, joined_rows, joined_part.shape[1]), joined_part.dtype),
            pltpu.VMEM((joined_rows, joined_part.shape[1]), joined_part.dtype),
        ],
        compiler_params=pltpu.CompilerParams(
            collective_id=collective_id, has_side_effects=True
        ),
    )(slot_grad, down_part, joined_part)


def on_device(tokens, out_grad, expert_ids, gates, w_gate, w_up, w_down):
    expert_count = lax.axis_size("expert")
    groups = lax.axis_size("dp")
    tok_rows = tokens.shape[0]
    model_width = tokens.shape[1]
    per_token = expert_ids.shape[1]
    hidden = w_gate.shape[2]
    entries = tok_rows * per_token
    slot_depth = 3 * entries // expert_count
    block = 8 * pl.cdiv(slot_depth, 8)
    slot_count = expert_count * block
    flat_ids = expert_ids.reshape(entries)
    onehot = (flat_ids[:, None] == jnp.arange(expert_count, dtype=jnp.int32)[None, :]).astype(
        jnp.int32
    )
    before = jnp.cumsum(onehot, axis=0) - onehot
    ranking = jnp.sum(before * onehot, axis=1)
    slot_of_entry = flat_ids * block + ranking
    source = (
        jnp.full((slot_count,), entries, jnp.int32)
        .at[slot_of_entry]
        .set(jnp.arange(entries, dtype=jnp.int32))
    )
    entry_scaled = (
        (gates[:, :, None] * out_grad.astype(jnp.float32)[:, None, :])
        .astype(jnp.bfloat16)
        .reshape(entries, model_width)
    )
    choose = (source[:, None] == jnp.arange(entries, dtype=jnp.int32)[None, :]).astype(jnp.bfloat16)
    choose_token = (
        source[:, None] // per_token == jnp.arange(tok_rows, dtype=jnp.int32)[None, :]
    ).astype(tokens.dtype)
    send_grads = jnp.dot(choose, entry_scaled, preferred_element_type=jnp.float32).astype(
        jnp.bfloat16
    ).reshape(expert_count, block, model_width)
    send_inputs = jnp.dot(choose_token, tokens, preferred_element_type=jnp.float32).astype(
        tokens.dtype
    ).reshape(expert_count, block, model_width)
    rows_in, grads_in, full_joined, full_down = forward_exchange(
        send_inputs, send_grads, w_gate[0], w_up[0], w_down[0], groups, slot_depth, 0
    )
    filled = (jnp.arange(slot_count, dtype=jnp.int32) % block < slot_depth)[:, None]
    rows_in = jnp.where(filled, rows_in.reshape(slot_count, model_width), 0).astype(tokens.dtype)
    grads_in = jnp.where(filled, grads_in.reshape(slot_count, model_width), 0).astype(
        jnp.bfloat16
    )
    preact = jnp.dot(rows_in, full_joined, preferred_element_type=jnp.float32)
    hidden_grad = lax.dot_general(
        grads_in, full_down, (((1,), (1,)), ((), ())), preferred_element_type=jnp.float32
    )
    gate_pre = preact[:, :hidden]
    up_pre = preact[:, hidden:]
    sigmoid = jax.nn.sigmoid(gate_pre)
    silu_value = gate_pre * sigmoid
    activated = (silu_value * up_pre).astype(jnp.bfloat16)
    gate_side = (hidden_grad * up_pre * sigmoid * (1.0 + gate_pre * (1.0 - sigmoid))).astype(
        jnp.bfloat16
    )
    up_side = (hidden_grad * silu_value).astype(jnp.bfloat16)
    both_sides = jnp.concatenate([gate_side, up_side], axis=1)
    slot_grad = lax.dot_general(
        both_sides, full_joined, (((1,), (1,)), ((), ())), preferred_element_type=jnp.float32
    ).astype(jnp.bfloat16)
    down_part = lax.dot_general(
        activated, grads_in, (((0,), (0,)), ((), ())), preferred_element_type=jnp.float32
    ).astype(jnp.bfloat16)
    joined_part = lax.dot_general(
        rows_in, both_sides, (((0,), (0,)), ((), ())), preferred_element_type=jnp.float32
    ).astype(jnp.bfloat16)
    returned, down_grad, gate_grad, up_grad = return_and_reduce(
        slot_grad.reshape(expert_count, block, model_width),
        down_part,
        joined_part,
        groups,
        slot_depth,
        1,
    )
    owner = (slot_of_entry[:, None] == jnp.arange(slot_count, dtype=jnp.int32)[None, :]).astype(
        jnp.bfloat16
    )
    input_grad = jnp.dot(
        owner.reshape(tok_rows, per_token, slot_count).sum(axis=1),
        jnp.where(filled, returned.reshape(slot_count, model_width), 0).astype(jnp.bfloat16),
        preferred_element_type=jnp.float32,
    ).astype(jnp.bfloat16)
    return (input_grad, gate_grad[None], up_grad[None], down_grad[None])


def solution(mesh):
    in_specs = (
        P(("dp", "expert"), None),
        P(("dp", "expert"), None),
        P(("dp", "expert"), None),
        P(("dp", "expert"), None),
        P("expert", "dp", None),
        P("expert", "dp", None),
        P("expert", None, "dp"),
    )
    out_specs = (
        P(("dp", "expert"), None),
        P("expert", "dp", None),
        P("expert", "dp", None),
        P("expert", None, None),
    )
    return jax.shard_map(
        on_device, mesh=mesh, in_specs=in_specs, out_specs=out_specs, check_vma=False
    )
```

```python
import functools
import jax
import jax.numpy as jnp
from jax import lax
from jax.experimental import pallas as pl
from jax.experimental.pallas import tpu as pltpu
from jax.sharding import PartitionSpec as P

MESH = pl.DeviceIdType.MESH


def forward_kernel(n, groups, depth, inputs_ref, grads_ref, wg_ref, wu_ref, wd_ref, inputs_out,
                   grads_out, joined_out, down_out, send_sem, recv_sem, local_sem, ag_send,
                   ag_recv, own_sem):
    me = lax.axis_index("expert")
    row = lax.axis_index("dp")
    width = wg_ref.shape[1]
    piece = wg_ref.shape[0]
    columns = wd_ref.shape[1]
    barrier = pltpu.get_barrier_semaphore()

    def greet(i, carry):
        peer = lax.rem(me + i, n)
        pl.semaphore_signal(barrier, inc=1, device_id=(row, peer), device_id_type=MESH)
        return carry

    def greet_group(i, carry):
        other = lax.rem(row + i, groups)
        pl.semaphore_signal(barrier, inc=1, device_id=(other, me), device_id_type=MESH)
        return carry

    lax.fori_loop(1, n, greet, 0)
    lax.fori_loop(1, groups, greet_group, 0)
    pl.semaphore_wait(barrier, n - 1 + groups - 1)
    sources = (inputs_ref, grads_ref)
    targets = (inputs_out, grads_out)
    local = [
        pltpu.make_async_copy(
            sources[a].at[me, pl.ds(0, depth)], targets[a].at[me, pl.ds(0, depth)], local_sem.at[a]
        )
        for a in range(2)
    ]
    for copy in local:
        copy.start()

    def remote(a, peer, slot):
        return pltpu.make_async_remote_copy(
            src_ref=sources[a].at[peer, pl.ds(0, depth)],
            dst_ref=targets[a].at[slot, pl.ds(0, depth)],
            send_sem=send_sem.at[a, peer],
            recv_sem=recv_sem.at[a, slot],
            device_id=(row, peer),
            device_id_type=MESH,
        )

    def start(i, carry):
        peer = lax.rem(me + i, n)
        for a in range(2):
            remote(a, peer, me).start()
        return carry

    lax.fori_loop(1, n, start, 0)

    def places(slot):
        rows = pl.ds(pl.multiple_of(slot * piece, piece), piece)
        cols = pl.ds(pl.multiple_of(slot * columns, columns), columns)
        return (
            (wg_ref, joined_out.at[rows, pl.ds(0, width)]),
            (wu_ref, joined_out.at[rows, pl.ds(width, width)]),
            (wd_ref, down_out.at[:, cols]),
        )

    def gather_copy(k, other, slot):
        src, dst = places(slot)[k]
        return pltpu.make_async_remote_copy(
            src_ref=src,
            dst_ref=dst,
            send_sem=ag_send.at[k, other],
            recv_sem=ag_recv.at[k, slot],
            device_id=(other, me),
            device_id_type=MESH,
        )

    own = [
        pltpu.make_async_copy(src, dst, own_sem.at[k])
        for k, (src, dst) in enumerate(places(row))
    ]
    for copy in own:
        copy.start()

    def gather_start(i, carry):
        other = lax.rem(row + i, groups)
        for k in range(3):
            gather_copy(k, other, row).start()
        return carry

    lax.fori_loop(1, groups, gather_start, 0)

    def gather_finish(i, carry):
        other = lax.rem(row + i, groups)
        source = lax.rem(row + groups - i, groups)
        for k in range(3):
            gather_copy(k, other, row).wait_send()
            gather_copy(k, source, source).wait_recv()
        return carry

    lax.fori_loop(1, groups, gather_finish, 0)
    for copy in own:
        copy.wait()

    def finish(i, carry):
        peer = lax.rem(me + i, n)
        source = lax.rem(me + n - i, n)
        for a in range(2):
            remote(a, peer, me).wait_send()
            remote(a, source, source).wait_recv()
        return carry

    lax.fori_loop(1, n, finish, 0)
    for copy in local:
        copy.wait()


def forward_exchange(send_inputs, send_grads, wg, wu, wd, groups, depth, collective_id):
    n = send_inputs.shape[0]
    any_spec = pl.BlockSpec(memory_space=pl.ANY)
    return pl.pallas_call(
        functools.partial(forward_kernel, n, groups, depth),
        out_shape=[
            jax.ShapeDtypeStruct(send_inputs.shape, send_inputs.dtype),
            jax.ShapeDtypeStruct(send_grads.shape, send_grads.dtype),
            jax.ShapeDtypeStruct((groups * wg.shape[0], 2 * wg.shape[1]), wg.dtype),
            jax.ShapeDtypeStruct((wd.shape[0], groups * wd.shape[1]), wd.dtype),
        ],
        in_specs=[any_spec] * 5,
        out_specs=[any_spec] * 4,
        scratch_shapes=[
            pltpu.SemaphoreType.DMA((2, n)),
            pltpu.SemaphoreType.DMA((2, n)),
            pltpu.SemaphoreType.DMA((2,)),
            pltpu.SemaphoreType.DMA((3, groups)),
            pltpu.SemaphoreType.DMA((3, groups)),
            pltpu.SemaphoreType.DMA((3,)),
        ],
        compiler_params=pltpu.CompilerParams(
            collective_id=collective_id, has_side_effects=True
        ),
    )(send_inputs, send_grads, wg, wu, wd)


def return_kernel(n, groups, depth, slot_ref, part_ref, joined_ref, out_ref, down_ref, gate_ref, up_ref,
                  send_sem, recv_sem, local_sem, rs_send, rs_recv, ag_send, ag_recv, js_send,
                  js_recv, own_sem, parts, reduced, joined_parts, joined_sum):
    me = lax.axis_index("expert")
    row = lax.axis_index("dp")
    rows = reduced.shape[0]
    joined_rows = joined_sum.shape[0]
    width = gate_ref.shape[1]
    barrier = pltpu.get_barrier_semaphore()

    def greet(i, carry):
        peer = lax.rem(me + i, n)
        pl.semaphore_signal(barrier, inc=1, device_id=(row, peer), device_id_type=MESH)
        return carry

    def greet_group(i, carry):
        other = lax.rem(row + i, groups)
        pl.semaphore_signal(barrier, inc=1, device_id=(other, me), device_id_type=MESH)
        return carry

    lax.fori_loop(1, n, greet, 0)
    lax.fori_loop(1, groups, greet_group, 0)
    pl.semaphore_wait(barrier, n - 1 + groups - 1)
    local = pltpu.make_async_copy(
        slot_ref.at[me, pl.ds(0, depth)], out_ref.at[me, pl.ds(0, depth)], local_sem
    )
    local.start()

    def remote(peer, slot):
        return pltpu.make_async_remote_copy(
            src_ref=slot_ref.at[peer, pl.ds(0, depth)],
            dst_ref=out_ref.at[slot, pl.ds(0, depth)],
            send_sem=send_sem.at[peer],
            recv_sem=recv_sem.at[slot],
            device_id=(row, peer),
            device_id_type=MESH,
        )

    def start(i, carry):
        remote(lax.rem(me + i, n), me).start()
        return carry

    lax.fori_loop(1, n, start, 0)

    def scatter_copy(other, slot):
        return pltpu.make_async_remote_copy(
            src_ref=part_ref.at[pl.ds(pl.multiple_of(other * rows, rows), rows)],
            dst_ref=parts.at[slot],
            send_sem=rs_send.at[other],
            recv_sem=rs_recv.at[slot],
            device_id=(other, me),
            device_id_type=MESH,
        )

    def joined_copy(other, slot):
        return pltpu.make_async_remote_copy(
            src_ref=joined_ref.at[pl.ds(pl.multiple_of(other * joined_rows, joined_rows), joined_rows)],
            dst_ref=joined_parts.at[slot],
            send_sem=js_send.at[other],
            recv_sem=js_recv.at[slot],
            device_id=(other, me),
            device_id_type=MESH,
        )

    own = pltpu.make_async_copy(
        part_ref.at[pl.ds(pl.multiple_of(row * rows, rows), rows)], parts.at[row], own_sem.at[0]
    )
    own.start()
    own_joined = pltpu.make_async_copy(
        joined_ref.at[pl.ds(pl.multiple_of(row * joined_rows, joined_rows), joined_rows)],
        joined_parts.at[row],
        own_sem.at[2],
    )
    own_joined.start()

    def scatter_start(i, carry):
        other = lax.rem(row + i, groups)
        scatter_copy(other, row).start()
        joined_copy(other, row).start()
        return carry

    lax.fori_loop(1, groups, scatter_start, 0)

    def scatter_finish(i, carry):
        scatter_copy(lax.rem(row + i, groups), row).wait_send()
        source = lax.rem(row + groups - i, groups)
        scatter_copy(source, source).wait_recv()
        return carry

    lax.fori_loop(1, groups, scatter_finish, 0)
    own.wait()
    total = parts[0].astype(jnp.float32)
    for slot in range(1, groups):
        total = total + parts[slot].astype(jnp.float32)
    reduced[...] = total.astype(reduced.dtype)

    def gather_copy(other, slot):
        return pltpu.make_async_remote_copy(
            src_ref=reduced,
            dst_ref=down_ref.at[pl.ds(pl.multiple_of(slot * rows, rows), rows)],
            send_sem=ag_send.at[other],
            recv_sem=ag_recv.at[slot],
            device_id=(other, me),
            device_id_type=MESH,
        )

    keep = pltpu.make_async_copy(
        reduced, down_ref.at[pl.ds(pl.multiple_of(row * rows, rows), rows)], own_sem.at[1]
    )
    keep.start()

    def gather_start(i, carry):
        gather_copy(lax.rem(row + i, groups), row).start()
        return carry

    lax.fori_loop(1, groups, gather_start, 0)

    def joined_finish(i, carry):
        joined_copy(lax.rem(row + i, groups), row).wait_send()
        source = lax.rem(row + groups - i, groups)
        joined_copy(source, source).wait_recv()
        return carry

    lax.fori_loop(1, groups, joined_finish, 0)
    own_joined.wait()
    joined_total = joined_parts[0].astype(jnp.float32)
    for slot in range(1, groups):
        joined_total = joined_total + joined_parts[slot].astype(jnp.float32)
    joined_sum[...] = joined_total.astype(joined_sum.dtype)
    halves = [
        pltpu.make_async_copy(joined_sum.at[:, pl.ds(0, width)], gate_ref, own_sem.at[3]),
        pltpu.make_async_copy(joined_sum.at[:, pl.ds(width, width)], up_ref, own_sem.at[4]),
    ]
    for copy in halves:
        copy.start()

    def gather_finish(i, carry):
        gather_copy(lax.rem(row + i, groups), row).wait_send()
        source = lax.rem(row + groups - i, groups)
        gather_copy(source, source).wait_recv()
        return carry

    lax.fori_loop(1, groups, gather_finish, 0)
    keep.wait()
    for copy in halves:
        copy.wait()

    def finish(i, carry):
        remote(lax.rem(me + i, n), me).wait_send()
        source = lax.rem(me + n - i, n)
        remote(source, source).wait_recv()
        return carry

    lax.fori_loop(1, n, finish, 0)
    local.wait()


def return_and_reduce(slot_grad, down_part, joined_part, groups, depth, collective_id):
    n = slot_grad.shape[0]
    rows = down_part.shape[0] // groups
    joined_rows = joined_part.shape[0] // groups
    width = joined_part.shape[1] // 2
    any_spec = pl.BlockSpec(memory_space=pl.ANY)
    return pl.pallas_call(
        functools.partial(return_kernel, n, groups, depth),
        out_shape=[
            jax.ShapeDtypeStruct(slot_grad.shape, slot_grad.dtype),
            jax.ShapeDtypeStruct(down_part.shape, down_part.dtype),
            jax.ShapeDtypeStruct((joined_rows, width), joined_part.dtype),
            jax.ShapeDtypeStruct((joined_rows, width), joined_part.dtype),
        ],
        in_specs=[any_spec] * 3,
        out_specs=[any_spec] * 4,
        scratch_shapes=[
            pltpu.SemaphoreType.DMA((n,)),
            pltpu.SemaphoreType.DMA((n,)),
            pltpu.SemaphoreType.DMA(()),
            pltpu.SemaphoreType.DMA((groups,)),
            pltpu.SemaphoreType.DMA((groups,)),
            pltpu.SemaphoreType.DMA((groups,)),
            pltpu.SemaphoreType.DMA((groups,)),
            pltpu.SemaphoreType.DMA((groups,)),
            pltpu.SemaphoreType.DMA((groups,)),
            pltpu.SemaphoreType.DMA((5,)),
            pltpu.VMEM((groups, rows, down_part.shape[1]), down_part.dtype),
            pltpu.VMEM((rows, down_part.shape[1]), down_part.dtype),
            pltpu.VMEM((groups, joined_rows, joined_part.shape[1]), joined_part.dtype),
            pltpu.VMEM((joined_rows, joined_part.shape[1]), joined_part.dtype),
        ],
        compiler_params=pltpu.CompilerParams(
            collective_id=collective_id, has_side_effects=True
        ),
    )(slot_grad, down_part, joined_part)


def on_device(tokens, out_grad, expert_ids, gates, w_gate, w_up, w_down):
    expert_count = lax.axis_size("expert")
    groups = lax.axis_size("dp")
    tok_rows = tokens.shape[0]
    model_width = tokens.shape[1]
    per_token = expert_ids.shape[1]
    hidden = w_gate.shape[2]
    entries = tok_rows * per_token
    slot_depth = 3 * entries // expert_count
    block = 8 * pl.cdiv(slot_depth, 8)
    slot_count = expert_count * block
    flat_ids = expert_ids.reshape(entries)
    onehot = (flat_ids[:, None] == jnp.arange(expert_count, dtype=jnp.int32)[None, :]).astype(
        jnp.int32
    )
    before = jnp.cumsum(onehot, axis=0) - onehot
    ranking = jnp.sum(before * onehot, axis=1)
    slot_of_entry = flat_ids * block + ranking
    entry_scaled = (
        (gates[:, :, None] * out_grad.astype(jnp.float32)[:, None, :])
        .astype(jnp.bfloat16)
        .reshape(entries, model_width)
    )
    choose = (
        jnp.arange(slot_count, dtype=jnp.int32)[:, None] == slot_of_entry[None, :]
    ).astype(jnp.bfloat16)
    choose_token = choose.reshape(slot_count, tok_rows, per_token).sum(axis=2).astype(tokens.dtype)
    send_grads = jnp.dot(choose, entry_scaled, preferred_element_type=jnp.float32).astype(
        jnp.bfloat16
    ).reshape(expert_count, block, model_width)
    send_inputs = jnp.dot(choose_token, tokens, preferred_element_type=jnp.float32).astype(
        tokens.dtype
    ).reshape(expert_count, block, model_width)
    rows_in, grads_in, full_joined, full_down = forward_exchange(
        send_inputs, send_grads, w_gate[0], w_up[0], w_down[0], groups, slot_depth, 0
    )
    filled = (jnp.arange(slot_count, dtype=jnp.int32) % block < slot_depth)[:, None]
    rows_in = jnp.where(filled, rows_in.reshape(slot_count, model_width), 0).astype(tokens.dtype)
    grads_in = jnp.where(filled, grads_in.reshape(slot_count, model_width), 0).astype(
        jnp.bfloat16
    )
    preact = jnp.dot(rows_in, full_joined, preferred_element_type=jnp.float32)
    hidden_grad = lax.dot_general(
        grads_in, full_down, (((1,), (1,)), ((), ())), preferred_element_type=jnp.float32
    )
    gate_pre = preact[:, :hidden]
    up_pre = preact[:, hidden:]
    sigmoid = jax.nn.sigmoid(gate_pre)
    silu_value = gate_pre * sigmoid
    activated = (silu_value * up_pre).astype(jnp.bfloat16)
    gate_side = (hidden_grad * up_pre * sigmoid * (1.0 + gate_pre * (1.0 - sigmoid))).astype(
        jnp.bfloat16
    )
    up_side = (hidden_grad * silu_value).astype(jnp.bfloat16)
    both_sides = jnp.concatenate([gate_side, up_side], axis=1)
    slot_grad = lax.dot_general(
        both_sides, full_joined, (((1,), (1,)), ((), ())), preferred_element_type=jnp.float32
    ).astype(jnp.bfloat16)
    down_part = lax.dot_general(
        activated, grads_in, (((0,), (0,)), ((), ())), preferred_element_type=jnp.float32
    ).astype(jnp.bfloat16)
    joined_part = lax.dot_general(
        rows_in, both_sides, (((0,), (0,)), ((), ())), preferred_element_type=jnp.float32
    ).astype(jnp.bfloat16)
    returned, down_grad, gate_grad, up_grad = return_and_reduce(
        slot_grad.reshape(expert_count, block, model_width),
        down_part,
        joined_part,
        groups,
        slot_depth,
        1,
    )
    owner = (slot_of_entry[:, None] == jnp.arange(slot_count, dtype=jnp.int32)[None, :]).astype(
        jnp.bfloat16
    )
    input_grad = jnp.dot(
        owner.reshape(tok_rows, per_token, slot_count).sum(axis=1),
        jnp.where(filled, returned.reshape(slot_count, model_width), 0).astype(jnp.bfloat16),
        preferred_element_type=jnp.float32,
    ).astype(jnp.bfloat16)
    return (input_grad, gate_grad[None], up_grad[None], down_grad[None])


def solution(mesh):
    in_specs = (
        P(("dp", "expert"), None),
        P(("dp", "expert"), None),
        P(("dp", "expert"), None),
        P(("dp", "expert"), None),
        P("expert", "dp", None),
        P("expert", "dp", None),
        P("expert", None, "dp"),
    )
    out_specs = (
        P(("dp", "expert"), None),
        P("expert", "dp", None),
        P("expert", "dp", None),
        P("expert", None, None),
    )
    return jax.shard_map(
        on_device, mesh=mesh, in_specs=in_specs, out_specs=out_specs, check_vma=False
    )
```

```python
import functools
import jax
import jax.numpy as jnp
from jax import lax
from jax.experimental import pallas as pl
from jax.experimental.pallas import tpu as pltpu
from jax.sharding import PartitionSpec as P

MESH = pl.DeviceIdType.MESH


def forward_kernel(n, groups, depth, inputs_ref, grads_ref, wg_ref, wu_ref, wd_ref, inputs_out,
                   grads_out, joined_out, down_out, send_sem, recv_sem, local_sem, ag_send,
                   ag_recv, own_sem):
    me = lax.axis_index("expert")
    row = lax.axis_index("dp")
    width = wg_ref.shape[1]
    piece = wg_ref.shape[0]
    columns = wd_ref.shape[1]
    barrier = pltpu.get_barrier_semaphore()

    def greet(i, carry):
        peer = lax.rem(me + i, n)
        pl.semaphore_signal(barrier, inc=1, device_id=(row, peer), device_id_type=MESH)
        return carry

    def greet_group(i, carry):
        other = lax.rem(row + i, groups)
        pl.semaphore_signal(barrier, inc=1, device_id=(other, me), device_id_type=MESH)
        return carry

    lax.fori_loop(1, n, greet, 0)
    lax.fori_loop(1, groups, greet_group, 0)
    pl.semaphore_wait(barrier, n - 1 + groups - 1)
    sources = (inputs_ref, grads_ref)
    targets = (inputs_out, grads_out)
    local = [
        pltpu.make_async_copy(
            sources[a].at[me, pl.ds(0, depth)], targets[a].at[me, pl.ds(0, depth)], local_sem.at[a]
        )
        for a in range(2)
    ]
    for copy in local:
        copy.start()

    def remote(a, peer, slot):
        return pltpu.make_async_remote_copy(
            src_ref=sources[a].at[peer, pl.ds(0, depth)],
            dst_ref=targets[a].at[slot, pl.ds(0, depth)],
            send_sem=send_sem.at[a, peer],
            recv_sem=recv_sem.at[a, slot],
            device_id=(row, peer),
            device_id_type=MESH,
        )

    def start(i, carry):
        peer = lax.rem(me + i, n)
        for a in range(2):
            remote(a, peer, me).start()
        return carry

    lax.fori_loop(1, n, start, 0)

    def places(slot):
        rows = pl.ds(pl.multiple_of(slot * piece, piece), piece)
        cols = pl.ds(pl.multiple_of(slot * columns, columns), columns)
        return (
            (wg_ref, joined_out.at[rows, pl.ds(0, width)]),
            (wu_ref, joined_out.at[rows, pl.ds(width, width)]),
            (wd_ref, down_out.at[:, cols]),
        )

    def gather_copy(k, other, slot):
        src, dst = places(slot)[k]
        return pltpu.make_async_remote_copy(
            src_ref=src,
            dst_ref=dst,
            send_sem=ag_send.at[k, other],
            recv_sem=ag_recv.at[k, slot],
            device_id=(other, me),
            device_id_type=MESH,
        )

    own = [
        pltpu.make_async_copy(src, dst, own_sem.at[k])
        for k, (src, dst) in enumerate(places(row))
    ]
    for copy in own:
        copy.start()

    def gather_start(i, carry):
        other = lax.rem(row + i, groups)
        for k in range(3):
            gather_copy(k, other, row).start()
        return carry

    lax.fori_loop(1, groups, gather_start, 0)

    def gather_finish(i, carry):
        other = lax.rem(row + i, groups)
        source = lax.rem(row + groups - i, groups)
        for k in range(3):
            gather_copy(k, other, row).wait_send()
            gather_copy(k, source, source).wait_recv()
        return carry

    lax.fori_loop(1, groups, gather_finish, 0)
    for copy in own:
        copy.wait()

    def finish(i, carry):
        peer = lax.rem(me + i, n)
        source = lax.rem(me + n - i, n)
        for a in range(2):
            remote(a, peer, me).wait_send()
            remote(a, source, source).wait_recv()
        return carry

    lax.fori_loop(1, n, finish, 0)
    for copy in local:
        copy.wait()


def forward_exchange(send_inputs, send_grads, wg, wu, wd, groups, depth, collective_id):
    n = send_inputs.shape[0]
    any_spec = pl.BlockSpec(memory_space=pl.ANY)
    return pl.pallas_call(
        functools.partial(forward_kernel, n, groups, depth),
        out_shape=[
            jax.ShapeDtypeStruct(send_inputs.shape, send_inputs.dtype),
            jax.ShapeDtypeStruct(send_grads.shape, send_grads.dtype),
            jax.ShapeDtypeStruct((groups * wg.shape[0], 2 * wg.shape[1]), wg.dtype),
            jax.ShapeDtypeStruct((wd.shape[0], groups * wd.shape[1]), wd.dtype),
        ],
        in_specs=[any_spec] * 5,
        out_specs=[any_spec] * 4,
        scratch_shapes=[
            pltpu.SemaphoreType.DMA((2, n)),
            pltpu.SemaphoreType.DMA((2, n)),
            pltpu.SemaphoreType.DMA((2,)),
            pltpu.SemaphoreType.DMA((3, groups)),
            pltpu.SemaphoreType.DMA((3, groups)),
            pltpu.SemaphoreType.DMA((3,)),
        ],
        compiler_params=pltpu.CompilerParams(
            collective_id=collective_id, has_side_effects=True
        ),
    )(send_inputs, send_grads, wg, wu, wd)


def return_kernel(n, groups, depth, slot_ref, part_ref, joined_ref, out_ref, down_ref, gate_ref, up_ref,
                  send_sem, recv_sem, local_sem, rs_send, rs_recv, ag_send, ag_recv, js_send,
                  js_recv, own_sem, parts, reduced, joined_parts, joined_sum):
    me = lax.axis_index("expert")
    row = lax.axis_index("dp")
    rows = reduced.shape[0]
    joined_rows = joined_sum.shape[0]
    width = gate_ref.shape[1]
    barrier = pltpu.get_barrier_semaphore()

    def greet(i, carry):
        peer = lax.rem(me + i, n)
        pl.semaphore_signal(barrier, inc=1, device_id=(row, peer), device_id_type=MESH)
        return carry

    def greet_group(i, carry):
        other = lax.rem(row + i, groups)
        pl.semaphore_signal(barrier, inc=1, device_id=(other, me), device_id_type=MESH)
        return carry

    lax.fori_loop(1, n, greet, 0)
    lax.fori_loop(1, groups, greet_group, 0)
    pl.semaphore_wait(barrier, n - 1 + groups - 1)
    local = pltpu.make_async_copy(
        slot_ref.at[me, pl.ds(0, depth)], out_ref.at[me, pl.ds(0, depth)], local_sem
    )
    local.start()

    def remote(peer, slot):
        return pltpu.make_async_remote_copy(
            src_ref=slot_ref.at[peer, pl.ds(0, depth)],
            dst_ref=out_ref.at[slot, pl.ds(0, depth)],
            send_sem=send_sem.at[peer],
            recv_sem=recv_sem.at[slot],
            device_id=(row, peer),
            device_id_type=MESH,
        )

    def start(i, carry):
        remote(lax.rem(me + i, n), me).start()
        return carry

    lax.fori_loop(1, n, start, 0)

    def scatter_copy(other, slot):
        return pltpu.make_async_remote_copy(
            src_ref=part_ref.at[pl.ds(pl.multiple_of(other * rows, rows), rows)],
            dst_ref=parts.at[slot],
            send_sem=rs_send.at[other],
            recv_sem=rs_recv.at[slot],
            device_id=(other, me),
            device_id_type=MESH,
        )

    def joined_copy(other, slot):
        return pltpu.make_async_remote_copy(
            src_ref=joined_ref.at[pl.ds(pl.multiple_of(other * joined_rows, joined_rows), joined_rows)],
            dst_ref=joined_parts.at[slot],
            send_sem=js_send.at[other],
            recv_sem=js_recv.at[slot],
            device_id=(other, me),
            device_id_type=MESH,
        )

    own = pltpu.make_async_copy(
        part_ref.at[pl.ds(pl.multiple_of(row * rows, rows), rows)], parts.at[row], own_sem.at[0]
    )
    own.start()
    own_joined = pltpu.make_async_copy(
        joined_ref.at[pl.ds(pl.multiple_of(row * joined_rows, joined_rows), joined_rows)],
        joined_parts.at[row],
        own_sem.at[2],
    )
    own_joined.start()

    def scatter_start(i, carry):
        other = lax.rem(row + i, groups)
        scatter_copy(other, row).start()
        joined_copy(other, row).start()
        return carry

    lax.fori_loop(1, groups, scatter_start, 0)

    def scatter_finish(i, carry):
        scatter_copy(lax.rem(row + i, groups), row).wait_send()
        source = lax.rem(row + groups - i, groups)
        scatter_copy(source, source).wait_recv()
        return carry

    lax.fori_loop(1, groups, scatter_finish, 0)
    own.wait()
    total = parts[0].astype(jnp.float32)
    for slot in range(1, groups):
        total = total + parts[slot].astype(jnp.float32)
    reduced[...] = total.astype(reduced.dtype)

    def gather_copy(other, slot):
        return pltpu.make_async_remote_copy(
            src_ref=reduced,
            dst_ref=down_ref.at[pl.ds(pl.multiple_of(slot * rows, rows), rows)],
            send_sem=ag_send.at[other],
            recv_sem=ag_recv.at[slot],
            device_id=(other, me),
            device_id_type=MESH,
        )

    keep = pltpu.make_async_copy(
        reduced, down_ref.at[pl.ds(pl.multiple_of(row * rows, rows), rows)], own_sem.at[1]
    )
    keep.start()

    def gather_start(i, carry):
        gather_copy(lax.rem(row + i, groups), row).start()
        return carry

    lax.fori_loop(1, groups, gather_start, 0)

    def joined_finish(i, carry):
        joined_copy(lax.rem(row + i, groups), row).wait_send()
        source = lax.rem(row + groups - i, groups)
        joined_copy(source, source).wait_recv()
        return carry

    lax.fori_loop(1, groups, joined_finish, 0)
    own_joined.wait()
    joined_total = joined_parts[0].astype(jnp.float32)
    for slot in range(1, groups):
        joined_total = joined_total + joined_parts[slot].astype(jnp.float32)
    joined_sum[...] = joined_total.astype(joined_sum.dtype)
    halves = [
        pltpu.make_async_copy(joined_sum.at[:, pl.ds(0, width)], gate_ref, own_sem.at[3]),
        pltpu.make_async_copy(joined_sum.at[:, pl.ds(width, width)], up_ref, own_sem.at[4]),
    ]
    for copy in halves:
        copy.start()

    def gather_finish(i, carry):
        gather_copy(lax.rem(row + i, groups), row).wait_send()
        source = lax.rem(row + groups - i, groups)
        gather_copy(source, source).wait_recv()
        return carry

    lax.fori_loop(1, groups, gather_finish, 0)
    keep.wait()
    for copy in halves:
        copy.wait()

    def finish(i, carry):
        remote(lax.rem(me + i, n), me).wait_send()
        source = lax.rem(me + n - i, n)
        remote(source, source).wait_recv()
        return carry

    lax.fori_loop(1, n, finish, 0)
    local.wait()


def return_and_reduce(slot_grad, down_part, joined_part, groups, depth, collective_id):
    n = slot_grad.shape[0]
    rows = down_part.shape[0] // groups
    joined_rows = joined_part.shape[0] // groups
    width = joined_part.shape[1] // 2
    any_spec = pl.BlockSpec(memory_space=pl.ANY)
    return pl.pallas_call(
        functools.partial(return_kernel, n, groups, depth),
        out_shape=[
            jax.ShapeDtypeStruct(slot_grad.shape, slot_grad.dtype),
            jax.ShapeDtypeStruct(down_part.shape, down_part.dtype),
            jax.ShapeDtypeStruct((joined_rows, width), joined_part.dtype),
            jax.ShapeDtypeStruct((joined_rows, width), joined_part.dtype),
        ],
        in_specs=[any_spec] * 3,
        out_specs=[any_spec] * 4,
        scratch_shapes=[
            pltpu.SemaphoreType.DMA((n,)),
            pltpu.SemaphoreType.DMA((n,)),
            pltpu.SemaphoreType.DMA(()),
            pltpu.SemaphoreType.DMA((groups,)),
            pltpu.SemaphoreType.DMA((groups,)),
            pltpu.SemaphoreType.DMA((groups,)),
            pltpu.SemaphoreType.DMA((groups,)),
            pltpu.SemaphoreType.DMA((groups,)),
            pltpu.SemaphoreType.DMA((groups,)),
            pltpu.SemaphoreType.DMA((5,)),
            pltpu.VMEM((groups, rows, down_part.shape[1]), down_part.dtype),
            pltpu.VMEM((rows, down_part.shape[1]), down_part.dtype),
            pltpu.VMEM((groups, joined_rows, joined_part.shape[1]), joined_part.dtype),
            pltpu.VMEM((joined_rows, joined_part.shape[1]), joined_part.dtype),
        ],
        compiler_params=pltpu.CompilerParams(
            collective_id=collective_id, has_side_effects=True
        ),
    )(slot_grad, down_part, joined_part)


def on_device(tokens, out_grad, expert_ids, gates, w_gate, w_up, w_down):
    expert_count = lax.axis_size("expert")
    groups = lax.axis_size("dp")
    tok_rows = tokens.shape[0]
    model_width = tokens.shape[1]
    per_token = expert_ids.shape[1]
    hidden = w_gate.shape[2]
    entries = tok_rows * per_token
    slot_depth = 3 * entries // expert_count
    block = 8 * pl.cdiv(slot_depth, 8)
    slot_count = expert_count * block
    flat_ids = expert_ids.reshape(entries)
    order = jnp.arange(entries, dtype=jnp.int32)
    earlier = (flat_ids[:, None] == flat_ids[None, :]) & (order[:, None] > order[None, :])
    ranking = jnp.sum(earlier.astype(jnp.int32), axis=1)
    slot_of_entry = flat_ids * block + ranking
    entry_scaled = (
        (gates[:, :, None] * out_grad.astype(jnp.float32)[:, None, :])
        .astype(jnp.bfloat16)
        .reshape(entries, model_width)
    )
    choose = (
        jnp.arange(slot_count, dtype=jnp.int32)[:, None] == slot_of_entry[None, :]
    ).astype(jnp.bfloat16)
    choose_token = choose.reshape(slot_count, tok_rows, per_token).sum(axis=2).astype(tokens.dtype)
    send_grads = jnp.dot(choose, entry_scaled, preferred_element_type=jnp.float32).astype(
        jnp.bfloat16
    ).reshape(expert_count, block, model_width)
    send_inputs = jnp.dot(choose_token, tokens, preferred_element_type=jnp.float32).astype(
        tokens.dtype
    ).reshape(expert_count, block, model_width)
    rows_in, grads_in, full_joined, full_down = forward_exchange(
        send_inputs, send_grads, w_gate[0], w_up[0], w_down[0], groups, slot_depth, 0
    )
    filled = (jnp.arange(slot_count, dtype=jnp.int32) % block < slot_depth)[:, None]
    rows_in = jnp.where(filled, rows_in.reshape(slot_count, model_width), 0).astype(tokens.dtype)
    grads_in = jnp.where(filled, grads_in.reshape(slot_count, model_width), 0).astype(
        jnp.bfloat16
    )
    preact = jnp.dot(rows_in, full_joined, preferred_element_type=jnp.float32)
    hidden_grad = lax.dot_general(
        grads_in, full_down, (((1,), (1,)), ((), ())), preferred_element_type=jnp.float32
    )
    gate_pre = preact[:, :hidden]
    up_pre = preact[:, hidden:]
    sigmoid = jax.nn.sigmoid(gate_pre)
    silu_value = gate_pre * sigmoid
    activated = (silu_value * up_pre).astype(jnp.bfloat16)
    gate_side = (hidden_grad * up_pre * sigmoid * (1.0 + gate_pre * (1.0 - sigmoid))).astype(
        jnp.bfloat16
    )
    up_side = (hidden_grad * silu_value).astype(jnp.bfloat16)
    both_sides = jnp.concatenate([gate_side, up_side], axis=1)
    slot_grad = lax.dot_general(
        both_sides, full_joined, (((1,), (1,)), ((), ())), preferred_element_type=jnp.float32
    ).astype(jnp.bfloat16)
    down_part = lax.dot_general(
        activated, grads_in, (((0,), (0,)), ((), ())), preferred_element_type=jnp.float32
    ).astype(jnp.bfloat16)
    joined_part = lax.dot_general(
        rows_in, both_sides, (((0,), (0,)), ((), ())), preferred_element_type=jnp.float32
    ).astype(jnp.bfloat16)
    returned, down_grad, gate_grad, up_grad = return_and_reduce(
        slot_grad.reshape(expert_count, block, model_width),
        down_part,
        joined_part,
        groups,
        slot_depth,
        1,
    )
    owner = (slot_of_entry[:, None] == jnp.arange(slot_count, dtype=jnp.int32)[None, :]).astype(
        jnp.bfloat16
    )
    input_grad = jnp.dot(
        owner.reshape(tok_rows, per_token, slot_count).sum(axis=1),
        jnp.where(filled, returned.reshape(slot_count, model_width), 0).astype(jnp.bfloat16),
        preferred_element_type=jnp.float32,
    ).astype(jnp.bfloat16)
    return (input_grad, gate_grad[None], up_grad[None], down_grad[None])


def solution(mesh):
    in_specs = (
        P(("dp", "expert"), None),
        P(("dp", "expert"), None),
        P(("dp", "expert"), None),
        P(("dp", "expert"), None),
        P("expert", "dp", None),
        P("expert", "dp", None),
        P("expert", None, "dp"),
    )
    out_specs = (
        P(("dp", "expert"), None),
        P("expert", "dp", None),
        P("expert", "dp", None),
        P("expert", None, None),
    )
    return jax.shard_map(
        on_device, mesh=mesh, in_specs=in_specs, out_specs=out_specs, check_vma=False
    )
```

```python
import functools
import jax
import jax.numpy as jnp
from jax import lax
from jax.experimental import pallas as pl
from jax.experimental.pallas import tpu as pltpu
from jax.sharding import PartitionSpec as P

MESH = pl.DeviceIdType.MESH


def forward_kernel(n, groups, depth, inputs_ref, grads_ref, wg_ref, wu_ref, wd_ref, inputs_out,
                   grads_out, joined_out, down_out, send_sem, recv_sem, local_sem, ag_send,
                   ag_recv, own_sem):
    me = lax.axis_index("expert")
    row = lax.axis_index("dp")
    width = wg_ref.shape[1]
    piece = wg_ref.shape[0]
    columns = wd_ref.shape[1]
    barrier = pltpu.get_barrier_semaphore()

    def greet(i, carry):
        peer = lax.rem(me + i, n)
        pl.semaphore_signal(barrier, inc=1, device_id=(row, peer), device_id_type=MESH)
        return carry

    def greet_group(i, carry):
        other = lax.rem(row + i, groups)
        pl.semaphore_signal(barrier, inc=1, device_id=(other, me), device_id_type=MESH)
        return carry

    lax.fori_loop(1, n, greet, 0)
    lax.fori_loop(1, groups, greet_group, 0)
    pl.semaphore_wait(barrier, n - 1 + groups - 1)
    sources = (inputs_ref, grads_ref)
    targets = (inputs_out, grads_out)
    local = [
        pltpu.make_async_copy(
            sources[a].at[me, pl.ds(0, depth)], targets[a].at[me, pl.ds(0, depth)], local_sem.at[a]
        )
        for a in range(2)
    ]
    for copy in local:
        copy.start()

    def remote(a, peer, slot):
        return pltpu.make_async_remote_copy(
            src_ref=sources[a].at[peer, pl.ds(0, depth)],
            dst_ref=targets[a].at[slot, pl.ds(0, depth)],
            send_sem=send_sem.at[a, peer],
            recv_sem=recv_sem.at[a, slot],
            device_id=(row, peer),
            device_id_type=MESH,
        )

    def start(i, carry):
        peer = lax.rem(me + i, n)
        for a in range(2):
            remote(a, peer, me).start()
        return carry

    lax.fori_loop(1, n, start, 0)

    def places(slot):
        rows = pl.ds(pl.multiple_of(slot * piece, piece), piece)
        cols = pl.ds(pl.multiple_of(slot * columns, columns), columns)
        return (
            (wg_ref, joined_out.at[rows, pl.ds(0, width)]),
            (wu_ref, joined_out.at[rows, pl.ds(width, width)]),
            (wd_ref, down_out.at[:, cols]),
        )

    def gather_copy(k, other, slot):
        src, dst = places(slot)[k]
        return pltpu.make_async_remote_copy(
            src_ref=src,
            dst_ref=dst,
            send_sem=ag_send.at[k, other],
            recv_sem=ag_recv.at[k, slot],
            device_id=(other, me),
            device_id_type=MESH,
        )

    own = [
        pltpu.make_async_copy(src, dst, own_sem.at[k])
        for k, (src, dst) in enumerate(places(row))
    ]
    for copy in own:
        copy.start()

    def gather_start(i, carry):
        other = lax.rem(row + i, groups)
        for k in range(3):
            gather_copy(k, other, row).start()
        return carry

    lax.fori_loop(1, groups, gather_start, 0)

    def gather_finish(i, carry):
        other = lax.rem(row + i, groups)
        source = lax.rem(row + groups - i, groups)
        for k in range(3):
            gather_copy(k, other, row).wait_send()
            gather_copy(k, source, source).wait_recv()
        return carry

    lax.fori_loop(1, groups, gather_finish, 0)
    for copy in own:
        copy.wait()

    def finish(i, carry):
        peer = lax.rem(me + i, n)
        source = lax.rem(me + n - i, n)
        for a in range(2):
            remote(a, peer, me).wait_send()
            remote(a, source, source).wait_recv()
        return carry

    lax.fori_loop(1, n, finish, 0)
    for copy in local:
        copy.wait()


def forward_exchange(send_inputs, send_grads, wg, wu, wd, groups, depth, collective_id):
    n = send_inputs.shape[0]
    any_spec = pl.BlockSpec(memory_space=pl.ANY)
    return pl.pallas_call(
        functools.partial(forward_kernel, n, groups, depth),
        out_shape=[
            jax.ShapeDtypeStruct(send_inputs.shape, send_inputs.dtype),
            jax.ShapeDtypeStruct(send_grads.shape, send_grads.dtype),
            jax.ShapeDtypeStruct((groups * wg.shape[0], 2 * wg.shape[1]), wg.dtype),
            jax.ShapeDtypeStruct((wd.shape[0], groups * wd.shape[1]), wd.dtype),
        ],
        in_specs=[any_spec] * 5,
        out_specs=[any_spec] * 4,
        scratch_shapes=[
            pltpu.SemaphoreType.DMA((2, n)),
            pltpu.SemaphoreType.DMA((2, n)),
            pltpu.SemaphoreType.DMA((2,)),
            pltpu.SemaphoreType.DMA((3, groups)),
            pltpu.SemaphoreType.DMA((3, groups)),
            pltpu.SemaphoreType.DMA((3,)),
        ],
        compiler_params=pltpu.CompilerParams(
            collective_id=collective_id, has_side_effects=True
        ),
    )(send_inputs, send_grads, wg, wu, wd)


def return_kernel(n, groups, depth, slot_ref, part_ref, joined_ref, out_ref, down_ref, gate_ref, up_ref,
                  send_sem, recv_sem, local_sem, rs_send, rs_recv, ag_send, ag_recv, js_send,
                  js_recv, own_sem, parts, reduced, joined_parts, joined_sum):
    me = lax.axis_index("expert")
    row = lax.axis_index("dp")
    rows = reduced.shape[0]
    joined_rows = joined_sum.shape[0]
    width = gate_ref.shape[1]
    barrier = pltpu.get_barrier_semaphore()

    def greet(i, carry):
        peer = lax.rem(me + i, n)
        pl.semaphore_signal(barrier, inc=1, device_id=(row, peer), device_id_type=MESH)
        return carry

    def greet_group(i, carry):
        other = lax.rem(row + i, groups)
        pl.semaphore_signal(barrier, inc=1, device_id=(other, me), device_id_type=MESH)
        return carry

    lax.fori_loop(1, n, greet, 0)
    lax.fori_loop(1, groups, greet_group, 0)
    pl.semaphore_wait(barrier, n - 1 + groups - 1)
    local = pltpu.make_async_copy(
        slot_ref.at[me, pl.ds(0, depth)], out_ref.at[me, pl.ds(0, depth)], local_sem
    )
    local.start()

    def remote(peer, slot):
        return pltpu.make_async_remote_copy(
            src_ref=slot_ref.at[peer, pl.ds(0, depth)],
            dst_ref=out_ref.at[slot, pl.ds(0, depth)],
            send_sem=send_sem.at[peer],
            recv_sem=recv_sem.at[slot],
            device_id=(row, peer),
            device_id_type=MESH,
        )

    def start(i, carry):
        remote(lax.rem(me + i, n), me).start()
        return carry

    lax.fori_loop(1, n, start, 0)

    def scatter_copy(other, slot):
        return pltpu.make_async_remote_copy(
            src_ref=part_ref.at[pl.ds(pl.multiple_of(other * rows, rows), rows)],
            dst_ref=parts.at[slot],
            send_sem=rs_send.at[other],
            recv_sem=rs_recv.at[slot],
            device_id=(other, me),
            device_id_type=MESH,
        )

    def joined_copy(other, slot):
        return pltpu.make_async_remote_copy(
            src_ref=joined_ref.at[pl.ds(pl.multiple_of(other * joined_rows, joined_rows), joined_rows)],
            dst_ref=joined_parts.at[slot],
            send_sem=js_send.at[other],
            recv_sem=js_recv.at[slot],
            device_id=(other, me),
            device_id_type=MESH,
        )

    own = pltpu.make_async_copy(
        part_ref.at[pl.ds(pl.multiple_of(row * rows, rows), rows)], parts.at[row], own_sem.at[0]
    )
    own.start()
    own_joined = pltpu.make_async_copy(
        joined_ref.at[pl.ds(pl.multiple_of(row * joined_rows, joined_rows), joined_rows)],
        joined_parts.at[row],
        own_sem.at[2],
    )
    own_joined.start()

    def scatter_start(i, carry):
        other = lax.rem(row + i, groups)
        scatter_copy(other, row).start()
        joined_copy(other, row).start()
        return carry

    lax.fori_loop(1, groups, scatter_start, 0)

    def scatter_finish(i, carry):
        scatter_copy(lax.rem(row + i, groups), row).wait_send()
        source = lax.rem(row + groups - i, groups)
        scatter_copy(source, source).wait_recv()
        return carry

    lax.fori_loop(1, groups, scatter_finish, 0)
    own.wait()
    total = parts[0].astype(jnp.float32)
    for slot in range(1, groups):
        total = total + parts[slot].astype(jnp.float32)
    reduced[...] = total.astype(reduced.dtype)

    def gather_copy(other, slot):
        return pltpu.make_async_remote_copy(
            src_ref=reduced,
            dst_ref=down_ref.at[pl.ds(pl.multiple_of(slot * rows, rows), rows)],
            send_sem=ag_send.at[other],
            recv_sem=ag_recv.at[slot],
            device_id=(other, me),
            device_id_type=MESH,
        )

    keep = pltpu.make_async_copy(
        reduced, down_ref.at[pl.ds(pl.multiple_of(row * rows, rows), rows)], own_sem.at[1]
    )
    keep.start()

    def gather_start(i, carry):
        gather_copy(lax.rem(row + i, groups), row).start()
        return carry

    lax.fori_loop(1, groups, gather_start, 0)

    def joined_finish(i, carry):
        joined_copy(lax.rem(row + i, groups), row).wait_send()
        source = lax.rem(row + groups - i, groups)
        joined_copy(source, source).wait_recv()
        return carry

    lax.fori_loop(1, groups, joined_finish, 0)
    own_joined.wait()
    joined_total = joined_parts[0].astype(jnp.float32)
    for slot in range(1, groups):
        joined_total = joined_total + joined_parts[slot].astype(jnp.float32)
    joined_sum[...] = joined_total.astype(joined_sum.dtype)
    halves = [
        pltpu.make_async_copy(joined_sum.at[:, pl.ds(0, width)], gate_ref, own_sem.at[3]),
        pltpu.make_async_copy(joined_sum.at[:, pl.ds(width, width)], up_ref, own_sem.at[4]),
    ]
    for copy in halves:
        copy.start()

    def gather_finish(i, carry):
        gather_copy(lax.rem(row + i, groups), row).wait_send()
        source = lax.rem(row + groups - i, groups)
        gather_copy(source, source).wait_recv()
        return carry

    lax.fori_loop(1, groups, gather_finish, 0)
    keep.wait()
    for copy in halves:
        copy.wait()

    def finish(i, carry):
        remote(lax.rem(me + i, n), me).wait_send()
        source = lax.rem(me + n - i, n)
        remote(source, source).wait_recv()
        return carry

    lax.fori_loop(1, n, finish, 0)
    local.wait()


def return_and_reduce(slot_grad, down_part, joined_part, groups, depth, collective_id):
    n = slot_grad.shape[0]
    rows = down_part.shape[0] // groups
    joined_rows = joined_part.shape[0] // groups
    width = joined_part.shape[1] // 2
    any_spec = pl.BlockSpec(memory_space=pl.ANY)
    return pl.pallas_call(
        functools.partial(return_kernel, n, groups, depth),
        out_shape=[
            jax.ShapeDtypeStruct(slot_grad.shape, slot_grad.dtype),
            jax.ShapeDtypeStruct(down_part.shape, down_part.dtype),
            jax.ShapeDtypeStruct((joined_rows, width), joined_part.dtype),
            jax.ShapeDtypeStruct((joined_rows, width), joined_part.dtype),
        ],
        in_specs=[any_spec] * 3,
        out_specs=[any_spec] * 4,
        scratch_shapes=[
            pltpu.SemaphoreType.DMA((n,)),
            pltpu.SemaphoreType.DMA((n,)),
            pltpu.SemaphoreType.DMA(()),
            pltpu.SemaphoreType.DMA((groups,)),
            pltpu.SemaphoreType.DMA((groups,)),
            pltpu.SemaphoreType.DMA((groups,)),
            pltpu.SemaphoreType.DMA((groups,)),
            pltpu.SemaphoreType.DMA((groups,)),
            pltpu.SemaphoreType.DMA((groups,)),
            pltpu.SemaphoreType.DMA((5,)),
            pltpu.VMEM((groups, rows, down_part.shape[1]), down_part.dtype),
            pltpu.VMEM((rows, down_part.shape[1]), down_part.dtype),
            pltpu.VMEM((groups, joined_rows, joined_part.shape[1]), joined_part.dtype),
            pltpu.VMEM((joined_rows, joined_part.shape[1]), joined_part.dtype),
        ],
        compiler_params=pltpu.CompilerParams(
            collective_id=collective_id, has_side_effects=True
        ),
    )(slot_grad, down_part, joined_part)


def on_device(tokens, out_grad, expert_ids, gates, w_gate, w_up, w_down):
    expert_count = lax.axis_size("expert")
    groups = lax.axis_size("dp")
    tok_rows = tokens.shape[0]
    model_width = tokens.shape[1]
    per_token = expert_ids.shape[1]
    hidden = w_gate.shape[2]
    entries = tok_rows * per_token
    slot_depth = 3 * entries // expert_count
    block = 8 * pl.cdiv(slot_depth, 8)
    slot_count = expert_count * block
    flat_ids = expert_ids.reshape(entries)
    order = jnp.arange(entries, dtype=jnp.int32)
    earlier = (flat_ids[:, None] == flat_ids[None, :]) & (order[:, None] > order[None, :])
    ranking = jnp.sum(earlier.astype(jnp.int32), axis=1)
    slot_of_entry = flat_ids * block + ranking
    entry_scaled = (
        (gates[:, :, None] * out_grad.astype(jnp.float32)[:, None, :])
        .astype(jnp.bfloat16)
        .reshape(entries, model_width)
    )
    choose = (
        jnp.arange(slot_count, dtype=jnp.int32)[:, None] == slot_of_entry[None, :]
    ).astype(jnp.bfloat16)
    choose_token = choose.reshape(slot_count, tok_rows, per_token).sum(axis=2).astype(tokens.dtype)
    send_grads = jnp.dot(choose, entry_scaled, preferred_element_type=jnp.float32).astype(
        jnp.bfloat16
    ).reshape(expert_count, block, model_width)
    send_inputs = jnp.dot(choose_token, tokens, preferred_element_type=jnp.float32).astype(
        tokens.dtype
    ).reshape(expert_count, block, model_width)
    rows_in, grads_in, full_joined, full_down = forward_exchange(
        send_inputs, send_grads, w_gate[0], w_up[0], w_down[0], groups, slot_depth, 0
    )
    filled = (jnp.arange(slot_count, dtype=jnp.int32) % block < slot_depth)[:, None]
    rows_in = jnp.where(filled, rows_in.reshape(slot_count, model_width), 0).astype(tokens.dtype)
    grads_in = jnp.where(filled, grads_in.reshape(slot_count, model_width), 0).astype(
        jnp.bfloat16
    )
    preact = jnp.dot(rows_in, full_joined, preferred_element_type=jnp.float32)
    hidden_grad = lax.dot_general(
        grads_in, full_down, (((1,), (1,)), ((), ())), preferred_element_type=jnp.float32
    )
    gate_pre = preact[:, :hidden]
    up_pre = preact[:, hidden:]
    sigmoid = jax.nn.sigmoid(gate_pre)
    silu_value = gate_pre * sigmoid
    activated = (silu_value * up_pre).astype(jnp.bfloat16)
    gate_side = (hidden_grad * up_pre * sigmoid * (1.0 + gate_pre * (1.0 - sigmoid))).astype(
        jnp.bfloat16
    )
    up_side = (hidden_grad * silu_value).astype(jnp.bfloat16)
    both_sides = jnp.concatenate([gate_side, up_side], axis=1)
    slot_grad = lax.dot_general(
        both_sides, full_joined, (((1,), (1,)), ((), ())), preferred_element_type=jnp.float32
    ).astype(jnp.bfloat16)
    down_part = lax.dot_general(
        activated, grads_in, (((0,), (0,)), ((), ())), preferred_element_type=jnp.float32
    ).astype(jnp.bfloat16)
    joined_part = lax.dot_general(
        rows_in, both_sides, (((0,), (0,)), ((), ())), preferred_element_type=jnp.float32
    ).astype(jnp.bfloat16)
    returned, down_grad, gate_grad, up_grad = return_and_reduce(
        slot_grad.reshape(expert_count, block, model_width),
        down_part,
        joined_part,
        groups,
        slot_depth,
        1,
    )
    input_grad = lax.dot_general(
        choose_token,
        jnp.where(filled, returned.reshape(slot_count, model_width), 0).astype(jnp.bfloat16),
        (((0,), (0,)), ((), ())),
        preferred_element_type=jnp.float32,
    ).astype(jnp.bfloat16)
    return (input_grad, gate_grad[None], up_grad[None], down_grad[None])


def solution(mesh):
    in_specs = (
        P(("dp", "expert"), None),
        P(("dp", "expert"), None),
        P(("dp", "expert"), None),
        P(("dp", "expert"), None),
        P("expert", "dp", None),
        P("expert", "dp", None),
        P("expert", None, "dp"),
    )
    out_specs = (
        P(("dp", "expert"), None),
        P("expert", "dp", None),
        P("expert", "dp", None),
        P("expert", None, None),
    )
    return jax.shard_map(
        on_device, mesh=mesh, in_specs=in_specs, out_specs=out_specs, check_vma=False
    )
```
